32 devices in a mesh: mod: 2 (over core), dp: 16 (over z, y, x).
Axes of the slice: x: 2, y: 2, z: 4, core: 2. Of those that a mesh axis runs over, the one named last changes fastest.
Arguments:
- rows: bfloat16 [2, 32, 196, 768], P('mod', 'dp'), may hold values from -6 to 6
- cotangent: bfloat16 [2, 32, 196, 768], P('mod', 'dp'), may hold values from -6 to 6
- master: float32 [7095552], P(('mod', 'dp')), as said below
- first_moment: float32 [7095552], P(('mod', 'dp')), may hold values from -0.0014648438 to 0.0014648438
- second_moment: float32 [7095552], P(('mod', 'dp')), may hold values from 5.919201e-09 to 2.3535872e-08
- average: float32 [7095552], P(('mod', 'dp')), as said below
- lengths: int32 [32], P('dp'), may hold values from 1 to 196, 3136 in all
- buckets: int32 [392, 392], replicated, may hold values from 0 to 62
Outputs:
- result_rows: bfloat16 [2, 32, 196, 768], P('mod', 'dp')
- grad_rows: float32 [2, 32, 196, 768], P('mod', 'dp')
- grad_norm: float32 [], replicated
- new_master: float32 [7095552], P(('mod', 'dp'))
- new_first: float32 [7095552], P(('mod', 'dp'))
- new_second: float32 [7095552], P(('mod', 'dp'))
- new_average: float32 [7095552], P(('mod', 'dp'))
- new_copy: bfloat16 [7095552], P(('mod', 'dp'))
The draws below stay inside these ranges and needn't reach their ends.
Inputs may be any that keep to these rules, and one draw needn't show every extreme that they name: `master`: a flat vector of parameters in the order of the steps, gains about 1, biases and matrices about zero. `average`: laid out as master.
All inputs are finite; a program needn't handle non-finite values. No bound on the sum of `lengths` on one device may be relied on, other than what follows from the above.
Results may differ from the reference program's by a relative error of at most 0.011.
Values may be sent and summed in bfloat16 or wider, within the bound.
No kernel may reach another device: no remote copies, remote signals or barrier semaphores. Data moves between devices by JAX's collectives and lax.ppermute only.
A program may use at most 192 MiB of HBM per device.

```python
import math
import jax
import jax.numpy as jnp
import numpy as np
from jax import lax

D = 768
H = 12
HD = 64
FF = 3072
NB = 63
P_SIZE = 196
STEP = 5
SEQ_DEV = 2
SEQS = 32
TOKENS = 12544
NPARAM = 7095552


def params_law(key):
    parts = jax.random.split(key, 12)
    blocks = []
    layout = [(D, D, D), (D, D, D), (D, D, D), (D, D, D), (D, FF, D), (FF, D, FF)]
    for index, entry in enumerate(layout):
        blocks.append(jax.random.normal(parts[index], (entry[0] * entry[1],), jnp.float32) * float(entry[2]) ** (-0.5))
    kinds_model = jnp.array([1.0, 0.0, 0.0, 0.0, 1.0, 0.0, 0.0, 1.0, 0.0, 0.0], jnp.float32)[:, None]
    gains = jax.random.uniform(parts[6], (10, D), jnp.float32, 0.7, 1.3)
    shifts = 0.2 * jax.random.normal(parts[7], (10, D), jnp.float32)
    blocks.append((kinds_model * gains + (1.0 - kinds_model) * shifts).reshape(-1))
    kinds_inner = jnp.array([0.0, 1.0, 0.0], jnp.float32)[:, None]
    gains_inner = jax.random.uniform(parts[8], (3, FF), jnp.float32, 0.7, 1.3)
    shifts_inner = 0.2 * jax.random.normal(parts[9], (3, FF), jnp.float32)
    blocks.append((kinds_inner * gains_inner + (1.0 - kinds_inner) * shifts_inner).reshape(-1))
    table = 0.7 * jax.random.normal(parts[10], (NB, H), jnp.float32)
    scales = jax.random.uniform(parts[11], (1, H), jnp.float32, 0.5, 1.5)
    blocks.append(jnp.concatenate([table, scales], axis=0).reshape(-1))
    return jnp.concatenate(blocks)


def draw_master(key, part):
    return params_law(jax.random.fold_in(key, 11))


def draw_average(key, part):
    return params_law(jax.random.fold_in(key, 23))


def place_ends(drawn, own_key, smallest, largest):
    index_at = [jax.random.randint(jax.random.fold_in(own_key, axis), (), 0, length) for axis, length in enumerate(drawn.shape)]
    longest = drawn.shape.index(max(drawn.shape))
    next_to = index_at[:longest] + [(index_at[longest] + 1) % drawn.shape[longest]] + index_at[longest + 1:]
    return drawn.at[tuple(index_at)].set(smallest).at[tuple(next_to)].set(largest)


def steps_of(own_key, shape, cuts, smallest, high):
    level = 1.0
    for position, blocks in cuts:
        heights = jax.random.uniform(jax.random.fold_in(jax.random.fold_in(own_key, 6), position), (blocks,), jnp.float32, smallest / len(cuts), high / len(cuts))
        level = level * jnp.repeat(jnp.exp(heights), shape[position] // blocks).reshape((-1,) + (1,) * (len(shape) - 1 - position))
    return level


def length_profile(count, total, limit, lean):
    loads = [(1 << 20) // math.isqrt(rank ** lean) + 1 for rank in range(2, count + 1)]
    surplus, holding = total - limit - (count - 1), [1] * (count - 1)
    while surplus > 0:
        free = [i for i in range(count - 1) if holding[i] < limit]
        whole, left = sum([loads[i] for i in free]), surplus
        for i in free:
            extra = min(limit - holding[i], max(1, left * loads[i] // whole), surplus)
            holding[i] = holding[i] + extra
            surplus = surplus - extra
    return np.array([limit] + holding)


def uneven(rng, count, total, reach, skew):
    if count == 2:
        one = jax.random.randint(rng, (), max(1, total - reach), min(reach, total - 1) + 1)
        return jnp.stack([one, total - one])
    sizes = jnp.asarray(length_profile(count, total, reach, skew), jnp.int32)
    couples = (count - 1) // 2
    donor, sink = sizes[1:1 + 2 * couples:2], sizes[2:2 + 2 * couples:2]
    room = jnp.minimum(donor - 1, reach - sink)
    passed = jax.random.randint(jax.random.fold_in(rng, 1), (couples,), 0, 1 << 20) % (room + 1)
    sizes = sizes.at[1:1 + 2 * couples:2].set(donor - passed).at[2:2 + 2 * couples:2].set(sink + passed)
    return sizes[jax.random.permutation(jax.random.fold_in(rng, 2), count)]


def normal_values(own_key, shape, width, reach, shards=(), held_as=jnp.bfloat16):
    level = steps_of(own_key, shape, shards, -0.22, 0.18) if shards else 1.0
    values = jax.random.normal(own_key, shape, jnp.float32) * width * level
    return jnp.minimum(jnp.maximum(values, -reach), reach).astype(held_as)


def setup_inputs(seed: int = 0) -> dict:
    splits = jax.random.split(jax.random.key(seed), 9)
    return {
        "rows": normal_values(splits[0], (2, SEQS, P_SIZE, D), 1.0, 6.0, ((0, 2), (1, 16))),
        "cotangent": normal_values(splits[1], (2, SEQS, P_SIZE, D), 1.0, 6.0, ((0, 2), (1, 16))),
        "master": draw_master(jax.random.fold_in(splits[8], 71), 0),
        "first_moment": normal_values(splits[3], (NPARAM,), (0.25 / NPARAM ** 0.5), 0.0014648438, ((0, 32),), jnp.float32),
        "second_moment": jnp.clip(jnp.exp(math.log(2.3535871918056728e-08) - 1.3803242 * jax.random.uniform(splits[4], (NPARAM,), jnp.float32) ** steps_of(splits[4], (NPARAM,), ((0, 32),), -0.2, 0.2)), 5.919201129245266e-09, 2.3535871918056728e-08),
        "average": draw_average(jax.random.fold_in(splits[8], 71), 0),
        "lengths": uneven(splits[6], SEQS, SEQS * P_SIZE // 2, P_SIZE, 2).astype(jnp.int32),
        "buckets": place_ends(jax.random.randint(splits[7], (2 * P_SIZE, 2 * P_SIZE), 0, NB), jax.random.fold_in(splits[7], 1), 0, NB - 1).astype(jnp.int32),
    }


@jax.custom_vjp
def low(v):
    return lax.optimization_barrier(v.astype(jnp.bfloat16)).astype(jnp.float32)

@jax.custom_vjp
def low_back(v):
    return v

def low_keep(v):
    return (low(v), None)

def low_pass(kept, grad):
    return (grad,)

def back_keep(v):
    return (v, None)

def back_low(kept, grad):
    return (low(grad),)
low.defvjp(low_keep, low_pass)
low_back.defvjp(back_keep, back_low)

def layer_norm(values, gain, shift):
    center = values - lax.optimization_barrier(jnp.mean(values, axis=-1, keepdims=True))
    spread = lax.optimization_barrier(jnp.mean(center * center, axis=-1, keepdims=True))
    return center * lax.rsqrt(spread + 1e-05) * gain + shift

def matmul(left, right):
    return jnp.dot(left, right, precision=lax.Precision.HIGHEST, preferred_element_type=jnp.float32)

def unpack(flat):
    pairs = [(D, D), (D, D), (D, D), (D, D), (D, FF), (FF, D), (10, D), (3, FF), (NB + 1, H)]
    pieces = []
    offset = 0
    for dims_pair in pairs:
        extent = dims_pair[0] * dims_pair[1]
        pieces.append(flat[offset:offset + extent].reshape(dims_pair))
        offset += extent
    return pieces

def group_layer(params, blocks, valid, buckets):
    w_query, w_key, w_value, w_out, w_inner, w_outer, vec_model, vec_inner, head_table = unpack(params)
    groups_n = blocks.shape[1]
    flat_rows = blocks.reshape(-1, D)
    normed = low(layer_norm(flat_rows, vec_model[0], vec_model[1]))
    query = low_back(low(matmul(normed, w_query) + vec_model[2]))
    keys = low_back(low(matmul(normed, w_key)))
    values = low_back(low(matmul(normed, w_value) + vec_model[3]))

    def joint(tensor):
        return tensor.reshape(2, groups_n, P_SIZE, H, HD).transpose(1, 0, 2, 3, 4).reshape(groups_n, 2 * P_SIZE, H, HD)
    key_valid = valid.transpose(1, 0, 2).reshape(groups_n, 2 * P_SIZE)
    rel_bias = jnp.take(head_table[:NB], buckets, axis=0).transpose(2, 0, 1)
    logits = jnp.einsum('gqhe,gkhe->ghqk', joint(query), joint(keys), precision=lax.Precision.HIGHEST) * 0.125 + rel_bias[None]
    logits = low_back(jnp.where(key_valid[:, None, None, :] > 0, logits, -1e+30))
    probs = low(jax.nn.softmax(logits, axis=-1))
    attended = low_back(jnp.einsum('ghqk,gkhe->gqhe', probs, joint(values), precision=lax.Precision.HIGHEST))
    scaled = attended * head_table[NB][None, None, :, None]
    scaled = scaled.reshape(groups_n, 2, P_SIZE, D).transpose(1, 0, 2, 3).reshape(-1, D)
    mixed = low(layer_norm(scaled, vec_model[4], vec_model[5]))
    middle = flat_rows + low_back(matmul(mixed, w_out) + vec_model[6])
    normed_two = low(layer_norm(middle, vec_model[7], vec_model[8]))
    inner = low_back(matmul(normed_two, w_inner) + vec_inner[0])
    inner_normed = low(layer_norm(jax.nn.gelu(inner, approximate=False), vec_inner[1], vec_inner[2]))
    result = middle + low_back(matmul(inner_normed, w_outer) + vec_model[9])
    return result.reshape(blocks.shape)

def reference(rows, cotangent, master, first_moment, second_moment, average, lengths, buckets):
    params = master.astype(jnp.bfloat16).astype(jnp.float32)
    inputs = rows.astype(jnp.float32)
    slots = jnp.arange(P_SIZE, dtype=jnp.int32)
    text_valid = (slots[None, :] < lengths[:, None]).astype(jnp.float32)
    valid = jnp.stack([jnp.ones_like(text_valid), text_valid])
    count_groups = SEQS // SEQ_DEV

    def forward(weights, data):
        grouped = data.reshape(2, count_groups, SEQ_DEV, P_SIZE, D).transpose(1, 0, 2, 3, 4)
        valid_grouped = valid.reshape(2, count_groups, SEQ_DEV, P_SIZE).transpose(1, 0, 2, 3)
        step_fn = jax.checkpoint(lambda pair: group_layer(weights, pair[0], pair[1], buckets))
        outputs = lax.map(step_fn, (grouped, valid_grouped))
        return outputs.transpose(1, 0, 2, 3, 4).reshape(2, SEQS, P_SIZE, D)
    result, pullback = jax.vjp(forward, params, inputs)
    cot = cotangent.astype(jnp.float32) * valid[..., None]
    grad_params, grad_rows = pullback(cot)
    grad = grad_params / TOKENS
    grad_norm = jnp.sqrt(jnp.sum(grad * grad))
    clip_scale = jnp.minimum(1.0, 0.25 / (grad_norm + 1e-06))
    clipped = grad * clip_scale
    new_first = 0.5 * first_moment + 0.5 * clipped
    new_second = 0.6 * second_moment + 0.4 * clipped * clipped
    direction = new_first / (1.0 - 0.5 ** STEP) / (jnp.sqrt(new_second / (1.0 - 0.6 ** STEP)) + 1e-08)
    new_master = master - 0.04 * (direction + 0.01 * master)
    new_average = 0.5 * average + 0.5 * new_master
    return (result.astype(jnp.bfloat16), grad_rows, grad_norm, new_master, new_first, new_second, new_average, new_master.astype(jnp.bfloat16))
```

```python
import functools
import jax
import jax.numpy as jnp
from jax import lax
from jax.experimental import pallas as pl
from jax.experimental.pallas import tpu as pltpu
from jax.sharding import PartitionSpec as P

D = 768
H = 12
HD = 64
FF = 3072
NB = 63
P_SIZE = 196
STEP = 5


HALF = D // 2
BLOCK = 144
PHASE_ROWS = 32 * BLOCK
BF = jnp.bfloat16
F32 = jnp.float32
DP = 16
EDGE = 17664


def x_swap():
    return [(i, i ^ 1) for i in range(DP)]


def y_swap():
    return [(i, i ^ 2) for i in range(DP)]


def z_turn(step):
    return [(i, (i // 4 + step) % 4 * 4 + i % 4) for i in range(DP)]


def send_dp(block, route):
    return lax.ppermute(block, "dp", route)


def send_mod(block):
    return lax.ppermute(block, "mod", [(0, 1), (1, 0)])


def pack_shard(own, side, place):
    lead = 8832 * side + 552 * place
    count = BLOCK * D
    lent = lax.dynamic_slice(own, (count - lead,), (count,))
    given = send_mod(lent)
    nxt = [(i, i + 1) for i in range(2 * DP - 1)]
    edge = lax.ppermute(own[own.shape[0] - EDGE :], ("mod", "dp"), nxt)
    kept = lax.dynamic_slice(jnp.concatenate([edge, own[:count]]), (EDGE - lead,), (count,))
    kept = kept.reshape(BLOCK, D)
    given = given.reshape(BLOCK, D)
    return jnp.where(side == 0, kept, given), jnp.where(side == 0, given, kept)


def unpack_shard(first, second, vec, side, place):
    lead = 8832 * side + 552 * place
    even = jnp.where(side == 0, first, second).reshape(-1)
    lent = jnp.where(side == 0, second, first)
    odd = send_mod(lent).reshape(-1)
    back = [(i + 1, i) for i in range(2 * DP - 1)]
    edge = lax.ppermute(even[:EDGE], ("mod", "dp"), back)
    is_last = jnp.logical_and(side == 1, place == DP - 1)
    edge = jnp.where(is_last, vec.reshape(-1)[:EDGE], edge)
    return lax.dynamic_slice(jnp.concatenate([even, odd, edge]), (lead,), (221736,))


def sum_all_small(part):
    for route in (x_swap(), y_swap(), z_turn(2)):
        part = part + send_dp(part, route)
    part = part + send_dp(part, [(i, i ^ 4) for i in range(DP)])
    return part + send_mod(part)


def gather_phase(block):
    stack = jnp.stack([block] + [send_dp(block, z_turn(step)) for step in (1, 2, 3)])
    left, right = stack[:, :, :HALF], stack[:, :, HALF:]
    left_x = send_dp(left, x_swap())
    right_y = send_dp(right, y_swap())
    left_y = send_dp(left, y_swap())
    right_x = send_dp(right, x_swap())
    left_xy = send_dp(left_x, y_swap())
    right_xy = send_dp(right_y, x_swap())
    mine = [left, left_x, left_y, left_xy, right, right_x, right_y, right_xy]
    return mine + [send_mod(piece) for piece in mine]


def coords():
    side = lax.axis_index("mod")
    place = lax.axis_index("dp")
    return jnp.stack([side, place // 4, place // 2 % 2, place % 2]).astype(jnp.int32)


def assemble_body(phase, spot, *refs):
    pieces, out, sem = refs[:16], refs[16], refs[17]
    side, z, y, x = spot[0], spot[1], spot[2], spot[3]
    copies = []
    for index in range(16):
        other, half, yr, xr = index // 8, index // 4 % 2, index // 2 % 2, index % 2
        owner = side ^ other
        parity = owner if phase == 0 else 1 - owner
        for turn in range(4):
            home = ((z - turn) & 3) * 4 + (y ^ yr) * 2 + (x ^ xr)
            copies.append(
                pltpu.make_async_copy(
                    pieces[index].at[turn],
                    out.at[home * 2 + parity, :, pl.ds(half * HALF, HALF)],
                    sem.at[index * 4 + turn],
                )
            )
    for copy in copies:
        copy.start()
    for copy in copies:
        copy.wait()


def assemble(phase, spot, pieces):
    return pl.pallas_call(
        functools.partial(assemble_body, phase),
        out_shape=jax.ShapeDtypeStruct((32, BLOCK, D), BF),
        in_specs=[pl.BlockSpec(memory_space=pltpu.SMEM)] + [pl.BlockSpec(memory_space=pl.ANY)] * 16,
        out_specs=pl.BlockSpec(memory_space=pltpu.VMEM),
        scratch_shapes=[pltpu.SemaphoreType.DMA((64,))],
        name="assemble",
    )(spot, *pieces).reshape(PHASE_ROWS, D)


def scatter_body(phase, spot, src, out, sem):
    side, z, y, x = spot[0], spot[1], spot[2], spot[3]
    copies = []
    for block in range(32):
        home, parity = block // 2, block % 2
        owner = parity if phase == 0 else 1 - parity
        other = side ^ owner
        turn = (home // 4 - z) & 3
        yr = (home // 2 % 2) ^ y
        xr = (home % 2) ^ x
        for half in range(2):
            copies.append(
                pltpu.make_async_copy(
                    src.at[block, :, pl.ds(half * HALF, HALF)],
                    out.at[other, half, yr, xr, turn],
                    sem.at[block * 2 + half],
                )
            )
    for copy in copies:
        copy.start()
    for copy in copies:
        copy.wait()


def scatter(phase, spot, grads):
    return pl.pallas_call(
        functools.partial(scatter_body, phase),
        out_shape=jax.ShapeDtypeStruct((2, 2, 2, 2, 4, BLOCK, HALF), BF),
        in_specs=[pl.BlockSpec(memory_space=pltpu.SMEM), pl.BlockSpec(memory_space=pltpu.VMEM)],
        out_specs=pl.BlockSpec(memory_space=pl.ANY),
        scratch_shapes=[pltpu.SemaphoreType.DMA((64,))],
        name="scatter",
    )(spot, grads.reshape(32, BLOCK, D))


def plus(left, right):
    return (left.astype(F32) + right.astype(F32)).astype(BF)


def reduce_phase(parts):
    theirs = send_mod(parts[1])
    left_out = send_dp(plus(parts[0, 0, :, 1], theirs[0, :, 1]), x_swap())
    right_out = send_dp(plus(parts[0, 1, 1], theirs[1, 1]), y_swap())
    left_in = plus(parts[0, 0, :, 0], theirs[0, :, 0])
    right_in = plus(parts[0, 1, 0], theirs[1, 0])
    left_next = send_dp(plus(left_in[1], left_out[1]), y_swap())
    right_next = send_dp(plus(right_in[1], right_out[1]), x_swap())
    left = left_in[0].astype(F32) + left_out[0].astype(F32) + left_next.astype(F32)
    right = right_in[0].astype(F32) + right_out[0].astype(F32) + right_next.astype(F32)
    both = jnp.concatenate([left, right], axis=-1)
    low = both.astype(BF)
    total = both[0]
    for step in (1, 2, 3):
        total = total + send_dp(low[step], z_turn(step)).astype(F32)
    return total


def from_partner(block, axis, bit):
    count = lax.axis_size(axis)
    route = []
    for low in range(count):
        high = low | 1 << bit
        if high != low and high < count:
            route += [(low, high), (high, low)]
    return lax.ppermute(block, axis, route)


def layer_norm(values, gain, shift):
    center = values - jnp.mean(values, axis=-1, keepdims=True)
    spread = jnp.mean(center * center, axis=-1, keepdims=True)
    return center * lax.rsqrt(spread + 1e-05) * gain + shift


def norm_back(values, gain, shift, grad_after):
    _, pullback = jax.vjp(layer_norm, values, gain, shift)
    return pullback(grad_after)


def matmul(left, right):
    return jnp.dot(left, right, preferred_element_type=jnp.float32)


def matmul_tn(left, right):
    return lax.dot_general(
        left, right, (((0,), (0,)), ((), ())), preferred_element_type=jnp.float32
    )


def matmul_nt(left, right):
    return lax.dot_general(
        left, right, (((1,), (1,)), ((), ())), preferred_element_type=jnp.float32
    )


def exact_gelu(values):
    return jax.nn.gelu(values, approximate=False)


def unpack(flat):
    pairs = [(D, D), (D, D), (D, D), (D, D), (D, FF), (FF, D), (10, D), (3, FF), (NB + 1, H)]
    pieces = []
    offset = 0
    for dims_pair in pairs:
        extent = dims_pair[0] * dims_pair[1]
        pieces.append(flat[offset : offset + extent].reshape(dims_pair))
        offset += extent
    return pieces


def on_device(rows, cotangent, master, first_moment, second_moment, average, lengths, buckets):
    side = lax.axis_index("mod")
    place = lax.axis_index("dp")
    fast = lax.axis_size("dp") == DP
    own_copy = master.astype(jnp.bfloat16)
    if fast:
        spot = coords()
        first, second = pack_shard(own_copy, side, place)
        is_last = jnp.logical_and(side == 1, place == DP - 1)
        vec = jnp.where(is_last, own_copy[-EDGE:], jnp.zeros((), BF))
        vec = jnp.pad(vec, (0, D)).reshape(24, D)
        flat = jnp.concatenate(
            [
                assemble(0, spot, gather_phase(first)),
                assemble(1, spot, gather_phase(second)),
                sum_all_small(vec)[:23],
            ]
        ).reshape(-1)
    else:
        flat = lax.all_gather(own_copy, ("mod", "dp"), axis=0, tiled=True)
    w_query, w_key, w_value, w_out, w_inner, w_outer, vec_model, vec_inner, head_table = unpack(
        flat
    )
    model_vec = vec_model.astype(jnp.float32)
    inner_vec = vec_inner.astype(jnp.float32)
    head_vals = head_table.astype(jnp.float32)
    head_scale = head_vals[NB]
    num_seq = rows.shape[1]
    num_rows = num_seq * P_SIZE
    slots = jnp.arange(P_SIZE, dtype=jnp.int32)
    text_valid = (slots[None, :] < lengths[:, None]).astype(jnp.float32)
    image_valid = jnp.ones_like(text_valid)
    own_valid = jnp.where(side == 0, image_valid, text_valid)
    other_valid = jnp.where(side == 0, text_valid, image_valid)
    key_valid = jnp.concatenate([own_valid, other_valid], axis=1)
    doubled = jnp.concatenate([buckets, buckets], axis=1)
    start = side * P_SIZE
    block_ids = lax.dynamic_slice(doubled, (start, start), (P_SIZE, 2 * P_SIZE))
    rel_bias = jnp.take(head_vals[:NB], block_ids, axis=0).transpose(2, 0, 1)
    inputs = rows[0].astype(jnp.float32).reshape(num_rows, D)
    normed = layer_norm(inputs, model_vec[0], model_vec[1])
    normed_low = normed.astype(jnp.bfloat16)
    query = (
        (matmul(normed_low, w_query) + model_vec[2])
        .astype(jnp.bfloat16)
        .reshape(num_seq, P_SIZE, H, HD)
    )
    keys_own = matmul(normed_low, w_key).astype(jnp.bfloat16).reshape(num_seq, P_SIZE, H, HD)
    values_own = (
        (matmul(normed_low, w_value) + model_vec[3])
        .astype(jnp.bfloat16)
        .reshape(num_seq, P_SIZE, H, HD)
    )
    keys_other, values_other = from_partner((keys_own, values_own), "mod", 0)
    keys_all = jnp.concatenate([keys_own, keys_other], axis=1)
    values_all = jnp.concatenate([values_own, values_other], axis=1)

    def masked_scores():
        logits = (
            jnp.einsum("gqhe,gkhe->ghqk", query, keys_all, preferred_element_type=jnp.float32)
            * 0.125
            + rel_bias[None]
        )
        return jnp.where(key_valid[:, None, None, :] > 0, logits, -1e30)

    scores = masked_scores()
    log_total = jax.nn.logsumexp(scores, axis=-1, keepdims=True)
    probs = jnp.exp(scores - log_total)
    attended = jnp.einsum(
        "ghqk,gkhe->gqhe",
        probs.astype(jnp.bfloat16),
        values_all,
        preferred_element_type=jnp.float32,
    )
    scaled = (attended * head_scale[None, None, :, None]).reshape(num_rows, D)
    mixed = layer_norm(scaled, model_vec[4], model_vec[5])
    mixed_low = mixed.astype(jnp.bfloat16)
    middle = inputs + (matmul(mixed_low, w_out) + model_vec[6])
    normed_two = layer_norm(middle, model_vec[7], model_vec[8])
    normed_two_low = normed_two.astype(jnp.bfloat16)
    inner = matmul(normed_two_low, w_inner) + inner_vec[0]
    activated = exact_gelu(inner)
    inner_normed = layer_norm(activated, inner_vec[1], inner_vec[2])
    inner_low = inner_normed.astype(jnp.bfloat16)
    result = middle + (matmul(inner_low, w_outer) + model_vec[9])
    result_rows = result.astype(jnp.bfloat16).reshape(1, num_seq, P_SIZE, D)
    grad_out = cotangent[0].astype(jnp.float32).reshape(num_rows, D) * own_valid.reshape(
        num_rows, 1
    )
    grad_branch = grad_out.astype(jnp.bfloat16)
    grad_w_outer = matmul_tn(inner_low, grad_branch)
    grad_b_outer = jnp.sum(grad_branch.astype(jnp.float32), axis=0)
    grad_inner_normed = matmul_nt(grad_branch, w_outer)
    grad_activated, grad_gain_ff, grad_shift_ff = norm_back(
        activated, inner_vec[1], inner_vec[2], grad_inner_normed
    )
    _, gelu_pull = jax.vjp(exact_gelu, inner)
    grad_inner_low = gelu_pull(grad_activated)[0].astype(jnp.bfloat16)
    grad_w_inner = matmul_tn(normed_two_low, grad_inner_low)
    grad_b_inner = jnp.sum(grad_inner_low.astype(jnp.float32), axis=0)
    grad_normed_two = matmul_nt(grad_inner_low, w_inner)
    grad_mid_part, grad_gain_two, grad_shift_two = norm_back(
        middle, model_vec[7], model_vec[8], grad_normed_two
    )
    grad_middle = grad_out + grad_mid_part
    grad_attn_low = grad_middle.astype(jnp.bfloat16)
    grad_w_out = matmul_tn(mixed_low, grad_attn_low)
    grad_b_out = jnp.sum(grad_attn_low.astype(jnp.float32), axis=0)
    grad_mixed = matmul_nt(grad_attn_low, w_out)
    grad_scaled, grad_gain_attn, grad_shift_attn = norm_back(
        scaled, model_vec[4], model_vec[5], grad_mixed
    )
    grad_scaled_heads = grad_scaled.reshape(num_seq, P_SIZE, H, HD)
    grad_head_scale = jnp.sum(grad_scaled_heads * attended, axis=(0, 1, 3))
    grad_attended = (grad_scaled_heads * head_scale[None, None, :, None]).astype(jnp.bfloat16)
    scores_again = masked_scores()
    probs_again = jnp.exp(scores_again - log_total)
    grad_probs = jnp.einsum(
        "gqhe,gkhe->ghqk", grad_attended, values_all, preferred_element_type=jnp.float32
    )
    grad_values_all = jnp.einsum(
        "ghqk,gqhe->gkhe",
        probs_again.astype(jnp.bfloat16),
        grad_attended,
        preferred_element_type=jnp.float32,
    )
    grad_scores = probs_again * (
        grad_probs - jnp.sum(probs_again * grad_probs, axis=-1, keepdims=True)
    )
    grad_scores_low = grad_scores.astype(jnp.bfloat16)
    grad_query = (
        (
            jnp.einsum(
                "ghqk,gkhe->gqhe", grad_scores_low, keys_all, preferred_element_type=jnp.float32
            )
            * 0.125
        )
        .astype(jnp.bfloat16)
        .reshape(num_rows, D)
    )
    grad_keys_all = (
        jnp.einsum("ghqk,gqhe->gkhe", grad_scores_low, query, preferred_element_type=jnp.float32)
        * 0.125
    )
    back_keys, back_values = (
        from_partner(grad_keys_all[:, P_SIZE:].astype(jnp.bfloat16), "mod", 0).astype(jnp.float32),
        from_partner(grad_values_all[:, P_SIZE:].astype(jnp.bfloat16), "mod", 0).astype(
            jnp.float32
        ),
    )
    grad_key = (grad_keys_all[:, :P_SIZE] + back_keys).astype(jnp.bfloat16).reshape(num_rows, D)
    grad_value = (
        (grad_values_all[:, :P_SIZE] + back_values).astype(jnp.bfloat16).reshape(num_rows, D)
    )
    bias_terms = jnp.sum(grad_scores_low.astype(jnp.float32), axis=0).reshape(
        H, 2 * P_SIZE * P_SIZE
    )
    bucket_hot = (
        block_ids.reshape(-1)[:, None] == jnp.arange(NB, dtype=jnp.int32)[None, :]
    ).astype(jnp.float32)
    grad_table = jnp.einsum("pb,hp->bh", bucket_hot, bias_terms, precision=lax.Precision.HIGHEST)
    grad_w_query = matmul_tn(normed_low, grad_query)
    grad_w_key = matmul_tn(normed_low, grad_key)
    grad_w_value = matmul_tn(normed_low, grad_value)
    grad_b_query = jnp.sum(grad_query.astype(jnp.float32), axis=0)
    grad_b_value = jnp.sum(grad_value.astype(jnp.float32), axis=0)
    grad_normed = (
        matmul_nt(grad_query, w_query) + matmul_nt(grad_key, w_key) + matmul_nt(grad_value, w_value)
    )
    grad_in_part, grad_gain_one, grad_shift_one = norm_back(
        inputs, model_vec[0], model_vec[1], grad_normed
    )
    grad_rows = (grad_middle + grad_in_part).reshape(1, num_seq, P_SIZE, D)
    grad_model_vec = jnp.stack(
        [
            grad_gain_one,
            grad_shift_one,
            grad_b_query,
            grad_b_value,
            grad_gain_attn,
            grad_shift_attn,
            grad_b_out,
            grad_gain_two,
            grad_shift_two,
            grad_b_outer,
        ]
    )
    grad_inner_vec = jnp.stack([grad_b_inner, grad_gain_ff, grad_shift_ff])
    grad_heads = jnp.concatenate([grad_table, grad_head_scale[None, :]], axis=0)
    tokens_all = 2 * num_seq * P_SIZE * lax.axis_size("dp")
    local_grad = (
        jnp.concatenate(
            [
                grad_w_query.reshape(-1),
                grad_w_key.reshape(-1),
                grad_w_value.reshape(-1),
                grad_w_out.reshape(-1),
                grad_w_inner.reshape(-1),
                grad_w_outer.reshape(-1),
                grad_model_vec.reshape(-1),
                grad_inner_vec.reshape(-1),
                grad_heads.reshape(-1),
            ]
        )
        / tokens_all
    )
    if fast:
        table = local_grad.reshape(-1, D)
        low = table[: 2 * PHASE_ROWS].astype(BF)
        second = reduce_phase(scatter(1, spot, low[PHASE_ROWS:]))
        first = reduce_phase(scatter(0, spot, low[:PHASE_ROWS]))
        vec_grad = sum_all_small(jnp.pad(table[2 * PHASE_ROWS :], ((0, 1), (0, 0))))
        grad_shard = unpack_shard(first, second, vec_grad, side, place)
    else:
        half_size = local_grad.shape[0] // 2
        own_half = lax.dynamic_slice_in_dim(local_grad, side * half_size, half_size)
        other_half = lax.dynamic_slice_in_dim(local_grad, (1 - side) * half_size, half_size)
        partner_half = from_partner(other_half.astype(jnp.bfloat16), "mod", 0).astype(other_half.dtype)
        grad_shard = lax.psum_scatter(own_half + partner_half, "dp", scatter_dimension=0, tiled=True)
    square_sum = lax.psum(jnp.sum(grad_shard * grad_shard), ("mod", "dp"))
    grad_norm = jnp.sqrt(square_sum)
    clip_scale = jnp.minimum(1.0, 0.25 / (grad_norm + 1e-06))
    clipped = grad_shard * clip_scale
    new_first = 0.5 * first_moment + 0.5 * clipped
    new_second = 0.6 * second_moment + 0.4 * clipped * clipped
    direction = new_first / (1.0 - 0.5**STEP) / (jnp.sqrt(new_second / (1.0 - 0.6**STEP)) + 1e-08)
    new_master = master - 0.04 * (direction + 0.01 * master)
    new_average = 0.5 * average + 0.5 * new_master
    return (
        result_rows,
        grad_rows,
        grad_norm,
        new_master,
        new_first,
        new_second,
        new_average,
        new_master.astype(jnp.bfloat16),
    )


def solution(mesh):
    placed = (
        P("mod", "dp", None, None),
        P("mod", "dp", None, None),
        P(("mod", "dp")),
        P(("mod", "dp")),
        P(("mod", "dp")),
        P(("mod", "dp")),
        P("dp"),
        P(),
    )
    return jax.shard_map(
        on_device,
        mesh=mesh,
        in_specs=placed,
        out_specs=(
            P("mod", "dp", None, None),
            P("mod", "dp", None, None),
            P(),
            P(("mod", "dp")),
            P(("mod", "dp")),
            P(("mod", "dp")),
            P(("mod", "dp")),
            P(("mod", "dp")),
        ),
        check_vma=False,
    )
```

```python
import functools
import jax
import jax.numpy as jnp
from jax import lax
from jax.experimental import pallas as pl
from jax.experimental.pallas import tpu as pltpu
from jax.sharding import PartitionSpec as P

D = 768
H = 12
HD = 64
FF = 3072
NB = 63
P_SIZE = 196
STEP = 5


HALF = D // 2
BLOCK = 144
PHASE_ROWS = 32 * BLOCK
BF = jnp.bfloat16
F32 = jnp.float32
DP = 16
EDGE = 17664
PAD = 208
KEYS = 512
HALF_KEYS = KEYS // 2
PAIR = 2 * HD


def x_swap():
    return [(i, i ^ 1) for i in range(DP)]


def y_swap():
    return [(i, i ^ 2) for i in range(DP)]


def z_turn(step):
    return [(i, (i // 4 + step) % 4 * 4 + i % 4) for i in range(DP)]


def send_dp(block, route):
    return lax.ppermute(block, "dp", route)


def send_mod(block):
    return lax.ppermute(block, "mod", [(0, 1), (1, 0)])


def pack_shard(own, side, place):
    lead = 8832 * side + 552 * place
    count = BLOCK * D
    lent = lax.dynamic_slice(own, (count - lead,), (count,))
    given = send_mod(lent)
    nxt = [(i, i + 1) for i in range(2 * DP - 1)]
    edge = lax.ppermute(own[own.shape[0] - EDGE :], ("mod", "dp"), nxt)
    kept = lax.dynamic_slice(jnp.concatenate([edge, own[:count]]), (EDGE - lead,), (count,))
    kept = kept.reshape(BLOCK, D)
    given = given.reshape(BLOCK, D)
    return jnp.where(side == 0, kept, given), jnp.where(side == 0, given, kept)


def unpack_shard(first, second, vec, side, place):
    lead = 8832 * side + 552 * place
    even = jnp.where(side == 0, first, second).reshape(-1)
    lent = jnp.where(side == 0, second, first)
    odd = send_mod(lent).reshape(-1)
    back = [(i + 1, i) for i in range(2 * DP - 1)]
    edge = lax.ppermute(even[:EDGE], ("mod", "dp"), back)
    is_last = jnp.logical_and(side == 1, place == DP - 1)
    edge = jnp.where(is_last, vec.reshape(-1)[:EDGE], edge)
    return lax.dynamic_slice(jnp.concatenate([even, odd, edge]), (lead,), (221736,))


def sum_all_small(part):
    for route in (x_swap(), y_swap(), z_turn(2)):
        part = part + send_dp(part, route)
    part = part + send_dp(part, [(i, i ^ 4) for i in range(DP)])
    return part + send_mod(part)


def gather_phase(block):
    stack = jnp.stack([block] + [send_dp(block, z_turn(step)) for step in (1, 2, 3)])
    left, right = stack[:, :, :HALF], stack[:, :, HALF:]
    left_x = send_dp(left, x_swap())
    right_y = send_dp(right, y_swap())
    left_y = send_dp(left, y_swap())
    right_x = send_dp(right, x_swap())
    left_xy = send_dp(left_x, y_swap())
    right_xy = send_dp(right_y, x_swap())
    mine = [left, left_x, left_y, left_xy, right, right_x, right_y, right_xy]
    return mine + [send_mod(piece) for piece in mine]


def coords():
    side = lax.axis_index("mod")
    place = lax.axis_index("dp")
    return jnp.stack([side, place // 4, place // 2 % 2, place % 2]).astype(jnp.int32)


def assemble_body(phase, spot, *refs):
    pieces, out, sem = refs[:16], refs[16], refs[17]
    side, z, y, x = spot[0], spot[1], spot[2], spot[3]
    copies = []
    for index in range(16):
        other, half, yr, xr = index // 8, index // 4 % 2, index // 2 % 2, index % 2
        owner = side ^ other
        parity = owner if phase == 0 else 1 - owner
        for turn in range(4):
            home = ((z - turn) & 3) * 4 + (y ^ yr) * 2 + (x ^ xr)
            copies.append(
                pltpu.make_async_copy(
                    pieces[index].at[turn],
                    out.at[home * 2 + parity, :, pl.ds(half * HALF, HALF)],
                    sem.at[index * 4 + turn],
                )
            )
    for copy in copies:
        copy.start()
    for copy in copies:
        copy.wait()


def assemble(phase, spot, pieces):
    return pl.pallas_call(
        functools.partial(assemble_body, phase),
        out_shape=jax.ShapeDtypeStruct((32, BLOCK, D), BF),
        in_specs=[pl.BlockSpec(memory_space=pltpu.SMEM)] + [pl.BlockSpec(memory_space=pl.ANY)] * 16,
        out_specs=pl.BlockSpec(memory_space=pltpu.VMEM),
        scratch_shapes=[pltpu.SemaphoreType.DMA((64,))],
        name="assemble",
    )(spot, *pieces).reshape(PHASE_ROWS, D)


def scatter_body(phase, pieces, spot, *refs):
    sources, out, sem = refs[:-2], refs[-2], refs[-1]
    side, z, y, x = spot[0], spot[1], spot[2], spot[3]
    copies = []
    for block in range(32):
        home, parity = block // 2, block % 2
        owner = parity if phase == 0 else 1 - parity
        other = side ^ owner
        turn = (home // 4 - z) & 3
        yr = (home // 2 % 2) ^ y
        xr = (home % 2) ^ x
        for index, source_row, block_row, count in pieces[block]:
            for half in range(2):
                copies.append(
                    pltpu.make_async_copy(
                        sources[index].at[pl.ds(source_row, count), pl.ds(half * HALF, HALF)],
                        out.at[other, half, yr, xr, turn, pl.ds(block_row, count), :],
                        sem.at[len(copies)],
                    )
                )
    for copy in copies:
        copy.start()
    for copy in copies:
        copy.wait()


def scatter(phase, spot, tables):
    starts = [0]
    for table in tables:
        starts.append(starts[-1] + table.shape[0])
    pieces = []
    for block in range(32):
        low = phase * PHASE_ROWS + block * BLOCK
        parts = []
        for index in range(len(tables)):
            first, last = max(low, starts[index]), min(low + BLOCK, starts[index + 1])
            if first < last:
                parts.append((index, first - starts[index], first - low, last - first))
        pieces.append(parts)
    used = sorted({part[0] for parts in pieces for part in parts})
    pieces = [[(used.index(part[0]),) + part[1:] for part in parts] for parts in pieces]
    count = 2 * sum(len(parts) for parts in pieces)
    return pl.pallas_call(
        functools.partial(scatter_body, phase, pieces),
        out_shape=jax.ShapeDtypeStruct((2, 2, 2, 2, 4, BLOCK, HALF), BF),
        in_specs=[pl.BlockSpec(memory_space=pltpu.SMEM)]
        + [pl.BlockSpec(memory_space=pl.ANY)] * len(used),
        out_specs=pl.BlockSpec(memory_space=pl.ANY),
        scratch_shapes=[pltpu.SemaphoreType.DMA((count,))],
        name="scatter",
    )(spot, *[tables[index] for index in used])


def plus(left, right):
    return (left.astype(F32) + right.astype(F32)).astype(BF)


def reduce_phase(parts):
    theirs = send_mod(parts[1])
    left_out = send_dp(plus(parts[0, 0, :, 1], theirs[0, :, 1]), x_swap())
    right_out = send_dp(plus(parts[0, 1, 1], theirs[1, 1]), y_swap())
    left_in = plus(parts[0, 0, :, 0], theirs[0, :, 0])
    right_in = plus(parts[0, 1, 0], theirs[1, 0])
    left_next = send_dp(plus(left_in[1], left_out[1]), y_swap())
    right_next = send_dp(plus(right_in[1], right_out[1]), x_swap())
    left = left_in[0].astype(F32) + left_out[0].astype(F32) + left_next.astype(F32)
    right = right_in[0].astype(F32) + right_out[0].astype(F32) + right_next.astype(F32)
    both = jnp.concatenate([left, right], axis=-1)
    low = both.astype(BF)
    total = both[0]
    for step in (1, 2, 3):
        total = total + send_dp(low[step], z_turn(step)).astype(F32)
    return total


def dot_f32(left, right, dims):
    return lax.dot_general(left, right, (dims, ((), ())), preferred_element_type=F32)


NN = ((1,), (0,))
NT = ((1,), (1,))
TN = ((0,), (0,))


def bias_of(table_ref, ids_ref, head):
    entry = jnp.broadcast_to(table_ref[pl.ds(head, 1), :], (PAD, 128))
    return [
        jnp.take_along_axis(
            entry, ids_ref[:, c * 128 : (c + 1) * 128], axis=1, mode="promise_in_bounds"
        )
        for c in range(KEYS // 128)
    ]


def joint_keys(own_ref, other_ref, seq):
    rows = pl.ds(seq * PAD, PAD)
    gap = jnp.zeros((HALF_KEYS - PAD, PAIR), BF)
    return jnp.concatenate([own_ref[rows, :], gap, other_ref[rows, :], gap], axis=0)


def key_mask(counts_ref, seq):
    lane = lax.broadcasted_iota(jnp.int32, (1, KEYS), 1)
    own, other = counts_ref[seq], counts_ref[2 + seq]
    return jnp.logical_or(
        lane < own, jnp.logical_and(lane >= HALF_KEYS, lane < HALF_KEYS + other)
    )


def half_only(values, part):
    lane = lax.broadcasted_iota(jnp.int32, values.shape, 1)
    keep = lane < HD if part == 0 else lane >= HD
    return jnp.where(keep, values, jnp.zeros((), values.dtype))


def attend_body(counts, ids, table, query, key_own, key_other, value_own, value_other, out, logs):
    pair = pl.program_id(0)
    keys = [joint_keys(key_own, key_other, seq) for seq in range(2)]
    values = [joint_keys(value_own, value_other, seq) for seq in range(2)]
    masks = [key_mask(counts, seq) for seq in range(2)]
    lane = lax.broadcasted_iota(jnp.int32, (PAD, 128), 1)
    done = [None, None]
    for part in range(2):
        head = 2 * pair + part
        bias = jnp.concatenate(bias_of(table, ids, head), axis=1)
        for seq in range(2):
            rows = pl.ds(seq * PAD, PAD)
            scores = dot_f32(half_only(query[rows, :], part), keys[seq], NT) * 0.125 + bias
            scores = jnp.where(masks[seq], scores, -1e30)
            top = jnp.max(scores, axis=1, keepdims=True)
            powers = jnp.exp(scores - top)
            total = jnp.sum(powers, axis=1, keepdims=True)
            probs = (powers * (1.0 / total)).astype(BF)
            got = dot_f32(probs, values[seq], NN)
            done[seq] = got if part == 0 else jnp.where(lane < HD, done[seq], got)
            logs[rows, :] = jnp.where(lane == head, top + jnp.log(total), logs[rows, :])
    for seq in range(2):
        out[pl.ds(seq * PAD, PAD), :] = done[seq]


def fixed(shape):
    return pl.BlockSpec(shape, lambda i: (0,) * len(shape))


def by_pair():
    return pl.BlockSpec((2 * PAD, PAIR), lambda i: (0, i))


def attend(counts, ids, table, query, key_own, key_other, value_own, value_other):
    return pl.pallas_call(
        attend_body,
        grid=(H // 2,),
        out_shape=(
            jax.ShapeDtypeStruct((2 * PAD, D), F32),
            jax.ShapeDtypeStruct((2 * PAD, 128), F32),
        ),
        in_specs=[pl.BlockSpec(memory_space=pltpu.SMEM), fixed((PAD, KEYS)), fixed((16, 128))]
        + [by_pair()] * 5,
        out_specs=(by_pair(), fixed((2 * PAD, 128))),
        name="attend",
    )(counts, ids, table, query, key_own, key_other, value_own, value_other)


def attend_back_body(
    counts, ids, table, logs, query, key_own, key_other, value_own, value_other, grad,
    grad_query, grad_key_own, grad_value_own, grad_key_other, grad_value_other, terms,
):
    pair = pl.program_id(0)
    keys = [joint_keys(key_own, key_other, seq) for seq in range(2)]
    values = [joint_keys(value_own, value_other, seq) for seq in range(2)]
    masks = [key_mask(counts, seq) for seq in range(2)]
    lane = lax.broadcasted_iota(jnp.int32, (PAD, 128), 1)
    to_query, to_key, to_value = [0.0, 0.0], [0.0, 0.0], [0.0, 0.0]
    for part in range(2):
        head = 2 * pair + part
        bias = jnp.concatenate(bias_of(table, ids, head), axis=1)
        both = 0.0
        for seq in range(2):
            rows = pl.ds(seq * PAD, PAD)
            asked = half_only(query[rows, :], part)
            into = half_only(grad[rows, :], part)
            scores = dot_f32(asked, keys[seq], NT) * 0.125 + bias
            scores = jnp.where(masks[seq], scores, -1e30)
            log = jnp.sum(jnp.where(lane == head, logs[rows, :], 0.0), axis=1, keepdims=True)
            probs = jnp.exp(scores - log)
            grad_probs = dot_f32(into, values[seq], NT)
            mean = jnp.sum(probs * grad_probs, axis=1, keepdims=True)
            grad_scores = (probs * (grad_probs - mean)).astype(BF)
            both = both + grad_scores.astype(F32)
            to_value[seq] = to_value[seq] + dot_f32(probs.astype(BF), into, TN)
            to_query[seq] = to_query[seq] + dot_f32(grad_scores, half_only(keys[seq], part), NN)
            to_key[seq] = to_key[seq] + dot_f32(grad_scores, asked, TN)
        for c in range(KEYS // 128):
            terms[c, pl.ds(head, PAD, stride=16), :] = both[:, c * 128 : (c + 1) * 128]
    for seq in range(2):
        rows = pl.ds(seq * PAD, PAD)
        grad_query[rows, :] = (to_query[seq] * 0.125).astype(BF)
        grad_key_own[rows, :] = to_key[seq][:PAD] * 0.125
        grad_key_other[rows, :] = (to_key[seq][HALF_KEYS : HALF_KEYS + PAD] * 0.125).astype(BF)
        grad_value_own[rows, :] = to_value[seq][:PAD]
        grad_value_other[rows, :] = to_value[seq][HALF_KEYS : HALF_KEYS + PAD].astype(BF)


def attend_back(counts, ids, table, logs, query, keys, values, grad):
    def rows_of(kind):
        return jax.ShapeDtypeStruct((2 * PAD, D), kind)

    return pl.pallas_call(
        attend_back_body,
        grid=(H // 2,),
        out_shape=(
            rows_of(BF),
            rows_of(F32),
            rows_of(F32),
            rows_of(BF),
            rows_of(BF),
            jax.ShapeDtypeStruct((KEYS // 128, PAD * 16, 128), F32),
        ),
        in_specs=[
            pl.BlockSpec(memory_space=pltpu.SMEM),
            fixed((PAD, KEYS)),
            fixed((16, 128)),
            fixed((2 * PAD, 128)),
        ]
        + [by_pair()] * 6,
        out_specs=(by_pair(),) * 5 + (fixed((KEYS // 128, PAD * 16, 128)),),
        name="attend_back",
    )(counts, ids, table, logs, query, *keys, *values, grad)


GROUP = 4


def table_body(ids, terms, out):
    bucket = lax.broadcasted_iota(jnp.int32, (NB + 1, KEYS), 0)

    def step(index, totals):
        fresh = []
        for lane_group in range(GROUP):
            row = index * GROUP + lane_group
            hot = jnp.where(ids[pl.ds(row, 1), :] == bucket, 1.0, 0.0).astype(BF)
            start = pl.multiple_of(row * 16, 16)
            term = jnp.concatenate(
                [terms[c, pl.ds(start, 16), :] for c in range(KEYS // 128)], axis=1
            )
            high = term.astype(BF)
            low = (term - high.astype(F32)).astype(BF)
            both = jnp.concatenate([high, low], axis=0)
            fresh.append(totals[lane_group] + dot_f32(hot, both, NT))
        return tuple(fresh)

    zero = jnp.zeros((NB + 1, 32), F32)
    totals = lax.fori_loop(0, P_SIZE // GROUP, step, (zero,) * GROUP)
    total = totals[0] + totals[1] + totals[2] + totals[3]
    out[...] = total


def table_grad(ids, terms):
    whole = pl.BlockSpec(memory_space=pltpu.VMEM)
    both = pl.pallas_call(
        table_body,
        out_shape=jax.ShapeDtypeStruct((NB + 1, 32), F32),
        in_specs=[whole, whole],
        out_specs=whole,
        name="table_grad",
    )(ids, terms)
    return both[:NB, :H] + both[:NB, 16 : 16 + H]


def from_partner(block, axis, bit):
    count = lax.axis_size(axis)
    route = []
    for low in range(count):
        high = low | 1 << bit
        if high != low and high < count:
            route += [(low, high), (high, low)]
    return lax.ppermute(block, axis, route)


def layer_norm(values, gain, shift):
    center = values - jnp.mean(values, axis=-1, keepdims=True)
    spread = jnp.mean(center * center, axis=-1, keepdims=True)
    return center * lax.rsqrt(spread + 1e-05) * gain + shift


def norm_back(values, gain, shift, grad_after):
    _, pullback = jax.vjp(layer_norm, values, gain, shift)
    return pullback(grad_after)


def matmul(left, right):
    return jnp.dot(left, right, preferred_element_type=jnp.float32)


def matmul_tn(left, right):
    return lax.dot_general(
        left, right, (((0,), (0,)), ((), ())), preferred_element_type=jnp.float32
    )


def matmul_nt(left, right):
    return lax.dot_general(
        left, right, (((1,), (1,)), ((), ())), preferred_element_type=jnp.float32
    )


def exact_gelu(values):
    return jax.nn.gelu(values, approximate=False)


def unpack(flat):
    pairs = [(D, D), (D, D), (D, D), (D, D), (D, FF), (FF, D), (10, D), (3, FF), (NB + 1, H)]
    pieces = []
    offset = 0
    for dims_pair in pairs:
        extent = dims_pair[0] * dims_pair[1]
        pieces.append(flat[offset : offset + extent].reshape(dims_pair))
        offset += extent
    return pieces


def unpack_tables(first, second, vec):
    square = [first[i * D : (i + 1) * D] for i in range(4)]
    cut = PHASE_ROWS - 4 * D
    w_inner = jnp.concatenate(
        [first[4 * D :].reshape(cut // 4, FF), second[: FF - cut].reshape(D - cut // 4, FF)]
    )
    return square + [
        w_inner,
        second[FF - cut :],
        vec[:10],
        vec[10:22].reshape(3, FF),
        vec[22].reshape(NB + 1, H),
    ]


def widen(values):
    return jnp.pad(values, ((0, 0), (0, PAD - P_SIZE), (0, 0))).reshape(2 * PAD, D)


def narrow(values):
    return values.reshape(1, 2, PAD, D)[:, :, :P_SIZE]


def on_device(rows, cotangent, master, first_moment, second_moment, average, lengths, buckets):
    side = lax.axis_index("mod")
    place = lax.axis_index("dp")
    fast = lax.axis_size("dp") == DP
    own_copy = master.astype(jnp.bfloat16)
    if fast:
        spot = coords()
        first, second = pack_shard(own_copy, side, place)
        is_last = jnp.logical_and(side == 1, place == DP - 1)
        vec = jnp.where(is_last, own_copy[-EDGE:], jnp.zeros((), BF))
        vec = jnp.pad(vec, (0, D)).reshape(24, D)
        weights = unpack_tables(
            assemble(0, spot, gather_phase(first)),
            assemble(1, spot, gather_phase(second)),
            sum_all_small(vec),
        )
    else:
        weights = unpack(lax.all_gather(own_copy, ("mod", "dp"), axis=0, tiled=True))
    w_query, w_key, w_value, w_out, w_inner, w_outer, vec_model, vec_inner, head_table = weights
    model_vec = vec_model.astype(jnp.float32)
    inner_vec = vec_inner.astype(jnp.float32)
    head_vals = head_table.astype(jnp.float32)
    scale_row = jnp.repeat(head_vals[NB], HD)
    table = jnp.pad(head_vals.T, ((0, 16 - H), (0, 128 - NB - 1)))
    full = jnp.full_like(lengths, P_SIZE)
    own_count = jnp.where(side == 0, full, lengths)
    other_count = jnp.where(side == 0, lengths, full)
    counts = jnp.concatenate([own_count, other_count]).astype(jnp.int32)
    slots = jnp.arange(PAD, dtype=jnp.int32)
    own_valid = (slots[None, :] < own_count[:, None]).astype(F32).reshape(2 * PAD, 1)
    near = lax.dynamic_slice(buckets, (side * P_SIZE, side * P_SIZE), (P_SIZE, P_SIZE))
    far = lax.dynamic_slice(buckets, (side * P_SIZE, (1 - side) * P_SIZE), (P_SIZE, P_SIZE))
    room = ((0, PAD - P_SIZE), (0, HALF_KEYS - P_SIZE))
    ids = jnp.concatenate([jnp.pad(near, room), jnp.pad(far, room)], axis=1)

    inputs = widen(rows[0]).astype(F32)
    normed = layer_norm(inputs, model_vec[0], model_vec[1])
    normed_low = normed.astype(BF)
    keys_own = matmul(normed_low, w_key).astype(BF)
    values_own = (matmul(normed_low, w_value) + model_vec[3]).astype(BF)
    keys_other, values_other = from_partner((keys_own, values_own), "mod", 0)
    query = (matmul(normed_low, w_query) + model_vec[2]).astype(BF)
    keys_both, values_both = (keys_own, keys_other), (values_own, values_other)
    attended, logs = attend(counts, ids, table, query, *keys_both, *values_both)

    scaled = attended * scale_row
    mixed = layer_norm(scaled, model_vec[4], model_vec[5])
    mixed_low = mixed.astype(BF)
    middle = inputs + (matmul(mixed_low, w_out) + model_vec[6])
    normed_two = layer_norm(middle, model_vec[7], model_vec[8])
    normed_two_low = normed_two.astype(BF)
    inner = matmul(normed_two_low, w_inner) + inner_vec[0]
    activated = exact_gelu(inner)
    inner_normed = layer_norm(activated, inner_vec[1], inner_vec[2])
    inner_low = inner_normed.astype(BF)
    result = middle + (matmul(inner_low, w_outer) + model_vec[9])
    result_rows = narrow(result.astype(BF))

    tokens_all = 2 * rows.shape[1] * P_SIZE * lax.axis_size("dp")
    share = 1.0 / tokens_all

    def weight_grad(left, right):
        value = matmul_tn(left, right) * share
        return value.astype(BF) if fast else value

    grad_out = widen(cotangent[0]).astype(F32) * own_valid
    grad_branch = grad_out.astype(BF)
    grad_w_outer = weight_grad(inner_low, grad_branch)
    grad_b_outer = jnp.sum(grad_branch.astype(F32), axis=0)
    grad_inner_normed = matmul_nt(grad_branch, w_outer)
    grad_activated, grad_gain_ff, grad_shift_ff = norm_back(
        activated, inner_vec[1], inner_vec[2], grad_inner_normed
    )
    _, gelu_pull = jax.vjp(exact_gelu, inner)
    grad_inner_low = gelu_pull(grad_activated)[0].astype(BF)
    grad_w_inner = weight_grad(normed_two_low, grad_inner_low)
    grad_b_inner = jnp.sum(grad_inner_low.astype(F32), axis=0)
    grad_normed_two = matmul_nt(grad_inner_low, w_inner)
    grad_mid_part, grad_gain_two, grad_shift_two = norm_back(
        middle, model_vec[7], model_vec[8], grad_normed_two
    )
    grad_middle = grad_out + grad_mid_part
    grad_attn_low = grad_middle.astype(BF)
    grad_w_out = weight_grad(mixed_low, grad_attn_low)
    grad_b_out = jnp.sum(grad_attn_low.astype(F32), axis=0)
    grad_mixed = matmul_nt(grad_attn_low, w_out)
    grad_scaled, grad_gain_attn, grad_shift_attn = norm_back(
        scaled, model_vec[4], model_vec[5], grad_mixed
    )
    grad_head_scale = jnp.sum(jnp.sum(grad_scaled * attended, axis=0).reshape(H, HD), axis=1)
    grad_attended = (grad_scaled * scale_row).astype(BF)
    grad_query, key_kept, value_kept, key_sent, value_sent, terms = attend_back(
        counts, ids, table, logs, query, keys_both, values_both, grad_attended
    )
    back_keys, back_values = from_partner((key_sent, value_sent), "mod", 0)
    grad_key = (key_kept + back_keys.astype(F32)).astype(BF)
    grad_value = (value_kept + back_values.astype(F32)).astype(BF)
    grad_table = table_grad(ids, terms)
    grad_w_query = weight_grad(normed_low, grad_query)
    grad_w_key = weight_grad(normed_low, grad_key)
    grad_w_value = weight_grad(normed_low, grad_value)
    grad_b_query = jnp.sum(grad_query.astype(F32), axis=0)
    grad_b_value = jnp.sum(grad_value.astype(F32), axis=0)
    grad_normed = (
        matmul_nt(grad_query, w_query) + matmul_nt(grad_key, w_key) + matmul_nt(grad_value, w_value)
    )
    grad_in_part, grad_gain_one, grad_shift_one = norm_back(
        inputs, model_vec[0], model_vec[1], grad_normed
    )
    grad_rows = narrow(grad_middle + grad_in_part)
    grad_model_vec = jnp.stack(
        [
            grad_gain_one,
            grad_shift_one,
            grad_b_query,
            grad_b_value,
            grad_gain_attn,
            grad_shift_attn,
            grad_b_out,
            grad_gain_two,
            grad_shift_two,
            grad_b_outer,
        ]
    )
    grad_inner_vec = jnp.stack([grad_b_inner, grad_gain_ff, grad_shift_ff])
    grad_heads = jnp.concatenate([grad_table, grad_head_scale[None, :]], axis=0)
    vec_grad = (
        jnp.concatenate(
            [grad_model_vec, grad_inner_vec.reshape(12, D), grad_heads.reshape(1, D)], axis=0
        )
        * share
    )
    matrices = [grad_w_query, grad_w_key, grad_w_value, grad_w_out]
    matrices += [grad_w_inner.reshape(FF, D), grad_w_outer]
    if fast:
        second = reduce_phase(scatter(1, spot, matrices))
        first = reduce_phase(scatter(0, spot, matrices))
        vec_grad = sum_all_small(jnp.pad(vec_grad, ((0, 1), (0, 0))))
        square = jnp.sum(first * first) + jnp.sum(second * second)
        square = square + jnp.where(is_last, jnp.sum(vec_grad * vec_grad), 0.0)
        square_sum = sum_all_small(jnp.full((8, 128), square))[0, 0]
        grad_shard = unpack_shard(first, second, vec_grad, side, place)
    else:
        local_grad = jnp.concatenate([part.reshape(-1) for part in matrices + [vec_grad]])
        half_size = local_grad.shape[0] // 2
        own_half = lax.dynamic_slice_in_dim(local_grad, side * half_size, half_size)
        other_half = lax.dynamic_slice_in_dim(local_grad, (1 - side) * half_size, half_size)
        partner_half = from_partner(other_half.astype(BF), "mod", 0).astype(F32)
        grad_shard = lax.psum_scatter(own_half + partner_half, "dp", scatter_dimension=0, tiled=True)
        square_sum = lax.psum(jnp.sum(grad_shard * grad_shard), ("mod", "dp"))
    grad_norm = jnp.sqrt(square_sum)
    clip_scale = jnp.minimum(1.0, 0.25 / (grad_norm + 1e-06))
    clipped = grad_shard * clip_scale
    new_first = 0.5 * first_moment + 0.5 * clipped
    new_second = 0.6 * second_moment + 0.4 * clipped * clipped
    direction = new_first / (1.0 - 0.5**STEP) / (jnp.sqrt(new_second / (1.0 - 0.6**STEP)) + 1e-08)
    new_master = master - 0.04 * (direction + 0.01 * master)
    new_average = 0.5 * average + 0.5 * new_master
    return (
        result_rows,
        grad_rows,
        grad_norm,
        new_master,
        new_first,
        new_second,
        new_average,
        new_master.astype(jnp.bfloat16),
    )


def solution(mesh):
    placed = (
        P("mod", "dp", None, None),
        P("mod", "dp", None, None),
        P(("mod", "dp")),
        P(("mod", "dp")),
        P(("mod", "dp")),
        P(("mod", "dp")),
        P("dp"),
        P(),
    )
    return jax.shard_map(
        on_device,
        mesh=mesh,
        in_specs=placed,
        out_specs=(
            P("mod", "dp", None, None),
            P("mod", "dp", None, None),
            P(),
            P(("mod", "dp")),
            P(("mod", "dp")),
            P(("mod", "dp")),
            P(("mod", "dp")),
            P(("mod", "dp")),
        ),
        check_vma=False,
    )
```

```python
import functools
import jax
import jax.numpy as jnp
from jax import lax
from jax.experimental import pallas as pl
from jax.experimental.pallas import tpu as pltpu
from jax.sharding import PartitionSpec as P

D = 768
H = 12
HD = 64
FF = 3072
NB = 63
P_SIZE = 196
STEP = 5


HALF = D // 2
BLOCK = 144
PHASE_ROWS = 32 * BLOCK
BF = jnp.bfloat16
F32 = jnp.float32
DP = 16
EDGE = 17664
PAD = 208
KEYS = 512
HALF_KEYS = KEYS // 2
PAIR = 2 * HD


def x_swap():
    return [(i, i ^ 1) for i in range(DP)]


def y_swap():
    return [(i, i ^ 2) for i in range(DP)]


def z_turn(step):
    return [(i, (i // 4 + step) % 4 * 4 + i % 4) for i in range(DP)]


def send_dp(block, route):
    return lax.ppermute(block, "dp", route)


def send_mod(block):
    return lax.ppermute(block, "mod", [(0, 1), (1, 0)])


def pack_shard(own, side, place):
    lead = 8832 * side + 552 * place
    count = BLOCK * D
    lent = lax.dynamic_slice(own, (count - lead,), (count,))
    given = send_mod(lent)
    nxt = [(i, i + 1) for i in range(2 * DP - 1)]
    edge = lax.ppermute(own[own.shape[0] - EDGE :], ("mod", "dp"), nxt)
    kept = lax.dynamic_slice(jnp.concatenate([edge, own[:count]]), (EDGE - lead,), (count,))
    kept = kept.reshape(BLOCK, D)
    given = given.reshape(BLOCK, D)
    return jnp.where(side == 0, kept, given), jnp.where(side == 0, given, kept)


def unpack_shard(first, second, vec, side, place):
    lead = 8832 * side + 552 * place
    even = jnp.where(side == 0, first, second).reshape(-1)
    lent = jnp.where(side == 0, second, first)
    odd = send_mod(lent).reshape(-1)
    back = [(i + 1, i) for i in range(2 * DP - 1)]
    edge = lax.ppermute(even[:EDGE], ("mod", "dp"), back)
    is_last = jnp.logical_and(side == 1, place == DP - 1)
    edge = jnp.where(is_last, vec.reshape(-1)[:EDGE], edge)
    return lax.dynamic_slice(jnp.concatenate([even, odd, edge]), (lead,), (221736,))


def sum_all_small(part):
    for route in (x_swap(), y_swap(), z_turn(2)):
        part = part + send_dp(part, route)
    part = part + send_dp(part, [(i, i ^ 4) for i in range(DP)])
    return part + send_mod(part)


def gather_phase(block):
    stack = jnp.stack([block] + [send_dp(block, z_turn(step)) for step in (1, 2, 3)])
    left, right = stack[:, :, :HALF], stack[:, :, HALF:]
    left_x = send_dp(left, x_swap())
    right_y = send_dp(right, y_swap())
    left_y = send_dp(left, y_swap())
    right_x = send_dp(right, x_swap())
    left_xy = send_dp(left_x, y_swap())
    right_xy = send_dp(right_y, x_swap())
    mine = [left, left_x, left_y, left_xy, right, right_x, right_y, right_xy]
    return mine + [send_mod(piece) for piece in mine]


def coords():
    side = lax.axis_index("mod")
    place = lax.axis_index("dp")
    return jnp.stack([side, place // 4, place // 2 % 2, place % 2]).astype(jnp.int32)


def assemble_body(phase, spot, *refs):
    pieces, out, sem = refs[:16], refs[16], refs[17]
    side, z, y, x = spot[0], spot[1], spot[2], spot[3]
    copies = []
    for index in range(16):
        other, half, yr, xr = index // 8, index // 4 % 2, index // 2 % 2, index % 2
        owner = side ^ other
        parity = owner if phase == 0 else 1 - owner
        for turn in range(4):
            home = ((z - turn) & 3) * 4 + (y ^ yr) * 2 + (x ^ xr)
            copies.append(
                pltpu.make_async_copy(
                    pieces[index].at[turn],
                    out.at[home * 2 + parity, :, pl.ds(half * HALF, HALF)],
                    sem.at[index * 4 + turn],
                )
            )
    for copy in copies:
        copy.start()
    for copy in copies:
        copy.wait()


def assemble(phase, spot, pieces):
    return pl.pallas_call(
        functools.partial(assemble_body, phase),
        out_shape=jax.ShapeDtypeStruct((32, BLOCK, D), BF),
        in_specs=[pl.BlockSpec(memory_space=pltpu.SMEM)] + [pl.BlockSpec(memory_space=pl.ANY)] * 16,
        out_specs=pl.BlockSpec(memory_space=pltpu.VMEM),
        scratch_shapes=[pltpu.SemaphoreType.DMA((64,))],
        name="assemble",
    )(spot, *pieces).reshape(PHASE_ROWS, D)


def scatter_body(phase, pieces, spot, *refs):
    sources, kept, lent, sem = refs[:-3], refs[-3], refs[-2], refs[-1]
    side, z, y, x = spot[0], spot[1], spot[2], spot[3]
    copies = []
    for block in range(32):
        home, parity = block // 2, block % 2
        owner = parity if phase == 0 else 1 - parity
        turn = (home // 4 - z) & 3
        yr = (home // 2 % 2) ^ y
        xr = (home % 2) ^ x
        for index, source_row, block_row, count in pieces[block]:
            for half in range(2):
                stay, leave = [
                    pltpu.make_async_copy(
                        sources[index].at[pl.ds(source_row, count), pl.ds(half * HALF, HALF)],
                        target.at[half, yr, xr, turn, pl.ds(block_row, count), :],
                        sem.at[len(copies)],
                    )
                    for target in (kept, lent)
                ]
                pl.when(side == owner)(stay.start)
                pl.when(side != owner)(leave.start)
                copies.append(stay)
    for copy in copies:
        copy.wait()


def scatter(phase, spot, tables):
    starts = [0]
    for rows in (D, D, D, D, FF, FF):
        starts.append(starts[-1] + rows)
    pieces = []
    for block in range(32):
        low = phase * PHASE_ROWS + block * BLOCK
        parts = []
        for index in range(len(tables)):
            first, last = max(low, starts[index]), min(low + BLOCK, starts[index + 1])
            if first < last:
                parts.append((index, first - starts[index], first - low, last - first))
        pieces.append(parts)
    used = sorted({part[0] for parts in pieces for part in parts})
    pieces = [[(used.index(part[0]),) + part[1:] for part in parts] for parts in pieces]
    count = 2 * sum(len(parts) for parts in pieces)
    return pl.pallas_call(
        functools.partial(scatter_body, phase, pieces),
        out_shape=(jax.ShapeDtypeStruct((2, 2, 2, 4, BLOCK, HALF), BF),) * 2,
        in_specs=[pl.BlockSpec(memory_space=pltpu.SMEM)]
        + [pl.BlockSpec(memory_space=pltpu.VMEM)] * len(used),
        out_specs=(pl.BlockSpec(memory_space=pl.ANY),) * 2,
        scratch_shapes=[pltpu.SemaphoreType.DMA((count,))],
        name="scatter",
    )(spot, *[tables[index] for index in used])


def plus(left, right):
    return (left.astype(F32) + right.astype(F32)).astype(BF)


def reduce_phase(mine, theirs):
    left_out = send_dp(plus(mine[0, :, 1], theirs[0, :, 1]), x_swap())
    right_out = send_dp(plus(mine[1, 1], theirs[1, 1]), y_swap())
    left_in = plus(mine[0, :, 0], theirs[0, :, 0])
    right_in = plus(mine[1, 0], theirs[1, 0])
    left_next = send_dp(plus(left_in[1], left_out[1]), y_swap())
    right_next = send_dp(plus(right_in[1], right_out[1]), x_swap())
    left = left_in[0].astype(F32) + left_out[0].astype(F32) + left_next.astype(F32)
    right = right_in[0].astype(F32) + right_out[0].astype(F32) + right_next.astype(F32)
    both = jnp.concatenate([left, right], axis=-1)
    low = both.astype(BF)
    total = both[0]
    for step in (1, 2, 3):
        total = total + send_dp(low[step], z_turn(step)).astype(F32)
    return total


def dot_f32(left, right, dims):
    return lax.dot_general(left, right, (dims, ((), ())), preferred_element_type=F32)


NN = ((1,), (0,))
NT = ((1,), (1,))
TN = ((0,), (0,))


def bias_of(table_ref, ids_ref, head):
    entry = jnp.broadcast_to(table_ref[pl.ds(head, 1), :], (PAD, 128))
    return [
        jnp.take_along_axis(
            entry, ids_ref[:, c * 128 : (c + 1) * 128], axis=1, mode="promise_in_bounds"
        )
        for c in range(KEYS // 128)
    ]


def joint_keys(own_ref, other_ref, seq):
    rows = pl.ds(seq * PAD, PAD)
    gap = jnp.zeros((HALF_KEYS - PAD, PAIR), BF)
    return jnp.concatenate([own_ref[rows, :], gap, other_ref[rows, :], gap], axis=0)


def key_mask(counts_ref, seq):
    lane = lax.broadcasted_iota(jnp.int32, (1, KEYS), 1)
    own, other = counts_ref[seq], counts_ref[2 + seq]
    return jnp.logical_or(
        lane < own, jnp.logical_and(lane >= HALF_KEYS, lane < HALF_KEYS + other)
    )


def half_only(values, part):
    lane = lax.broadcasted_iota(jnp.int32, values.shape, 1)
    keep = lane < HD if part == 0 else lane >= HD
    return jnp.where(keep, values, jnp.zeros((), values.dtype))


def attend_body(counts, ids, table, query, key_own, key_other, value_own, value_other, out, logs):
    pair = pl.program_id(0)
    keys = [joint_keys(key_own, key_other, seq) for seq in range(2)]
    values = [joint_keys(value_own, value_other, seq) for seq in range(2)]
    masks = [key_mask(counts, seq) for seq in range(2)]
    lane = lax.broadcasted_iota(jnp.int32, (PAD, 128), 1)
    done = [None, None]
    for part in range(2):
        head = 2 * pair + part
        bias = jnp.concatenate(bias_of(table, ids, head), axis=1)
        for seq in range(2):
            rows = pl.ds(seq * PAD, PAD)
            scores = dot_f32(half_only(query[rows, :], part), keys[seq], NT) * 0.125 + bias
            scores = jnp.where(masks[seq], scores, -1e30)
            top = jnp.max(scores, axis=1, keepdims=True)
            powers = jnp.exp(scores - top)
            total = jnp.sum(powers, axis=1, keepdims=True)
            probs = (powers * (1.0 / total)).astype(BF)
            got = dot_f32(probs, values[seq], NN)
            done[seq] = got if part == 0 else jnp.where(lane < HD, done[seq], got)
            logs[rows, :] = jnp.where(lane == head, top + jnp.log(total), logs[rows, :])
    for seq in range(2):
        out[pl.ds(seq * PAD, PAD), :] = done[seq]


def fixed(shape):
    return pl.BlockSpec(shape, lambda i: (0,) * len(shape))


def by_pair():
    return pl.BlockSpec((2 * PAD, PAIR), lambda i: (0, i))


def attend(counts, ids, table, query, key_own, key_other, value_own, value_other):
    return pl.pallas_call(
        attend_body,
        grid=(H // 2,),
        out_shape=(
            jax.ShapeDtypeStruct((2 * PAD, D), F32),
            jax.ShapeDtypeStruct((2 * PAD, 128), F32),
        ),
        in_specs=[pl.BlockSpec(memory_space=pltpu.SMEM), fixed((PAD, KEYS)), fixed((16, 128))]
        + [by_pair()] * 5,
        out_specs=(by_pair(), fixed((2 * PAD, 128))),
        name="attend",
    )(counts, ids, table, query, key_own, key_other, value_own, value_other)


def attend_back_body(
    counts, ids, table, logs, query, key_own, key_other, value_own, value_other, grad,
    grad_query, grad_key_own, grad_value_own, grad_key_other, grad_value_other, terms,
):
    pair = pl.program_id(0)
    keys = [joint_keys(key_own, key_other, seq) for seq in range(2)]
    values = [joint_keys(value_own, value_other, seq) for seq in range(2)]
    masks = [key_mask(counts, seq) for seq in range(2)]
    lane = lax.broadcasted_iota(jnp.int32, (PAD, 128), 1)
    to_query, to_key, to_value = [0.0, 0.0], [0.0, 0.0], [0.0, 0.0]
    for part in range(2):
        head = 2 * pair + part
        bias = jnp.concatenate(bias_of(table, ids, head), axis=1)
        both = 0.0
        for seq in range(2):
            rows = pl.ds(seq * PAD, PAD)
            asked = half_only(query[rows, :], part)
            into = half_only(grad[rows, :], part)
            scores = dot_f32(asked, keys[seq], NT) * 0.125 + bias
            scores = jnp.where(masks[seq], scores, -1e30)
            log = jnp.sum(jnp.where(lane == head, logs[rows, :], 0.0), axis=1, keepdims=True)
            probs = jnp.exp(scores - log)
            grad_probs = dot_f32(into, values[seq], NT)
            mean = jnp.sum(probs * grad_probs, axis=1, keepdims=True)
            grad_scores = (probs * (grad_probs - mean)).astype(BF)
            both = both + grad_scores.astype(F32)
            to_value[seq] = to_value[seq] + dot_f32(probs.astype(BF), into, TN)
            to_query[seq] = to_query[seq] + dot_f32(grad_scores, half_only(keys[seq], part), NN)
            to_key[seq] = to_key[seq] + dot_f32(grad_scores, asked, TN)
        for c in range(KEYS // 128):
            terms[c, pl.ds(head, PAD, stride=16), :] = both[:, c * 128 : (c + 1) * 128]
    for seq in range(2):
        rows = pl.ds(seq * PAD, PAD)
        grad_query[rows, :] = (to_query[seq] * 0.125).astype(BF)
        grad_key_own[rows, :] = to_key[seq][:PAD] * 0.125
        grad_key_other[rows, :] = (to_key[seq][HALF_KEYS : HALF_KEYS + PAD] * 0.125).astype(BF)
        grad_value_own[rows, :] = to_value[seq][:PAD]
        grad_value_other[rows, :] = to_value[seq][HALF_KEYS : HALF_KEYS + PAD].astype(BF)


def attend_back(counts, ids, table, logs, query, keys, values, grad):
    def rows_of(kind):
        return jax.ShapeDtypeStruct((2 * PAD, D), kind)

    return pl.pallas_call(
        attend_back_body,
        grid=(H // 2,),
        out_shape=(
            rows_of(BF),
            rows_of(F32),
            rows_of(F32),
            rows_of(BF),
            rows_of(BF),
            jax.ShapeDtypeStruct((KEYS // 128, PAD * 16, 128), F32),
        ),
        in_specs=[
            pl.BlockSpec(memory_space=pltpu.SMEM),
            fixed((PAD, KEYS)),
            fixed((16, 128)),
            fixed((2 * PAD, 128)),
        ]
        + [by_pair()] * 6,
        out_specs=(by_pair(),) * 5 + (fixed((KEYS // 128, PAD * 16, 128)),),
        name="attend_back",
    )(counts, ids, table, logs, query, *keys, *values, grad)


GROUP = 4


def table_body(ids, terms, out):
    bucket = lax.broadcasted_iota(jnp.int32, (NB + 1, KEYS), 0)

    def step(index, totals):
        fresh = []
        for lane_group in range(GROUP):
            row = index * GROUP + lane_group
            hot = jnp.where(ids[pl.ds(row, 1), :] == bucket, 1.0, 0.0).astype(BF)
            start = pl.multiple_of(row * 16, 16)
            term = jnp.concatenate(
                [terms[c, pl.ds(start, 16), :] for c in range(KEYS // 128)], axis=1
            )
            high = term.astype(BF)
            low = (term - high.astype(F32)).astype(BF)
            both = jnp.concatenate([high, low], axis=0)
            fresh.append(totals[lane_group] + dot_f32(hot, both, NT))
        return tuple(fresh)

    zero = jnp.zeros((NB + 1, 32), F32)
    totals = lax.fori_loop(0, P_SIZE // GROUP, step, (zero,) * GROUP)
    total = totals[0] + totals[1] + totals[2] + totals[3]
    out[...] = total


def table_grad(ids, terms):
    whole = pl.BlockSpec(memory_space=pltpu.VMEM)
    both = pl.pallas_call(
        table_body,
        out_shape=jax.ShapeDtypeStruct((NB + 1, 32), F32),
        in_specs=[whole, whole],
        out_specs=whole,
        name="table_grad",
    )(ids, terms)
    return both[:NB, :H] + both[:NB, 16 : 16 + H]


CUT = PHASE_ROWS - 4 * D


def spread_body(first, second, out, held):
    for half, table in enumerate((first, second)):
        start = 4 * D if half == 0 else 0
        for c in range(D // 128):
            lanes = pl.ds(c * 128, 128)
            held[...] = table[pl.ds(start, CUT), lanes].astype(F32)
            for part in range(4):
                out[pl.ds(half * CUT // 4, CUT // 4), pl.ds(part * D + c * 128, 128)] = held[
                    pl.ds(part, CUT // 4, stride=4), :
                ].astype(BF)


def spread(first, second):
    whole = pl.BlockSpec(memory_space=pltpu.VMEM)
    return pl.pallas_call(
        spread_body,
        out_shape=jax.ShapeDtypeStruct((D, FF), BF),
        in_specs=[whole, whole],
        out_specs=whole,
        scratch_shapes=[pltpu.VMEM((CUT, 128), F32)],
        name="spread",
    )(first, second)


def inner_grad_body(share, left, right, out, turned, held):
    chunk = pl.program_id(0)

    @pl.when(chunk == 0)
    def _():
        gap = jnp.zeros((KEYS - 2 * PAD, D), BF)
        turned[...] = jnp.concatenate([left[...], gap], axis=0).T

    gap = jnp.zeros((KEYS - 2 * PAD, 256), BF)
    for part in range(4):
        start = pl.multiple_of(part * D + chunk * 256, 256)
        block = jnp.concatenate([right[:, pl.ds(start, 256)], gap], axis=0)
        value = dot_f32(turned[...], block, NN) * share
        for c in range(2):
            held[c, pl.ds(part, D, stride=4), :] = value[:, c * 128 : (c + 1) * 128]
    out[...] = jnp.concatenate([held[0], held[1]], axis=1).astype(BF)


def inner_grad(left, right, share):
    return pl.pallas_call(
        functools.partial(inner_grad_body, share),
        grid=(D // 256,),
        out_shape=jax.ShapeDtypeStruct((FF, D), BF),
        in_specs=[fixed((2 * PAD, D)), fixed((2 * PAD, FF))],
        out_specs=pl.BlockSpec((FF, 256), lambda i: (0, i)),
        scratch_shapes=[pltpu.VMEM((D, KEYS), BF), pltpu.VMEM((2, FF, 128), F32)],
        name="inner_grad",
    )(left, right)


def from_partner(block, axis, bit):
    count = lax.axis_size(axis)
    route = []
    for low in range(count):
        high = low | 1 << bit
        if high != low and high < count:
            route += [(low, high), (high, low)]
    return lax.ppermute(block, axis, route)


def layer_norm(values, gain, shift):
    center = values - jnp.mean(values, axis=-1, keepdims=True)
    spread = jnp.mean(center * center, axis=-1, keepdims=True)
    return center * lax.rsqrt(spread + 1e-05) * gain + shift


def norm_back(values, gain, shift, grad_after):
    _, pullback = jax.vjp(layer_norm, values, gain, shift)
    return pullback(grad_after)


def matmul(left, right):
    return jnp.dot(left, right, preferred_element_type=jnp.float32)


def matmul_tn(left, right):
    return lax.dot_general(
        left, right, (((0,), (0,)), ((), ())), preferred_element_type=jnp.float32
    )


def matmul_nt(left, right):
    return lax.dot_general(
        left, right, (((1,), (1,)), ((), ())), preferred_element_type=jnp.float32
    )


def exact_gelu(values):
    return jax.nn.gelu(values, approximate=False)


def unpack(flat):
    pairs = [(D, D), (D, D), (D, D), (D, D), (D, FF), (FF, D), (10, D), (3, FF), (NB + 1, H)]
    pieces = []
    offset = 0
    for dims_pair in pairs:
        extent = dims_pair[0] * dims_pair[1]
        pieces.append(flat[offset : offset + extent].reshape(dims_pair))
        offset += extent
    return pieces


def unpack_tables(first, second, vec):
    square = [first[i * D : (i + 1) * D] for i in range(4)]
    return square + [
        spread(first, second),
        second[CUT:],
        vec[:10],
        vec[10:22].reshape(3, FF),
        vec[22].reshape(NB + 1, H),
    ]


def widen(values):
    return jnp.pad(values, ((0, 0), (0, PAD - P_SIZE), (0, 0))).reshape(2 * PAD, D)


def narrow(values):
    return values.reshape(1, 2, PAD, D)[:, :, :P_SIZE]


def on_device(rows, cotangent, master, first_moment, second_moment, average, lengths, buckets):
    side = lax.axis_index("mod")
    place = lax.axis_index("dp")
    fast = lax.axis_size("dp") == DP
    own_copy = master.astype(jnp.bfloat16)
    if fast:
        spot = coords()
        first, second = pack_shard(own_copy, side, place)
        is_last = jnp.logical_and(side == 1, place == DP - 1)
        vec = jnp.where(is_last, own_copy[-EDGE:], jnp.zeros((), BF))
        vec = jnp.pad(vec, (0, D)).reshape(24, D)
        vec, first = lax.optimization_barrier((vec, first))
        weights = unpack_tables(
            assemble(0, spot, gather_phase(first)),
            assemble(1, spot, gather_phase(second)),
            sum_all_small(vec),
        )
    else:
        weights = unpack(lax.all_gather(own_copy, ("mod", "dp"), axis=0, tiled=True))
    w_query, w_key, w_value, w_out, w_inner, w_outer, vec_model, vec_inner, head_table = weights
    model_vec = vec_model.astype(jnp.float32)
    inner_vec = vec_inner.astype(jnp.float32)
    head_vals = head_table.astype(jnp.float32)
    scale_row = jnp.repeat(head_vals[NB], HD)
    table = jnp.pad(head_vals.T, ((0, 16 - H), (0, 128 - NB - 1)))
    full = jnp.full_like(lengths, P_SIZE)
    own_count = jnp.where(side == 0, full, lengths)
    other_count = jnp.where(side == 0, lengths, full)
    counts = jnp.concatenate([own_count, other_count]).astype(jnp.int32)
    slots = jnp.arange(PAD, dtype=jnp.int32)
    own_valid = (slots[None, :] < own_count[:, None]).astype(F32).reshape(2 * PAD, 1)
    near = lax.dynamic_slice(buckets, (side * P_SIZE, side * P_SIZE), (P_SIZE, P_SIZE))
    far = lax.dynamic_slice(buckets, (side * P_SIZE, (1 - side) * P_SIZE), (P_SIZE, P_SIZE))
    room = ((0, PAD - P_SIZE), (0, HALF_KEYS - P_SIZE))
    ids = jnp.concatenate([jnp.pad(near, room), jnp.pad(far, room)], axis=1)

    inputs = widen(rows[0]).astype(F32)
    normed = layer_norm(inputs, model_vec[0], model_vec[1])
    normed_low = normed.astype(BF)
    keys_own = matmul(normed_low, w_key).astype(BF)
    values_own = (matmul(normed_low, w_value) + model_vec[3]).astype(BF)
    keys_other, values_other = from_partner((keys_own, values_own), "mod", 0)
    query = (matmul(normed_low, w_query) + model_vec[2]).astype(BF)
    keys_both, values_both = (keys_own, keys_other), (values_own, values_other)
    attended, logs = attend(counts, ids, table, query, *keys_both, *values_both)

    scaled = attended * scale_row
    mixed = layer_norm(scaled, model_vec[4], model_vec[5])
    mixed_low = mixed.astype(BF)
    middle = inputs + (matmul(mixed_low, w_out) + model_vec[6])
    normed_two = layer_norm(middle, model_vec[7], model_vec[8])
    normed_two_low = normed_two.astype(BF)
    inner = matmul(normed_two_low, w_inner) + inner_vec[0]
    activated = exact_gelu(inner)
    inner_normed = layer_norm(activated, inner_vec[1], inner_vec[2])
    inner_low = inner_normed.astype(BF)
    result = middle + (matmul(inner_low, w_outer) + model_vec[9])
    result_rows = narrow(result.astype(BF))

    tokens_all = 2 * rows.shape[1] * P_SIZE * lax.axis_size("dp")
    share = 1.0 / tokens_all

    def weight_grad(left, right):
        value = matmul_tn(left, right) * share
        return value.astype(BF) if fast else value

    grad_out = widen(cotangent[0]).astype(F32) * own_valid
    grad_branch = grad_out.astype(BF)
    grad_w_outer = weight_grad(inner_low, grad_branch)
    grad_b_outer = jnp.sum(grad_branch.astype(F32), axis=0)
    grad_inner_normed = matmul_nt(grad_branch, w_outer)
    grad_activated, grad_gain_ff, grad_shift_ff = norm_back(
        activated, inner_vec[1], inner_vec[2], grad_inner_normed
    )
    _, gelu_pull = jax.vjp(exact_gelu, inner)
    grad_inner_low = gelu_pull(grad_activated)[0].astype(BF)
    if fast:
        grad_w_inner = inner_grad(normed_two_low, grad_inner_low, share)
    else:
        grad_w_inner = weight_grad(normed_two_low, grad_inner_low).reshape(FF, D)
    grad_b_inner = jnp.sum(grad_inner_low.astype(F32), axis=0)
    grad_normed_two = matmul_nt(grad_inner_low, w_inner)
    grad_mid_part, grad_gain_two, grad_shift_two = norm_back(
        middle, model_vec[7], model_vec[8], grad_normed_two
    )
    grad_middle = grad_out + grad_mid_part
    grad_attn_low = grad_middle.astype(BF)
    grad_w_out = weight_grad(mixed_low, grad_attn_low)
    grad_b_out = jnp.sum(grad_attn_low.astype(F32), axis=0)
    grad_mixed = matmul_nt(grad_attn_low, w_out)
    grad_scaled, grad_gain_attn, grad_shift_attn = norm_back(
        scaled, model_vec[4], model_vec[5], grad_mixed
    )
    grad_head_scale = jnp.sum(jnp.sum(grad_scaled * attended, axis=0).reshape(H, HD), axis=1)
    grad_attended = (grad_scaled * scale_row).astype(BF)
    if fast:
        late = scatter(1, spot, [None] * 4 + [grad_w_inner, grad_w_outer])
        late, grad_attended = lax.optimization_barrier((late, grad_attended))
        late = (late[0], send_mod(late[1]))
    grad_query, key_kept, value_kept, key_sent, value_sent, terms = attend_back(
        counts, ids, table, logs, query, keys_both, values_both, grad_attended
    )
    back_keys, back_values = from_partner((key_sent, value_sent), "mod", 0)
    grad_key = (key_kept + back_keys.astype(F32)).astype(BF)
    grad_value = (value_kept + back_values.astype(F32)).astype(BF)
    grad_table = table_grad(ids, terms)
    grad_w_query = weight_grad(normed_low, grad_query)
    grad_w_key = weight_grad(normed_low, grad_key)
    grad_w_value = weight_grad(normed_low, grad_value)
    grad_b_query = jnp.sum(grad_query.astype(F32), axis=0)
    grad_b_value = jnp.sum(grad_value.astype(F32), axis=0)
    grad_normed = (
        matmul_nt(grad_query, w_query) + matmul_nt(grad_key, w_key) + matmul_nt(grad_value, w_value)
    )
    grad_in_part, grad_gain_one, grad_shift_one = norm_back(
        inputs, model_vec[0], model_vec[1], grad_normed
    )
    grad_rows = narrow(grad_middle + grad_in_part)
    grad_model_vec = jnp.stack(
        [
            grad_gain_one,
            grad_shift_one,
            grad_b_query,
            grad_b_value,
            grad_gain_attn,
            grad_shift_attn,
            grad_b_out,
            grad_gain_two,
            grad_shift_two,
            grad_b_outer,
        ]
    )
    grad_inner_vec = jnp.stack([grad_b_inner, grad_gain_ff, grad_shift_ff])
    grad_heads = jnp.concatenate([grad_table, grad_head_scale[None, :]], axis=0)
    vec_grad = (
        jnp.concatenate(
            [grad_model_vec, grad_inner_vec.reshape(12, D), grad_heads.reshape(1, D)], axis=0
        )
        * share
    )
    matrices = [grad_w_query, grad_w_key, grad_w_value, grad_w_out, grad_w_inner, grad_w_outer]
    if fast:
        second = reduce_phase(*late)
        kept, lent = scatter(0, spot, matrices)
        first = reduce_phase(kept, send_mod(lent))
        vec_grad = sum_all_small(jnp.pad(vec_grad, ((0, 1), (0, 0))))
        square = jnp.sum(first * first) + jnp.sum(second * second)
        square = square + jnp.where(is_last, jnp.sum(vec_grad * vec_grad), 0.0)
        square_sum = sum_all_small(jnp.full((8, 128), square))[0, 0]
        grad_shard = unpack_shard(first, second, vec_grad, side, place)
    else:
        local_grad = jnp.concatenate([part.reshape(-1) for part in matrices + [vec_grad]])
        half_size = local_grad.shape[0] // 2
        own_half = lax.dynamic_slice_in_dim(local_grad, side * half_size, half_size)
        other_half = lax.dynamic_slice_in_dim(local_grad, (1 - side) * half_size, half_size)
        partner_half = from_partner(other_half.astype(BF), "mod", 0).astype(F32)
        grad_shard = lax.psum_scatter(own_half + partner_half, "dp", scatter_dimension=0, tiled=True)
        square_sum = lax.psum(jnp.sum(grad_shard * grad_shard), ("mod", "dp"))
    grad_norm = jnp.sqrt(square_sum)
    clip_scale = jnp.minimum(1.0, 0.25 / (grad_norm + 1e-06))
    clipped = grad_shard * clip_scale
    new_first = 0.5 * first_moment + 0.5 * clipped
    new_second = 0.6 * second_moment + 0.4 * clipped * clipped
    direction = new_first / (1.0 - 0.5**STEP) / (jnp.sqrt(new_second / (1.0 - 0.6**STEP)) + 1e-08)
    new_master = master - 0.04 * (direction + 0.01 * master)
    new_average = 0.5 * average + 0.5 * new_master
    return (
        result_rows,
        grad_rows,
        grad_norm,
        new_master,
        new_first,
        new_second,
        new_average,
        new_master.astype(jnp.bfloat16),
    )


def solution(mesh):
    placed = (
        P("mod", "dp", None, None),
        P("mod", "dp", None, None),
        P(("mod", "dp")),
        P(("mod", "dp")),
        P(("mod", "dp")),
        P(("mod", "dp")),
        P("dp"),
        P(),
    )
    return jax.shard_map(
        on_device,
        mesh=mesh,
        in_specs=placed,
        out_specs=(
            P("mod", "dp", None, None),
            P("mod", "dp", None, None),
            P(),
            P(("mod", "dp")),
            P(("mod", "dp")),
            P(("mod", "dp")),
            P(("mod", "dp")),
            P(("mod", "dp")),
        ),
        check_vma=False,
    )
```

```python
import functools
import jax
import jax.numpy as jnp
from jax import lax
from jax.experimental import pallas as pl
from jax.experimental.pallas import tpu as pltpu
from jax.sharding import PartitionSpec as P

D = 768
H = 12
HD = 64
FF = 3072
NB = 63
P_SIZE = 196
STEP = 5


HALF = D // 2
BLOCK = 144
PHASE_ROWS = 32 * BLOCK
BF = jnp.bfloat16
F32 = jnp.float32
DP = 16
EDGE = 17664
PAD = 208
KEYS = 512
HALF_KEYS = KEYS // 2
PAIR = 2 * HD


def x_swap():
    return [(i, i ^ 1) for i in range(DP)]


def y_swap():
    return [(i, i ^ 2) for i in range(DP)]


def z_turn(step):
    return [(i, (i // 4 + step) % 4 * 4 + i % 4) for i in range(DP)]


def send_dp(block, route):
    return lax.ppermute(block, "dp", route)


def send_mod(block):
    return lax.ppermute(block, "mod", [(0, 1), (1, 0)])


def pack_shard(own, side, place):
    lead = 8832 * side + 552 * place
    count = BLOCK * D
    lent = lax.dynamic_slice(own, (count - lead,), (count,))
    given = send_mod(lent)
    nxt = [(i, i + 1) for i in range(2 * DP - 1)]
    edge = lax.ppermute(own[own.shape[0] - EDGE :], ("mod", "dp"), nxt)
    kept = lax.dynamic_slice(jnp.concatenate([edge, own[:count]]), (EDGE - lead,), (count,))
    kept = kept.reshape(BLOCK, D)
    given = given.reshape(BLOCK, D)
    return jnp.where(side == 0, kept, given), jnp.where(side == 0, given, kept)


def unpack_shard(first, second, vec, side, place):
    lead = 8832 * side + 552 * place
    even = jnp.where(side == 0, first, second).reshape(-1)
    lent = jnp.where(side == 0, second, first)
    odd = send_mod(lent).reshape(-1)
    back = [(i + 1, i) for i in range(2 * DP - 1)]
    edge = lax.ppermute(even[:EDGE], ("mod", "dp"), back)
    is_last = jnp.logical_and(side == 1, place == DP - 1)
    edge = jnp.where(is_last, vec.reshape(-1)[:EDGE], edge)
    return lax.dynamic_slice(jnp.concatenate([even, odd, edge]), (lead,), (221736,))


def sum_z_small(part):
    part = part + send_dp(part, z_turn(2))
    return part + send_dp(part, [(i, i ^ 4) for i in range(DP)])


def sum_rest_small(part):
    part = part + send_dp(part, x_swap())
    part = part + send_dp(part, y_swap())
    return part + send_mod(part)


def xy_swap():
    return [(i, i ^ 3) for i in range(DP)]


def sum_scalar(value, side, place):
    slots = lax.broadcasted_iota(jnp.int32, (8, 128), 0) * 128
    slots = slots + lax.broadcasted_iota(jnp.int32, (8, 128), 1)
    own = jnp.where(slots == side * DP + place, value, 0.0)
    for routes in ([z_turn(1), z_turn(2), z_turn(3)], [x_swap(), y_swap(), xy_swap()]):
        got = [send_dp(own, route) for route in routes]
        own = own + got[0] + got[1] + got[2]
    return jnp.sum(own + send_mod(own))


def gather_z(block):
    return jnp.stack([block] + [send_dp(block, z_turn(step)) for step in (1, 2, 3)])


def gather_phase(stack):
    left, right = stack[:, :, :HALF], stack[:, :, HALF:]
    left_x = send_dp(left, x_swap())
    right_y = send_dp(right, y_swap())
    left_y = send_dp(left, y_swap())
    right_x = send_dp(right, x_swap())
    left_xy = send_dp(left_x, y_swap())
    right_xy = send_dp(right_y, x_swap())
    mine = [left, left_x, left_y, left_xy, right, right_x, right_y, right_xy]
    return mine + [send_mod(piece) for piece in mine]


def coords():
    side = lax.axis_index("mod")
    place = lax.axis_index("dp")
    return jnp.stack([side, place // 4, place // 2 % 2, place % 2]).astype(jnp.int32)


def assemble_body(phase, spot, *refs):
    pieces, out, sem = refs[:16], refs[-2], refs[-1]
    side, z, y, x = spot[0], spot[1], spot[2], spot[3]
    copies = []
    for index in range(16):
        other, half, yr, xr = index // 8, index // 4 % 2, index // 2 % 2, index % 2
        owner = side ^ other
        parity = owner if phase == 0 else 1 - owner
        for turn in range(4):
            home = ((z - turn) & 3) * 4 + (y ^ yr) * 2 + (x ^ xr)
            copies.append(
                pltpu.make_async_copy(
                    pieces[index].at[turn],
                    out.at[home * 2 + parity, :, pl.ds(half * HALF, HALF)],
                    sem.at[index * 4 + turn],
                )
            )
    for copy in copies:
        copy.start()
    for copy in copies:
        copy.wait()


def assemble(phase, spot, pieces, after=()):
    return pl.pallas_call(
        functools.partial(assemble_body, phase),
        out_shape=jax.ShapeDtypeStruct((32, BLOCK, D), BF),
        in_specs=[pl.BlockSpec(memory_space=pltpu.SMEM)] + [pl.BlockSpec(memory_space=pl.ANY)] * (16 + len(after)),
        out_specs=pl.BlockSpec(memory_space=pltpu.VMEM),
        scratch_shapes=[pltpu.SemaphoreType.DMA((64,))],
        name="assemble",
    )(spot, *pieces, *after).reshape(PHASE_ROWS, D)


def scatter_body(phase, pieces, spot, *refs):
    sources, kept, lent, sem = refs[:-3], refs[-3], refs[-2], refs[-1]
    side, z, y, x = spot[0], spot[1], spot[2], spot[3]
    copies = []
    for block in range(32):
        home, parity = block // 2, block % 2
        owner = parity if phase == 0 else 1 - parity
        turn = (home // 4 - z) & 3
        yr = (home // 2 % 2) ^ y
        xr = (home % 2) ^ x
        for index, source_row, block_row, count in pieces[block]:
            for half in range(2):
                stay, leave = [
                    pltpu.make_async_copy(
                        sources[index].at[pl.ds(source_row, count), pl.ds(half * HALF, HALF)],
                        target.at[half, yr, xr, turn, pl.ds(block_row, count), :],
                        sem.at[len(copies)],
                    )
                    for target in (kept, lent)
                ]
                pl.when(side == owner)(stay.start)
                pl.when(side != owner)(leave.start)
                copies.append(stay)
    for copy in copies:
        copy.wait()


def scatter(phase, spot, tables, after=()):
    starts = [0]
    for rows in (D, D, D, D, FF, FF):
        starts.append(starts[-1] + rows)
    pieces = []
    for block in range(32):
        low = phase * PHASE_ROWS + block * BLOCK
        parts = []
        for index in range(len(tables)):
            first, last = max(low, starts[index]), min(low + BLOCK, starts[index + 1])
            if first < last:
                parts.append((index, first - starts[index], first - low, last - first))
        pieces.append(parts)
    used = sorted({part[0] for parts in pieces for part in parts})
    pieces = [[(used.index(part[0]),) + part[1:] for part in parts] for parts in pieces]
    count = 2 * sum(len(parts) for parts in pieces)
    return pl.pallas_call(
        functools.partial(scatter_body, phase, pieces),
        out_shape=(jax.ShapeDtypeStruct((2, 2, 2, 4, BLOCK, HALF), BF),) * 2,
        in_specs=[pl.BlockSpec(memory_space=pltpu.SMEM)]
        + [pl.BlockSpec(memory_space=pltpu.VMEM)] * len(used)
        + [pl.BlockSpec(memory_space=pl.ANY)] * len(after),
        out_specs=(pl.BlockSpec(memory_space=pl.ANY),) * 2,
        scratch_shapes=[pltpu.SemaphoreType.DMA((count,))],
        name="scatter",
    )(spot, *[tables[index] for index in used], *after)


def plus(left, right):
    return (left.astype(F32) + right.astype(F32)).astype(BF)


def outs_body(*refs):
    left_mine, left_theirs, right_mine, right_theirs, left, right = refs[:4] + refs[-2:]
    index = pl.program_id(0)

    @pl.when(index < 2)
    def _():
        left[0] = plus(left_mine[0, 0, 0], left_theirs[0, 0, 0])

    @pl.when(index >= 2)
    def _():
        right[0] = plus(right_mine[0, 0, 0], right_theirs[0, 0, 0])


def reduce_outs(mine, theirs):
    block = (1, 1, 1, 4, BLOCK, HALF)
    left = pl.BlockSpec(block, lambda i: (0, jnp.minimum(i, 1), 1, 0, 0, 0))
    right = pl.BlockSpec(block, lambda i: (1, 1, jnp.maximum(i - 2, 0), 0, 0, 0))
    return pl.pallas_call(
        outs_body,
        grid=(4,),
        out_shape=(jax.ShapeDtypeStruct((2, 4, BLOCK, HALF), BF),) * 2,
        in_specs=[left, left, right, right],
        out_specs=(
            pl.BlockSpec((1, 4, BLOCK, HALF), lambda i: (jnp.minimum(i, 1), 0, 0, 0)),
            pl.BlockSpec((1, 4, BLOCK, HALF), lambda i: (jnp.maximum(i - 2, 0), 0, 0, 0)),
        ),
        name="reduce_outs",
    )(mine, theirs, mine, theirs)


def reduce_sends(outs):
    return send_dp(outs[0], x_swap()), send_dp(outs[1], y_swap())


def reduce_ins(mine, theirs):
    return plus(mine[0, :, 0], theirs[0, :, 0]), plus(mine[1, 0], theirs[1, 0])


def reduce_phase(sent, ins):
    left_out, right_out = sent
    left_in, right_in = ins
    left_next = send_dp(plus(left_in[1], left_out[1]), y_swap())
    right_next = send_dp(plus(right_in[1], right_out[1]), x_swap())
    left = left_in[0].astype(F32) + left_out[0].astype(F32) + left_next.astype(F32)
    right = right_in[0].astype(F32) + right_out[0].astype(F32) + right_next.astype(F32)
    both = jnp.concatenate([left, right], axis=-1)
    low = both.astype(BF)
    total = both[0]
    for step in (1, 2, 3):
        total = total + send_dp(low[step], z_turn(step)).astype(F32)
    return total


def dot_f32(left, right, dims):
    return lax.dot_general(left, right, (dims, ((), ())), preferred_element_type=F32)


NN = ((1,), (0,))
NT = ((1,), (1,))
TN = ((0,), (0,))


def bias_of(table_ref, ids_ref, head):
    entry = jnp.broadcast_to(table_ref[pl.ds(head, 1), :], (PAD, 128))
    return [
        jnp.take_along_axis(
            entry, ids_ref[:, c * 128 : (c + 1) * 128], axis=1, mode="promise_in_bounds"
        )
        for c in range(KEYS // 128)
    ]


def joint_keys(own_ref, other_ref, seq):
    rows = pl.ds(seq * PAD, PAD)
    gap = jnp.zeros((HALF_KEYS - PAD, PAIR), BF)
    return jnp.concatenate([own_ref[rows, :], gap, other_ref[rows, :], gap], axis=0)


def key_mask(counts_ref, seq):
    lane = lax.broadcasted_iota(jnp.int32, (1, KEYS), 1)
    own, other = counts_ref[seq], counts_ref[2 + seq]
    return jnp.logical_or(
        lane < own, jnp.logical_and(lane >= HALF_KEYS, lane < HALF_KEYS + other)
    )


def half_only(values, part):
    lane = lax.broadcasted_iota(jnp.int32, values.shape, 1)
    keep = lane < HD if part == 0 else lane >= HD
    return jnp.where(keep, values, jnp.zeros((), values.dtype))


def attend_body(counts, ids, table, query, key_own, key_other, value_own, value_other, out, logs):
    pair = pl.program_id(0)
    keys = [joint_keys(key_own, key_other, seq) for seq in range(2)]
    values = [joint_keys(value_own, value_other, seq) for seq in range(2)]
    masks = [key_mask(counts, seq) for seq in range(2)]
    lane = lax.broadcasted_iota(jnp.int32, (PAD, 128), 1)
    done = [None, None]
    for part in range(2):
        head = 2 * pair + part
        bias = jnp.concatenate(bias_of(table, ids, head), axis=1)
        for seq in range(2):
            rows = pl.ds(seq * PAD, PAD)
            scores = dot_f32(half_only(query[rows, :], part), keys[seq], NT) * 0.125 + bias
            scores = jnp.where(masks[seq], scores, -1e30)
            top = jnp.max(scores, axis=1, keepdims=True)
            powers = jnp.exp(scores - top)
            total = jnp.sum(powers, axis=1, keepdims=True)
            probs = (powers * (1.0 / total)).astype(BF)
            got = dot_f32(probs, values[seq], NN)
            done[seq] = got if part == 0 else jnp.where(lane < HD, done[seq], got)
            logs[rows, :] = jnp.where(lane == head, top + jnp.log(total), logs[rows, :])
    for seq in range(2):
        out[pl.ds(seq * PAD, PAD), :] = done[seq]


def fixed(shape):
    return pl.BlockSpec(shape, lambda i: (0,) * len(shape))


def by_pair():
    return pl.BlockSpec((2 * PAD, PAIR), lambda i: (0, i))


def attend(counts, ids, table, query, key_own, key_other, value_own, value_other):
    return pl.pallas_call(
        attend_body,
        grid=(H // 2,),
        out_shape=(
            jax.ShapeDtypeStruct((2 * PAD, D), F32),
            jax.ShapeDtypeStruct((2 * PAD, 128), F32),
        ),
        in_specs=[pl.BlockSpec(memory_space=pltpu.SMEM), fixed((PAD, KEYS)), fixed((16, 128))]
        + [by_pair()] * 5,
        out_specs=(by_pair(), fixed((2 * PAD, 128))),
        name="attend",
    )(counts, ids, table, query, key_own, key_other, value_own, value_other)


def attend_back_body(
    base, counts, ids, table, logs, query, key_own, key_other, value_own, value_other, grad, *refs
):
    grad_query, grad_key_own, grad_value_own, grad_key_other, grad_value_other, terms = refs[-6:]
    pair = pl.program_id(0) + base
    keys = [joint_keys(key_own, key_other, seq) for seq in range(2)]
    values = [joint_keys(value_own, value_other, seq) for seq in range(2)]
    masks = [key_mask(counts, seq) for seq in range(2)]
    lane = lax.broadcasted_iota(jnp.int32, (PAD, 128), 1)
    to_query, to_key, to_value = [0.0, 0.0], [0.0, 0.0], [0.0, 0.0]
    for part in range(2):
        head = 2 * pair + part
        bias = jnp.concatenate(bias_of(table, ids, head), axis=1)
        both = 0.0
        for seq in range(2):
            rows = pl.ds(seq * PAD, PAD)
            asked = half_only(query[rows, :], part)
            into = half_only(grad[rows, :], part)
            scores = dot_f32(asked, keys[seq], NT) * 0.125 + bias
            scores = jnp.where(masks[seq], scores, -1e30)
            log = jnp.sum(jnp.where(lane == head, logs[rows, :], 0.0), axis=1, keepdims=True)
            probs = jnp.exp(scores - log)
            grad_probs = dot_f32(into, values[seq], NT)
            mean = jnp.sum(probs * grad_probs, axis=1, keepdims=True)
            grad_scores = (probs * (grad_probs - mean)).astype(BF)
            both = both + grad_scores.astype(F32)
            to_value[seq] = to_value[seq] + dot_f32(probs.astype(BF), into, TN)
            to_query[seq] = to_query[seq] + dot_f32(grad_scores, half_only(keys[seq], part), NN)
            to_key[seq] = to_key[seq] + dot_f32(grad_scores, asked, TN)
        for c in range(KEYS // 128):
            terms[c, pl.ds(head - 2 * base, PAD, stride=8), :] = both[:, c * 128 : (c + 1) * 128]
    for seq in range(2):
        rows = pl.ds(seq * PAD, PAD)
        grad_query[rows, :] = (to_query[seq] * 0.125).astype(BF)
        grad_key_own[rows, :] = to_key[seq][:PAD] * 0.125
        grad_key_other[rows, :] = (to_key[seq][HALF_KEYS : HALF_KEYS + PAD] * 0.125).astype(BF)
        grad_value_own[rows, :] = to_value[seq][:PAD]
        grad_value_other[rows, :] = to_value[seq][HALF_KEYS : HALF_KEYS + PAD].astype(BF)


def attend_back(base, counts, ids, table, logs, query, keys, values, grad, before=(), after=()):
    def rows_of(kind):
        return jax.ShapeDtypeStruct((2 * PAD, D), kind)

    columns = pl.BlockSpec((2 * PAD, PAIR), lambda i: (0, i + base))
    any_ref = pl.BlockSpec(memory_space=pl.ANY)
    return pl.pallas_call(
        functools.partial(attend_back_body, base),
        grid=(H // 4,),
        out_shape=(
            rows_of(BF),
            rows_of(F32),
            rows_of(F32),
            rows_of(BF),
            rows_of(BF),
            jax.ShapeDtypeStruct((KEYS // 128, PAD * 8, 128), F32),
        ),
        in_specs=[
            pl.BlockSpec(memory_space=pltpu.SMEM),
            fixed((PAD, KEYS)),
            fixed((16, 128)),
            fixed((2 * PAD, 128)),
        ]
        + [columns] * 6
        + [any_ref] * (len(before) + len(after)),
        out_specs=(columns,) * 5 + (fixed((KEYS // 128, PAD * 8, 128)),),
        input_output_aliases={10 + i: i for i in range(len(before))},
        name="attend_back",
    )(counts, ids, table, logs, query, *keys, *values, grad, *before, *after)


GROUP = 4


def table_body(ids, early, late, *refs):
    out = refs[-1]
    bucket = lax.broadcasted_iota(jnp.int32, (NB + 1, KEYS), 0)

    def step(index, totals):
        fresh = []
        for lane_group in range(GROUP):
            row = index * GROUP + lane_group
            hot = jnp.where(ids[pl.ds(row, 1), :] == bucket, 1.0, 0.0).astype(BF)
            span = pl.ds(pl.multiple_of(row * 8, 8), 8)
            term = jnp.concatenate(
                [
                    jnp.concatenate([terms[c, span, :] for c in range(KEYS // 128)], axis=1)
                    for terms in (early, late)
                ],
                axis=0,
            )
            high = term.astype(BF)
            low = (term - high.astype(F32)).astype(BF)
            both = jnp.concatenate([high, low], axis=0)
            fresh.append(totals[lane_group] + dot_f32(hot, both, NT))
        return tuple(fresh)

    zero = jnp.zeros((NB + 1, 32), F32)
    totals = lax.fori_loop(0, P_SIZE // GROUP, step, (zero,) * GROUP)
    total = totals[0] + totals[1] + totals[2] + totals[3]
    out[...] = total


def table_grad(ids, terms, after=()):
    whole = pl.BlockSpec(memory_space=pltpu.VMEM)
    both = pl.pallas_call(
        table_body,
        out_shape=jax.ShapeDtypeStruct((NB + 1, 32), F32),
        in_specs=[whole] * 3 + [pl.BlockSpec(memory_space=pl.ANY)] * len(after),
        out_specs=whole,
        name="table_grad",
    )(ids, *terms, *after)
    both = both[:NB, :16] + both[:NB, 16:]
    return jnp.concatenate([both[:, : H // 2], both[:, 8 : 8 + H // 2]], axis=1)


CUT = PHASE_ROWS - 4 * D


def spread_body(half, table, *refs):
    out, held = refs[-2], refs[-1]
    start = 4 * D if half == 0 else 0
    for c in range(D // 128):
        held[...] = table[pl.ds(start, CUT), pl.ds(c * 128, 128)].astype(F32)
        for part in range(4):
            out[:, pl.ds(part * D + c * 128, 128)] = held[
                pl.ds(part, CUT // 4, stride=4), :
            ].astype(BF)


def spread(half, table, before=None):
    whole = pl.BlockSpec(memory_space=pltpu.VMEM)
    extra = () if before is None else (before,)
    return pl.pallas_call(
        functools.partial(spread_body, half),
        grid=(1,),
        out_shape=jax.ShapeDtypeStruct((D, FF), BF),
        in_specs=[whole] + [pl.BlockSpec(memory_space=pl.ANY)] * len(extra),
        out_specs=pl.BlockSpec((CUT // 4, FF), lambda i: (half, 0)),
        scratch_shapes=[pltpu.VMEM((CUT, 128), F32)],
        input_output_aliases={1: 0} if extra else {},
        name="spread",
    )(table, *extra)


def inner_grad_body(share, left, right, out, turned, held):
    chunk = pl.program_id(0)

    @pl.when(chunk == 0)
    def _():
        gap = jnp.zeros((KEYS - 2 * PAD, D), BF)
        turned[...] = jnp.concatenate([left[...], gap], axis=0).T

    gap = jnp.zeros((KEYS - 2 * PAD, 256), BF)
    for part in range(4):
        start = pl.multiple_of(part * D + chunk * 256, 256)
        block = jnp.concatenate([right[:, pl.ds(start, 256)], gap], axis=0)
        value = dot_f32(turned[...], block, NN) * share
        for c in range(2):
            held[c, pl.ds(part, D, stride=4), :] = value[:, c * 128 : (c + 1) * 128]
    out[...] = jnp.concatenate([held[0], held[1]], axis=1).astype(BF)


def inner_grad(left, right, share):
    return pl.pallas_call(
        functools.partial(inner_grad_body, share),
        grid=(D // 256,),
        out_shape=jax.ShapeDtypeStruct((FF, D), BF),
        in_specs=[fixed((2 * PAD, D)), fixed((2 * PAD, FF))],
        out_specs=pl.BlockSpec((FF, 256), lambda i: (0, i)),
        scratch_shapes=[pltpu.VMEM((D, KEYS), BF), pltpu.VMEM((2, FF, 128), F32)],
        name="inner_grad",
    )(left, right)


def from_partner(block, axis, bit):
    count = lax.axis_size(axis)
    route = []
    for low in range(count):
        high = low | 1 << bit
        if high != low and high < count:
            route += [(low, high), (high, low)]
    return lax.ppermute(block, axis, route)


def layer_norm(values, gain, shift):
    center = values - jnp.mean(values, axis=-1, keepdims=True)
    spread = jnp.mean(center * center, axis=-1, keepdims=True)
    return center * lax.rsqrt(spread + 1e-05) * gain + shift


def norm_back(values, gain, shift, grad_after):
    _, pullback = jax.vjp(layer_norm, values, gain, shift)
    return pullback(grad_after)


def matmul(left, right):
    return jnp.dot(left, right, preferred_element_type=jnp.float32)


def matmul_tn(left, right):
    return lax.dot_general(
        left, right, (((0,), (0,)), ((), ())), preferred_element_type=jnp.float32
    )


def matmul_nt(left, right):
    return lax.dot_general(
        left, right, (((1,), (1,)), ((), ())), preferred_element_type=jnp.float32
    )


def exact_gelu(values):
    return jax.nn.gelu(values, approximate=False)


def unpack(flat):
    pairs = [(D, D), (D, D), (D, D), (D, D), (D, FF), (FF, D), (10, D), (3, FF), (NB + 1, H)]
    pieces = []
    offset = 0
    for dims_pair in pairs:
        extent = dims_pair[0] * dims_pair[1]
        pieces.append(flat[offset : offset + extent].reshape(dims_pair))
        offset += extent
    return pieces


def widen(values):
    return jnp.pad(values, ((0, 0), (0, PAD - P_SIZE), (0, 0))).reshape(2 * PAD, D)


def narrow(values):
    return values.reshape(1, 2, PAD, D)[:, :, :P_SIZE]


def on_device(rows, cotangent, master, first_moment, second_moment, average, lengths, buckets):
    side = lax.axis_index("mod")
    place = lax.axis_index("dp")
    fast = lax.axis_size("dp") == DP
    own_copy = master.astype(jnp.bfloat16)
    if fast:
        spot = coords()
        first, second = pack_shard(own_copy, side, place)
        is_last = jnp.logical_and(side == 1, place == DP - 1)
        vec = jnp.where(is_last, own_copy[-EDGE:], jnp.zeros((), BF))
        vec = jnp.pad(vec, (0, D)).reshape(24, D)
        vec, first = lax.optimization_barrier((sum_z_small(vec), first))
        second_stack = gather_z(second)
        first_table = assemble(0, spot, gather_phase(gather_z(first)), (second_stack,))
        second_pieces = gather_phase(second_stack)
        vec = sum_rest_small(vec)
        square = [first_table[i * D : (i + 1) * D] for i in range(4)]
        vec_model, vec_inner = vec[:10], vec[10:22].reshape(3, FF)
        head_table = vec[22].reshape(NB + 1, H)
    else:
        weights = unpack(lax.all_gather(own_copy, ("mod", "dp"), axis=0, tiled=True))
        square, (w_inner, w_outer, vec_model, vec_inner, head_table) = weights[:4], weights[4:]
    w_query, w_key, w_value, w_out = square
    model_vec = vec_model.astype(jnp.float32)
    inner_vec = vec_inner.astype(jnp.float32)
    head_vals = head_table.astype(jnp.float32)
    scale_row = jnp.repeat(head_vals[NB], HD)
    table = jnp.pad(head_vals.T, ((0, 16 - H), (0, 128 - NB - 1)))
    full = jnp.full_like(lengths, P_SIZE)
    own_count = jnp.where(side == 0, full, lengths)
    other_count = jnp.where(side == 0, lengths, full)
    counts = jnp.concatenate([own_count, other_count]).astype(jnp.int32)
    slots = jnp.arange(PAD, dtype=jnp.int32)
    own_valid = (slots[None, :] < own_count[:, None]).astype(F32).reshape(2 * PAD, 1)
    near = lax.dynamic_slice(buckets, (side * P_SIZE, side * P_SIZE), (P_SIZE, P_SIZE))
    far = lax.dynamic_slice(buckets, (side * P_SIZE, (1 - side) * P_SIZE), (P_SIZE, P_SIZE))
    room = ((0, PAD - P_SIZE), (0, HALF_KEYS - P_SIZE))
    ids = jnp.concatenate([jnp.pad(near, room), jnp.pad(far, room)], axis=1)

    inputs = widen(rows[0]).astype(F32)
    normed = layer_norm(inputs, model_vec[0], model_vec[1])
    normed_low = normed.astype(BF)
    keys_own = matmul(normed_low, w_key).astype(BF)
    values_own = (matmul(normed_low, w_value) + model_vec[3]).astype(BF)
    keys_other, values_other = from_partner((keys_own, values_own), "mod", 0)
    query = (matmul(normed_low, w_query) + model_vec[2]).astype(BF)
    keys_both, values_both = (keys_own, keys_other), (values_own, values_other)
    attended, logs = attend(counts, ids, table, query, *keys_both, *values_both)

    if fast:
        w_inner = spread(0, first_table)
        second_table = assemble(1, spot, second_pieces, (attended, w_inner))
        w_inner = spread(1, second_table, w_inner)
        w_outer = second_table[CUT:]
    scaled = attended * scale_row
    mixed = layer_norm(scaled, model_vec[4], model_vec[5])
    mixed_low = mixed.astype(BF)
    middle = inputs + (matmul(mixed_low, w_out) + model_vec[6])
    normed_two = layer_norm(middle, model_vec[7], model_vec[8])
    normed_two_low = normed_two.astype(BF)
    inner = matmul(normed_two_low, w_inner) + inner_vec[0]
    activated = exact_gelu(inner)
    inner_normed = layer_norm(activated, inner_vec[1], inner_vec[2])
    inner_low = inner_normed.astype(BF)
    result = middle + (matmul(inner_low, w_outer) + model_vec[9])
    result_rows = narrow(result.astype(BF))

    tokens_all = 2 * rows.shape[1] * P_SIZE * lax.axis_size("dp")
    share = 1.0 / tokens_all

    def weight_grad(left, right):
        value = matmul_tn(left, right) * share
        return value.astype(BF) if fast else value

    grad_out = widen(cotangent[0]).astype(F32) * own_valid
    grad_branch = grad_out.astype(BF)
    grad_w_outer = weight_grad(inner_low, grad_branch)
    grad_b_outer = jnp.sum(grad_branch.astype(F32), axis=0)
    grad_inner_normed = matmul_nt(grad_branch, w_outer)
    grad_activated, grad_gain_ff, grad_shift_ff = norm_back(
        activated, inner_vec[1], inner_vec[2], grad_inner_normed
    )
    _, gelu_pull = jax.vjp(exact_gelu, inner)
    grad_inner_low = gelu_pull(grad_activated)[0].astype(BF)
    if fast:
        grad_w_inner = inner_grad(normed_two_low, grad_inner_low, share)
    else:
        grad_w_inner = weight_grad(normed_two_low, grad_inner_low).reshape(FF, D)
    grad_b_inner = jnp.sum(grad_inner_low.astype(F32), axis=0)
    grad_normed_two = matmul_nt(grad_inner_low, w_inner)
    grad_mid_part, grad_gain_two, grad_shift_two = norm_back(
        middle, model_vec[7], model_vec[8], grad_normed_two
    )
    grad_middle = grad_out + grad_mid_part
    grad_attn_low = grad_middle.astype(BF)
    grad_w_out = weight_grad(mixed_low, grad_attn_low)
    grad_b_out = jnp.sum(grad_attn_low.astype(F32), axis=0)
    grad_mixed = matmul_nt(grad_attn_low, w_out)
    grad_scaled, grad_gain_attn, grad_shift_attn = norm_back(
        scaled, model_vec[4], model_vec[5], grad_mixed
    )
    grad_head_scale = jnp.sum(jnp.sum(grad_scaled * attended, axis=0).reshape(H, HD), axis=1)
    grad_attended = (grad_scaled * scale_row).astype(BF)
    parts = (counts, ids, table, logs, query, keys_both, values_both, grad_attended)
    if fast:
        kept, lent = scatter(1, spot, [None] * 4 + [grad_w_inner, grad_w_outer])
        early = attend_back(0, *parts, after=(kept,))
        got = send_mod(lent)
        late_outs, late_ins = reduce_outs(kept, got), reduce_ins(kept, got)
        late = attend_back(H // 4, *parts, before=early[:5], after=late_outs)
    else:
        early = attend_back(0, *parts)
        late = attend_back(H // 4, *parts, before=early[:5])
    grad_query, key_kept, value_kept, key_sent, value_sent, late_terms = late
    terms = (early[5], late_terms)
    back_keys, back_values = from_partner((key_sent, value_sent), "mod", 0)
    grad_key = (key_kept + back_keys.astype(F32)).astype(BF)
    grad_value = (value_kept + back_values.astype(F32)).astype(BF)
    grad_w_query = weight_grad(normed_low, grad_query)
    grad_w_key = weight_grad(normed_low, grad_key)
    grad_w_value = weight_grad(normed_low, grad_value)
    matrices = [grad_w_query, grad_w_key, grad_w_value, grad_w_out, grad_w_inner, grad_w_outer]
    if fast:
        late_sent = reduce_sends(late_outs)
        kept, lent = scatter(0, spot, matrices, late_sent)
        got = send_mod(lent)
        first_outs = reduce_outs(kept, got)
        grad_table = table_grad(ids, terms, (result_rows, *first_outs))
    else:
        grad_table = table_grad(ids, terms)
    grad_b_query = jnp.sum(grad_query.astype(F32), axis=0)
    grad_b_value = jnp.sum(grad_value.astype(F32), axis=0)
    grad_normed = (
        matmul_nt(grad_query, w_query) + matmul_nt(grad_key, w_key) + matmul_nt(grad_value, w_value)
    )
    grad_in_part, grad_gain_one, grad_shift_one = norm_back(
        inputs, model_vec[0], model_vec[1], grad_normed
    )
    grad_rows = narrow(grad_middle + grad_in_part)
    grad_model_vec = jnp.stack(
        [
            grad_gain_one,
            grad_shift_one,
            grad_b_query,
            grad_b_value,
            grad_gain_attn,
            grad_shift_attn,
            grad_b_out,
            grad_gain_two,
            grad_shift_two,
            grad_b_outer,
        ]
    )
    grad_inner_vec = jnp.stack([grad_b_inner, grad_gain_ff, grad_shift_ff])
    grad_heads = jnp.concatenate([grad_table, grad_head_scale[None, :]], axis=0)
    vec_grad = (
        jnp.concatenate(
            [grad_model_vec, grad_inner_vec.reshape(12, D), grad_heads.reshape(1, D)], axis=0
        )
        * share
    )
    if fast:
        second = reduce_phase(late_sent, late_ins)
        first = reduce_phase(reduce_sends(first_outs), reduce_ins(kept, got))
        vec_grad = sum_rest_small(sum_z_small(jnp.pad(vec_grad, ((0, 1), (0, 0)))))
        square = jnp.sum(first * first) + jnp.sum(second * second)
        square = square + jnp.where(is_last, jnp.sum(vec_grad * vec_grad), 0.0)
        square_sum = sum_scalar(square, side, place)
        grad_shard = unpack_shard(first, second, vec_grad, side, place)
    else:
        local_grad = jnp.concatenate([part.reshape(-1) for part in matrices + [vec_grad]])
        half_size = local_grad.shape[0] // 2
        own_half = lax.dynamic_slice_in_dim(local_grad, side * half_size, half_size)
        other_half = lax.dynamic_slice_in_dim(local_grad, (1 - side) * half_size, half_size)
        partner_half = from_partner(other_half.astype(BF), "mod", 0).astype(F32)
        grad_shard = lax.psum_scatter(own_half + partner_half, "dp", scatter_dimension=0, tiled=True)
        square_sum = lax.psum(jnp.sum(grad_shard * grad_shard), ("mod", "dp"))
    grad_norm = jnp.sqrt(square_sum)
    clip_scale = jnp.minimum(1.0, 0.25 / (grad_norm + 1e-06))
    clipped = grad_shard * clip_scale
    new_first = 0.5 * first_moment + 0.5 * clipped
    new_second = 0.6 * second_moment + 0.4 * clipped * clipped
    direction = new_first / (1.0 - 0.5**STEP) / (jnp.sqrt(new_second / (1.0 - 0.6**STEP)) + 1e-08)
    new_master = master - 0.04 * (direction + 0.01 * master)
    new_average = 0.5 * average + 0.5 * new_master
    return (
        result_rows,
        grad_rows,
        grad_norm,
        new_master,
        new_first,
        new_second,
        new_average,
        new_master.astype(jnp.bfloat16),
    )


def solution(mesh):
    placed = (
        P("mod", "dp", None, None),
        P("mod", "dp", None, None),
        P(("mod", "dp")),
        P(("mod", "dp")),
        P(("mod", "dp")),
        P(("mod", "dp")),
        P("dp"),
        P(),
    )
    return jax.shard_map(
        on_device,
        mesh=mesh,
        in_specs=placed,
        out_specs=(
            P("mod", "dp", None, None),
            P("mod", "dp", None, None),
            P(),
            P(("mod", "dp")),
            P(("mod", "dp")),
            P(("mod", "dp")),
            P(("mod", "dp")),
            P(("mod", "dp")),
        ),
        check_vma=False,
    )
```

```python
import functools
import jax
import jax.numpy as jnp
from jax import lax
from jax.experimental import pallas as pl
from jax.experimental.pallas import tpu as pltpu
from jax.sharding import PartitionSpec as P

D = 768
H = 12
HD = 64
FF = 3072
NB = 63
P_SIZE = 196
STEP = 5


HALF = D // 2
BLOCK = 144
PHASE_ROWS = 32 * BLOCK
BF = jnp.bfloat16
F32 = jnp.float32
DP = 16
EDGE = 17664
PAD = 208
KEYS = 512
HALF_KEYS = KEYS // 2
PAIR = 2 * HD
LIGHT = pl.CostEstimate(flops=1, bytes_accessed=1, transcendentals=0)


def x_swap():
    return [(i, i ^ 1) for i in range(DP)]


def y_swap():
    return [(i, i ^ 2) for i in range(DP)]


def z_turn(step):
    return [(i, (i // 4 + step) % 4 * 4 + i % 4) for i in range(DP)]


def send_dp(block, route):
    return lax.ppermute(block, "dp", route)


def send_mod(block):
    return lax.ppermute(block, "mod", [(0, 1), (1, 0)])


def pack_shard(own, side, place):
    lead = 8832 * side + 552 * place
    count = BLOCK * D
    lent = lax.dynamic_slice(own, (count - lead,), (count,))
    given = send_mod(lent)
    nxt = [(i, i + 1) for i in range(2 * DP - 1)]
    edge = lax.ppermute(own[own.shape[0] - EDGE :], ("mod", "dp"), nxt)
    kept = lax.dynamic_slice(jnp.concatenate([edge, own[:count]]), (EDGE - lead,), (count,))
    kept = kept.reshape(BLOCK, D)
    given = given.reshape(BLOCK, D)
    return jnp.where(side == 0, kept, given), jnp.where(side == 0, given, kept)


def unpack_shard(first, second, vec, side, place):
    lead = 8832 * side + 552 * place
    even = jnp.where(side == 0, first, second).reshape(-1)
    lent = jnp.where(side == 0, second, first)
    odd = send_mod(lent).reshape(-1)
    back = [(i + 1, i) for i in range(2 * DP - 1)]
    edge = lax.ppermute(even[:EDGE], ("mod", "dp"), back)
    is_last = jnp.logical_and(side == 1, place == DP - 1)
    edge = jnp.where(is_last, vec.reshape(-1)[:EDGE], edge)
    return lax.dynamic_slice(jnp.concatenate([even, odd, edge]), (lead,), (221736,))


def sum_z_small(part):
    part = part + send_dp(part, z_turn(2))
    return part + send_dp(part, [(i, i ^ 4) for i in range(DP)])


def sum_rest_small(part):
    part = part + send_dp(part, x_swap())
    part = part + send_dp(part, y_swap())
    return part + send_mod(part)


def xy_swap():
    return [(i, i ^ 3) for i in range(DP)]


def sum_scalar(value, side, place):
    slots = lax.broadcasted_iota(jnp.int32, (8, 128), 0) * 128
    slots = slots + lax.broadcasted_iota(jnp.int32, (8, 128), 1)
    own = jnp.where(slots == side * DP + place, value, 0.0)
    for routes in ([z_turn(1), z_turn(2), z_turn(3)], [x_swap(), y_swap(), xy_swap()]):
        got = [send_dp(own, route) for route in routes]
        own = own + got[0] + got[1] + got[2]
    return jnp.sum(own + send_mod(own))


def gather_z(block):
    return jnp.stack([block] + [send_dp(block, z_turn(step)) for step in (1, 2, 3)])


def gather_phase(stack):
    left, right = stack[:, :, :HALF], stack[:, :, HALF:]
    left_x = send_dp(left, x_swap())
    right_y = send_dp(right, y_swap())
    left_y = send_dp(left, y_swap())
    right_x = send_dp(right, x_swap())
    left_xy = send_dp(left_x, y_swap())
    right_xy = send_dp(right_y, x_swap())
    mine = [left, left_x, left_y, left_xy, right, right_x, right_y, right_xy]
    return mine + [send_mod(piece) for piece in mine]


def coords():
    side = lax.axis_index("mod")
    place = lax.axis_index("dp")
    return jnp.stack([side, place // 4, place // 2 % 2, place % 2]).astype(jnp.int32)


def assemble_body(phase, spot, *refs):
    pieces, out, sem = refs[:16], refs[-2], refs[-1]
    side, z, y, x = spot[0], spot[1], spot[2], spot[3]
    copies = []
    for index in range(16):
        other, half, yr, xr = index // 8, index // 4 % 2, index // 2 % 2, index % 2
        owner = side ^ other
        parity = owner if phase == 0 else 1 - owner
        for turn in range(4):
            home = ((z - turn) & 3) * 4 + (y ^ yr) * 2 + (x ^ xr)
            copies.append(
                pltpu.make_async_copy(
                    pieces[index].at[turn],
                    out.at[home * 2 + parity, :, pl.ds(half * HALF, HALF)],
                    sem.at[index * 4 + turn],
                )
            )
    for copy in copies:
        copy.start()
    for copy in copies:
        copy.wait()


def assemble(phase, spot, pieces, after=()):
    return pl.pallas_call(
        functools.partial(assemble_body, phase),
        out_shape=jax.ShapeDtypeStruct((32, BLOCK, D), BF),
        in_specs=[pl.BlockSpec(memory_space=pltpu.SMEM)] + [pl.BlockSpec(memory_space=pl.ANY)] * (16 + len(after)),
        out_specs=pl.BlockSpec(memory_space=pltpu.VMEM),
        scratch_shapes=[pltpu.SemaphoreType.DMA((64,))],
        cost_estimate=LIGHT,
        name="assemble",
    )(spot, *pieces, *after).reshape(PHASE_ROWS, D)


def scatter_body(phase, pieces, spot, *refs):
    sources, kept, lent, sem = refs[:-3], refs[-3], refs[-2], refs[-1]
    side, z, y, x = spot[0], spot[1], spot[2], spot[3]
    copies = []
    for block in range(32):
        home, parity = block // 2, block % 2
        owner = parity if phase == 0 else 1 - parity
        turn = (home // 4 - z) & 3
        yr = (home // 2 % 2) ^ y
        xr = (home % 2) ^ x
        for index, source_row, block_row, count in pieces[block]:
            for half in range(2):
                stay, leave = [
                    pltpu.make_async_copy(
                        sources[index].at[pl.ds(source_row, count), pl.ds(half * HALF, HALF)],
                        target.at[half, yr, xr, turn, pl.ds(block_row, count), :],
                        sem.at[len(copies)],
                    )
                    for target in (kept, lent)
                ]
                pl.when(side == owner)(stay.start)
                pl.when(side != owner)(leave.start)
                copies.append(stay)
    for copy in copies:
        copy.wait()


def scatter(phase, spot, tables, after=()):
    starts = [0]
    for rows in (D, D, D, D, FF, FF):
        starts.append(starts[-1] + rows)
    pieces = []
    for block in range(32):
        low = phase * PHASE_ROWS + block * BLOCK
        parts = []
        for index in range(len(tables)):
            first, last = max(low, starts[index]), min(low + BLOCK, starts[index + 1])
            if first < last:
                parts.append((index, first - starts[index], first - low, last - first))
        pieces.append(parts)
    used = sorted({part[0] for parts in pieces for part in parts})
    pieces = [[(used.index(part[0]),) + part[1:] for part in parts] for parts in pieces]
    count = 2 * sum(len(parts) for parts in pieces)
    return pl.pallas_call(
        functools.partial(scatter_body, phase, pieces),
        out_shape=(jax.ShapeDtypeStruct((2, 2, 2, 4, BLOCK, HALF), BF),) * 2,
        in_specs=[pl.BlockSpec(memory_space=pltpu.SMEM)]
        + [pl.BlockSpec(memory_space=pltpu.VMEM)] * len(used)
        + [pl.BlockSpec(memory_space=pl.ANY)] * len(after),
        out_specs=(pl.BlockSpec(memory_space=pl.ANY),) * 2,
        scratch_shapes=[pltpu.SemaphoreType.DMA((count,))],
        cost_estimate=LIGHT,
        name="scatter",
    )(spot, *[tables[index] for index in used], *after)


def plus(left, right):
    return (left.astype(F32) + right.astype(F32)).astype(BF)


def outs_body(*refs):
    left_mine, left_theirs, right_mine, right_theirs, left, right = refs[:4] + refs[-2:]
    index = pl.program_id(0)

    @pl.when(index < 2)
    def _():
        left[0] = plus(left_mine[0, 0, 0], left_theirs[0, 0, 0])

    @pl.when(index >= 2)
    def _():
        right[0] = plus(right_mine[0, 0, 0], right_theirs[0, 0, 0])


def reduce_outs(mine, theirs, after=()):
    block = (1, 1, 1, 4, BLOCK, HALF)
    left = pl.BlockSpec(block, lambda i: (0, jnp.minimum(i, 1), 1, 0, 0, 0))
    right = pl.BlockSpec(block, lambda i: (1, 1, jnp.maximum(i - 2, 0), 0, 0, 0))
    return pl.pallas_call(
        outs_body,
        grid=(4,),
        out_shape=(jax.ShapeDtypeStruct((2, 4, BLOCK, HALF), BF),) * 2,
        in_specs=[left, left, right, right] + [pl.BlockSpec(memory_space=pl.ANY)] * len(after),
        out_specs=(
            pl.BlockSpec((1, 4, BLOCK, HALF), lambda i: (jnp.minimum(i, 1), 0, 0, 0)),
            pl.BlockSpec((1, 4, BLOCK, HALF), lambda i: (jnp.maximum(i - 2, 0), 0, 0, 0)),
        ),
        cost_estimate=LIGHT,
        name="reduce_outs",
    )(mine, theirs, mine, theirs, *after)


def reduce_sends(outs):
    return send_dp(outs[0], x_swap()), send_dp(outs[1], y_swap())


def reduce_ins(mine, theirs):
    return plus(mine[0, :, 0], theirs[0, :, 0]), plus(mine[1, 0], theirs[1, 0])


def reduce_next(sent, ins):
    left_next = send_dp(plus(ins[0][1], sent[0][1]), y_swap())
    right_next = send_dp(plus(ins[1][1], sent[1][1]), x_swap())
    return left_next, right_next


def reduce_both(sent, ins, nexts):
    left, right = [
        ins[k][0].astype(F32) + sent[k][0].astype(F32) + nexts[k].astype(F32) for k in range(2)
    ]
    both = jnp.concatenate([left, right], axis=-1)
    return both[0], both.astype(BF)


def reduce_z(low):
    return [send_dp(low[step], z_turn(step)) for step in (1, 2, 3)]


def reduce_total(own, turns):
    return own + turns[0].astype(F32) + turns[1].astype(F32) + turns[2].astype(F32)


def dot_f32(left, right, dims):
    return lax.dot_general(left, right, (dims, ((), ())), preferred_element_type=F32)


NN = ((1,), (0,))
NT = ((1,), (1,))
TN = ((0,), (0,))


def bias_of(table_ref, ids_ref, head):
    entry = jnp.broadcast_to(table_ref[pl.ds(head, 1), :], (PAD, 128))
    return [
        jnp.take_along_axis(
            entry, ids_ref[:, c * 128 : (c + 1) * 128], axis=1, mode="promise_in_bounds"
        )
        for c in range(KEYS // 128)
    ]


def joint_keys(own_ref, other_ref, seq):
    rows = pl.ds(seq * PAD, PAD)
    gap = jnp.zeros((HALF_KEYS - PAD, PAIR), BF)
    return jnp.concatenate([own_ref[rows, :], gap, other_ref[rows, :], gap], axis=0)


def key_mask(counts_ref, seq):
    lane = lax.broadcasted_iota(jnp.int32, (1, KEYS), 1)
    own, other = counts_ref[seq], counts_ref[2 + seq]
    return jnp.logical_or(
        lane < own, jnp.logical_and(lane >= HALF_KEYS, lane < HALF_KEYS + other)
    )


def half_only(values, part):
    lane = lax.broadcasted_iota(jnp.int32, values.shape, 1)
    keep = lane < HD if part == 0 else lane >= HD
    return jnp.where(keep, values, jnp.zeros((), values.dtype))


def attend_body(counts, ids, table, query, key_own, key_other, value_own, value_other, *refs):
    out, logs = refs[-2:]
    pair = pl.program_id(0)
    keys = [joint_keys(key_own, key_other, seq) for seq in range(2)]
    values = [joint_keys(value_own, value_other, seq) for seq in range(2)]
    masks = [key_mask(counts, seq) for seq in range(2)]
    lane = lax.broadcasted_iota(jnp.int32, (PAD, 128), 1)
    done = [None, None]
    for part in range(2):
        head = 2 * pair + part
        bias = jnp.concatenate(bias_of(table, ids, head), axis=1)
        for seq in range(2):
            rows = pl.ds(seq * PAD, PAD)
            scores = dot_f32(half_only(query[rows, :], part), keys[seq], NT) * 0.125 + bias
            scores = jnp.where(masks[seq], scores, -1e30)
            top = jnp.max(scores, axis=1, keepdims=True)
            powers = jnp.exp(scores - top)
            total = jnp.sum(powers, axis=1, keepdims=True)
            probs = (powers * (1.0 / total)).astype(BF)
            got = dot_f32(probs, values[seq], NN)
            done[seq] = got if part == 0 else jnp.where(lane < HD, done[seq], got)
            logs[rows, :] = jnp.where(lane == head, top + jnp.log(total), logs[rows, :])
    for seq in range(2):
        out[pl.ds(seq * PAD, PAD), :] = done[seq]


def fixed(shape):
    return pl.BlockSpec(shape, lambda i: (0,) * len(shape))


def by_pair():
    return pl.BlockSpec((2 * PAD, PAIR), lambda i: (0, i))


def attend(counts, ids, table, query, key_own, key_other, value_own, value_other, after):
    return pl.pallas_call(
        attend_body,
        grid=(H // 2,),
        out_shape=(
            jax.ShapeDtypeStruct((2 * PAD, D), F32),
            jax.ShapeDtypeStruct((2 * PAD, 128), F32),
        ),
        in_specs=[pl.BlockSpec(memory_space=pltpu.SMEM), fixed((PAD, KEYS)), fixed((16, 128))]
        + [by_pair()] * 5
        + [pl.BlockSpec(memory_space=pl.ANY)] * len(after),
        out_specs=(by_pair(), fixed((2 * PAD, 128))),
        cost_estimate=LIGHT,
        name="attend",
    )(counts, ids, table, query, key_own, key_other, value_own, value_other, *after)


def attend_back_body(
    base, counts, ids, table, logs, query, key_own, key_other, value_own, value_other, grad, *refs
):
    grad_query, grad_key_own, grad_value_own, grad_key_other, grad_value_other, terms = refs[-6:]
    pair = pl.program_id(0) + base
    keys = [joint_keys(key_own, key_other, seq) for seq in range(2)]
    values = [joint_keys(value_own, value_other, seq) for seq in range(2)]
    masks = [key_mask(counts, seq) for seq in range(2)]
    lane = lax.broadcasted_iota(jnp.int32, (PAD, 128), 1)
    to_query, to_key, to_value = [0.0, 0.0], [0.0, 0.0], [0.0, 0.0]
    for part in range(2):
        head = 2 * pair + part
        bias = jnp.concatenate(bias_of(table, ids, head), axis=1)
        both = 0.0
        for seq in range(2):
            rows = pl.ds(seq * PAD, PAD)
            asked = half_only(query[rows, :], part)
            into = half_only(grad[rows, :], part)
            scores = dot_f32(asked, keys[seq], NT) * 0.125 + bias
            scores = jnp.where(masks[seq], scores, -1e30)
            log = jnp.sum(jnp.where(lane == head, logs[rows, :], 0.0), axis=1, keepdims=True)
            probs = jnp.exp(scores - log)
            grad_probs = dot_f32(into, values[seq], NT)
            mean = jnp.sum(probs * grad_probs, axis=1, keepdims=True)
            grad_scores = (probs * (grad_probs - mean)).astype(BF)
            both = both + grad_scores.astype(F32)
            to_value[seq] = to_value[seq] + dot_f32(probs.astype(BF), into, TN)
            to_query[seq] = to_query[seq] + dot_f32(grad_scores, half_only(keys[seq], part), NN)
            to_key[seq] = to_key[seq] + dot_f32(grad_scores, asked, TN)
        for c in range(KEYS // 128):
            terms[c, pl.ds(head - 2 * base, PAD, stride=8), :] = both[:, c * 128 : (c + 1) * 128]
    for seq in range(2):
        rows = pl.ds(seq * PAD, PAD)
        grad_query[rows, :] = (to_query[seq] * 0.125).astype(BF)
        grad_key_own[rows, :] = to_key[seq][:PAD] * 0.125
        grad_key_other[rows, :] = (to_key[seq][HALF_KEYS : HALF_KEYS + PAD] * 0.125).astype(BF)
        grad_value_own[rows, :] = to_value[seq][:PAD]
        grad_value_other[rows, :] = to_value[seq][HALF_KEYS : HALF_KEYS + PAD].astype(BF)


def attend_back(base, counts, ids, table, logs, query, keys, values, grad, before=(), after=()):
    def rows_of(kind):
        return jax.ShapeDtypeStruct((2 * PAD, D), kind)

    columns = pl.BlockSpec((2 * PAD, PAIR), lambda i: (0, i + base))
    any_ref = pl.BlockSpec(memory_space=pl.ANY)
    return pl.pallas_call(
        functools.partial(attend_back_body, base),
        grid=(H // 4,),
        out_shape=(
            rows_of(BF),
            rows_of(F32),
            rows_of(F32),
            rows_of(BF),
            rows_of(BF),
            jax.ShapeDtypeStruct((KEYS // 128, PAD * 8, 128), F32),
        ),
        in_specs=[
            pl.BlockSpec(memory_space=pltpu.SMEM),
            fixed((PAD, KEYS)),
            fixed((16, 128)),
            fixed((2 * PAD, 128)),
        ]
        + [columns] * 6
        + [any_ref] * (len(before) + len(after)),
        out_specs=(columns,) * 5 + (fixed((KEYS // 128, PAD * 8, 128)),),
        input_output_aliases={10 + i: i for i in range(len(before))},
        cost_estimate=LIGHT,
        name="attend_back",
    )(counts, ids, table, logs, query, *keys, *values, grad, *before, *after)


GROUP = 4


def table_body(ids, early, late, *refs):
    out = refs[-1]
    bucket = lax.broadcasted_iota(jnp.int32, (NB + 1, KEYS), 0)

    def step(index, totals):
        fresh = []
        for lane_group in range(GROUP):
            row = index * GROUP + lane_group
            hot = jnp.where(ids[pl.ds(row, 1), :] == bucket, 1.0, 0.0).astype(BF)
            span = pl.ds(pl.multiple_of(row * 8, 8), 8)
            term = jnp.concatenate(
                [
                    jnp.concatenate([terms[c, span, :] for c in range(KEYS // 128)], axis=1)
                    for terms in (early, late)
                ],
                axis=0,
            )
            high = term.astype(BF)
            low = (term - high.astype(F32)).astype(BF)
            both = jnp.concatenate([high, low], axis=0)
            fresh.append(totals[lane_group] + dot_f32(hot, both, NT))
        return tuple(fresh)

    zero = jnp.zeros((NB + 1, 32), F32)
    totals = lax.fori_loop(0, P_SIZE // GROUP, step, (zero,) * GROUP)
    total = totals[0] + totals[1] + totals[2] + totals[3]
    out[...] = total


def table_grad(ids, terms, after=()):
    whole = pl.BlockSpec(memory_space=pltpu.VMEM)
    both = pl.pallas_call(
        table_body,
        out_shape=jax.ShapeDtypeStruct((NB + 1, 32), F32),
        in_specs=[whole] * 3 + [pl.BlockSpec(memory_space=pl.ANY)] * len(after),
        out_specs=whole,
        cost_estimate=LIGHT,
        name="table_grad",
    )(ids, *terms, *after)
    both = both[:NB, :16] + both[:NB, 16:]
    return jnp.concatenate([both[:, : H // 2], both[:, 8 : 8 + H // 2]], axis=1)


CUT = PHASE_ROWS - 4 * D


def spread_body(half, table, *refs):
    out, held = refs[-2], refs[-1]
    start = 4 * D if half == 0 else 0
    for c in range(D // 128):
        held[...] = table[pl.ds(start, CUT), pl.ds(c * 128, 128)].astype(F32)
        for part in range(4):
            out[:, pl.ds(part * D + c * 128, 128)] = held[
                pl.ds(part, CUT // 4, stride=4), :
            ].astype(BF)


def spread(half, table, before=None):
    whole = pl.BlockSpec(memory_space=pltpu.VMEM)
    extra = () if before is None else (before,)
    return pl.pallas_call(
        functools.partial(spread_body, half),
        grid=(1,),
        out_shape=jax.ShapeDtypeStruct((D, FF), BF),
        in_specs=[whole] + [pl.BlockSpec(memory_space=pl.ANY)] * len(extra),
        out_specs=pl.BlockSpec((CUT // 4, FF), lambda i: (half, 0)),
        scratch_shapes=[pltpu.VMEM((CUT, 128), F32)],
        input_output_aliases={1: 0} if extra else {},
        cost_estimate=LIGHT,
        name="spread",
    )(table, *extra)


def inner_grad_body(share, left, right, out, turned, held):
    chunk = pl.program_id(0)

    @pl.when(chunk == 0)
    def _():
        gap = jnp.zeros((KEYS - 2 * PAD, D), BF)
        turned[...] = jnp.concatenate([left[...], gap], axis=0).T

    gap = jnp.zeros((KEYS - 2 * PAD, 256), BF)
    for part in range(4):
        start = pl.multiple_of(part * D + chunk * 256, 256)
        block = jnp.concatenate([right[:, pl.ds(start, 256)], gap], axis=0)
        value = dot_f32(turned[...], block, NN) * share
        for c in range(2):
            held[c, pl.ds(part, D, stride=4), :] = value[:, c * 128 : (c + 1) * 128]
    out[...] = jnp.concatenate([held[0], held[1]], axis=1).astype(BF)


def inner_grad(left, right, share):
    return pl.pallas_call(
        functools.partial(inner_grad_body, share),
        grid=(D // 256,),
        out_shape=jax.ShapeDtypeStruct((FF, D), BF),
        in_specs=[fixed((2 * PAD, D)), fixed((2 * PAD, FF))],
        out_specs=pl.BlockSpec((FF, 256), lambda i: (0, i)),
        scratch_shapes=[pltpu.VMEM((D, KEYS), BF), pltpu.VMEM((2, FF, 128), F32)],
        cost_estimate=LIGHT,
        name="inner_grad",
    )(left, right)


def from_partner(block, axis, bit):
    count = lax.axis_size(axis)
    route = []
    for low in range(count):
        high = low | 1 << bit
        if high != low and high < count:
            route += [(low, high), (high, low)]
    return lax.ppermute(block, axis, route)


def layer_norm(values, gain, shift):
    center = values - jnp.mean(values, axis=-1, keepdims=True)
    spread = jnp.mean(center * center, axis=-1, keepdims=True)
    return center * lax.rsqrt(spread + 1e-05) * gain + shift


def norm_back(values, gain, shift, grad_after):
    _, pullback = jax.vjp(layer_norm, values, gain, shift)
    return pullback(grad_after)


def matmul(left, right):
    return jnp.dot(left, right, preferred_element_type=jnp.float32)


def matmul_tn(left, right):
    return lax.dot_general(
        left, right, (((0,), (0,)), ((), ())), preferred_element_type=jnp.float32
    )


def matmul_nt(left, right):
    return lax.dot_general(
        left, right, (((1,), (1,)), ((), ())), preferred_element_type=jnp.float32
    )


def exact_gelu(values):
    return jax.nn.gelu(values, approximate=False)


def unpack(flat):
    pairs = [(D, D), (D, D), (D, D), (D, D), (D, FF), (FF, D), (10, D), (3, FF), (NB + 1, H)]
    pieces = []
    offset = 0
    for dims_pair in pairs:
        extent = dims_pair[0] * dims_pair[1]
        pieces.append(flat[offset : offset + extent].reshape(dims_pair))
        offset += extent
    return pieces


def widen(values):
    return jnp.pad(values, ((0, 0), (0, PAD - P_SIZE), (0, 0))).reshape(2 * PAD, D)


def narrow(values):
    return values.reshape(1, 2, PAD, D)[:, :, :P_SIZE]


def on_device(rows, cotangent, master, first_moment, second_moment, average, lengths, buckets):
    side = lax.axis_index("mod")
    place = lax.axis_index("dp")
    fast = lax.axis_size("dp") == DP
    own_copy = master.astype(jnp.bfloat16)
    if fast:
        spot = coords()
        first, second = pack_shard(own_copy, side, place)
        is_last = jnp.logical_and(side == 1, place == DP - 1)
        vec = jnp.where(is_last, own_copy[-EDGE:], jnp.zeros((), BF))
        vec = jnp.pad(vec, (0, D)).reshape(24, D)
        vec = sum_rest_small(sum_z_small(vec))
        first_stack, second = lax.optimization_barrier((gather_z(first), second))
        second_stack = gather_z(second)
        first_table = assemble(0, spot, gather_phase(first_stack), (second_stack,))
        second_pieces = gather_phase(second_stack)
        square = [first_table[i * D : (i + 1) * D] for i in range(4)]
        vec_model, vec_inner = vec[:10], vec[10:22].reshape(3, FF)
        head_table = vec[22].reshape(NB + 1, H)
    else:
        weights = unpack(lax.all_gather(own_copy, ("mod", "dp"), axis=0, tiled=True))
        square, (w_inner, w_outer, vec_model, vec_inner, head_table) = weights[:4], weights[4:]
    w_query, w_key, w_value, w_out = square
    model_vec = vec_model.astype(jnp.float32)
    inner_vec = vec_inner.astype(jnp.float32)
    head_vals = head_table.astype(jnp.float32)
    scale_row = jnp.repeat(head_vals[NB], HD)
    table = jnp.pad(head_vals.T, ((0, 16 - H), (0, 128 - NB - 1)))
    full = jnp.full_like(lengths, P_SIZE)
    own_count = jnp.where(side == 0, full, lengths)
    other_count = jnp.where(side == 0, lengths, full)
    counts = jnp.concatenate([own_count, other_count]).astype(jnp.int32)
    slots = jnp.arange(PAD, dtype=jnp.int32)
    own_valid = (slots[None, :] < own_count[:, None]).astype(F32).reshape(2 * PAD, 1)
    near = lax.dynamic_slice(buckets, (side * P_SIZE, side * P_SIZE), (P_SIZE, P_SIZE))
    far = lax.dynamic_slice(buckets, (side * P_SIZE, (1 - side) * P_SIZE), (P_SIZE, P_SIZE))
    room = ((0, PAD - P_SIZE), (0, HALF_KEYS - P_SIZE))
    ids = jnp.concatenate([jnp.pad(near, room), jnp.pad(far, room)], axis=1)

    inputs = widen(rows[0]).astype(F32)
    normed = layer_norm(inputs, model_vec[0], model_vec[1])
    normed_low = normed.astype(BF)
    keys_own = matmul(normed_low, w_key).astype(BF)
    values_own = (matmul(normed_low, w_value) + model_vec[3]).astype(BF)
    keys_other, values_other = from_partner((keys_own, values_own), "mod", 0)
    asking = normed_low
    if fast:
        sent_early = (second_pieces[1], second_pieces[6])
        asking, sent_early = lax.optimization_barrier((asking, sent_early))
    query = (matmul(asking, w_query) + model_vec[2]).astype(BF)
    keys_both, values_both = (keys_own, keys_other), (values_own, values_other)
    sent_early = sent_early if fast else ()
    attended, logs = attend(counts, ids, table, query, *keys_both, *values_both, sent_early)

    if fast:
        w_inner = spread(0, first_table)
        second_table = assemble(1, spot, second_pieces, (attended, w_inner))
        w_inner = spread(1, second_table, w_inner)
        w_outer = second_table[CUT:]
    scaled = attended * scale_row
    mixed = layer_norm(scaled, model_vec[4], model_vec[5])
    mixed_low = mixed.astype(BF)
    middle = inputs + (matmul(mixed_low, w_out) + model_vec[6])
    normed_two = layer_norm(middle, model_vec[7], model_vec[8])
    normed_two_low = normed_two.astype(BF)
    inner = matmul(normed_two_low, w_inner) + inner_vec[0]
    activated = exact_gelu(inner)
    inner_normed = layer_norm(activated, inner_vec[1], inner_vec[2])
    inner_low = inner_normed.astype(BF)
    result = middle + (matmul(inner_low, w_outer) + model_vec[9])
    result_rows = narrow(result.astype(BF))

    tokens_all = 2 * rows.shape[1] * P_SIZE * lax.axis_size("dp")
    share = 1.0 / tokens_all

    def weight_grad(left, right):
        value = matmul_tn(left, right) * share
        return value.astype(BF) if fast else value

    grad_out = widen(cotangent[0]).astype(F32) * own_valid
    grad_branch = grad_out.astype(BF)
    grad_w_outer = weight_grad(inner_low, grad_branch)
    grad_b_outer = jnp.sum(grad_branch.astype(F32), axis=0)
    grad_inner_normed = matmul_nt(grad_branch, w_outer)
    grad_activated, grad_gain_ff, grad_shift_ff = norm_back(
        activated, inner_vec[1], inner_vec[2], grad_inner_normed
    )
    _, gelu_pull = jax.vjp(exact_gelu, inner)
    grad_inner_low = gelu_pull(grad_activated)[0].astype(BF)
    if fast:
        grad_w_inner = inner_grad(normed_two_low, grad_inner_low, share)
    else:
        grad_w_inner = weight_grad(normed_two_low, grad_inner_low).reshape(FF, D)
    grad_b_inner = jnp.sum(grad_inner_low.astype(F32), axis=0)
    grad_normed_two = matmul_nt(grad_inner_low, w_inner)
    grad_mid_part, grad_gain_two, grad_shift_two = norm_back(
        middle, model_vec[7], model_vec[8], grad_normed_two
    )
    grad_middle = grad_out + grad_mid_part
    grad_attn_low = grad_middle.astype(BF)
    grad_w_out = weight_grad(mixed_low, grad_attn_low)
    grad_b_out = jnp.sum(grad_attn_low.astype(F32), axis=0)
    grad_mixed = matmul_nt(grad_attn_low, w_out)
    grad_scaled, grad_gain_attn, grad_shift_attn = norm_back(
        scaled, model_vec[4], model_vec[5], grad_mixed
    )
    grad_head_scale = jnp.sum(jnp.sum(grad_scaled * attended, axis=0).reshape(H, HD), axis=1)
    grad_attended = (grad_scaled * scale_row).astype(BF)
    parts = (counts, ids, table, logs, query, keys_both, values_both, grad_attended)
    if fast:
        kept, lent = scatter(1, spot, [None] * 4 + [grad_w_inner, grad_w_outer])
        early = attend_back(0, *parts, after=(kept,))
        got = send_mod(lent)
        late_outs, late_ins = reduce_outs(kept, got), reduce_ins(kept, got)
        late = attend_back(H // 4, *parts, before=early[:5], after=late_outs)
    else:
        early = attend_back(0, *parts)
        late = attend_back(H // 4, *parts, before=early[:5])
    grad_query, key_kept, value_kept, key_sent, value_sent, late_terms = late
    terms = (early[5], late_terms)
    back_keys, back_values = from_partner((key_sent, value_sent), "mod", 0)
    if fast:
        back_keys, back_values, late_sent = lax.optimization_barrier(
            (back_keys, back_values, reduce_sends(late_outs))
        )
    grad_key = (key_kept + back_keys.astype(F32)).astype(BF)
    grad_value = (value_kept + back_values.astype(F32)).astype(BF)
    grad_w_query = weight_grad(normed_low, grad_query)
    grad_w_key = weight_grad(normed_low, grad_key)
    grad_w_value = weight_grad(normed_low, grad_value)
    matrices = [grad_w_query, grad_w_key, grad_w_value, grad_w_out, grad_w_inner, grad_w_outer]
    if fast:
        kept, lent = scatter(0, spot, matrices)
        got = send_mod(lent)
        late_next = reduce_next(late_sent, late_ins)
        first_outs = reduce_outs(kept, got, late_next)
        late_both, late_low = reduce_both(late_sent, late_ins, late_next)
        grad_table = table_grad(ids, terms, (result_rows, *first_outs))
        late_turns, first_sent, grad_table = lax.optimization_barrier(
            (reduce_z(late_low), reduce_sends(first_outs), grad_table)
        )
    else:
        grad_table = table_grad(ids, terms)
    grad_b_query = jnp.sum(grad_query.astype(F32), axis=0)
    grad_b_value = jnp.sum(grad_value.astype(F32), axis=0)
    grad_normed = (
        matmul_nt(grad_query, w_query) + matmul_nt(grad_key, w_key) + matmul_nt(grad_value, w_value)
    )
    grad_in_part, grad_gain_one, grad_shift_one = norm_back(
        inputs, model_vec[0], model_vec[1], grad_normed
    )
    grad_rows = narrow(grad_middle + grad_in_part)
    grad_model_vec = jnp.stack(
        [
            grad_gain_one,
            grad_shift_one,
            grad_b_query,
            grad_b_value,
            grad_gain_attn,
            grad_shift_attn,
            grad_b_out,
            grad_gain_two,
            grad_shift_two,
            grad_b_outer,
        ]
    )
    grad_inner_vec = jnp.stack([grad_b_inner, grad_gain_ff, grad_shift_ff])
    grad_heads = jnp.concatenate([grad_table, grad_head_scale[None, :]], axis=0)
    vec_grad = (
        jnp.concatenate(
            [grad_model_vec, grad_inner_vec.reshape(12, D), grad_heads.reshape(1, D)], axis=0
        )
        * share
    )
    if fast:
        second = reduce_total(late_both, late_turns)
        first_ins = reduce_ins(kept, got)
        first_next = reduce_next(first_sent, first_ins)
        first_both, first_low = reduce_both(first_sent, first_ins, first_next)
        vec_grad = sum_z_small(jnp.pad(vec_grad, ((0, 1), (0, 0))))
        vec_grad, first_low = lax.optimization_barrier((vec_grad, first_low))
        first = reduce_total(first_both, reduce_z(first_low))
        vec_grad = sum_rest_small(vec_grad)
        square = jnp.sum(first * first) + jnp.sum(second * second)
        square = square + jnp.where(is_last, jnp.sum(vec_grad * vec_grad), 0.0)
        square_sum = sum_scalar(square, side, place)
        grad_shard = unpack_shard(first, second, vec_grad, side, place)
    else:
        local_grad = jnp.concatenate([part.reshape(-1) for part in matrices + [vec_grad]])
        half_size = local_grad.shape[0] // 2
        own_half = lax.dynamic_slice_in_dim(local_grad, side * half_size, half_size)
        other_half = lax.dynamic_slice_in_dim(local_grad, (1 - side) * half_size, half_size)
        partner_half = from_partner(other_half.astype(BF), "mod", 0).astype(F32)
        grad_shard = lax.psum_scatter(own_half + partner_half, "dp", scatter_dimension=0, tiled=True)
        square_sum = lax.psum(jnp.sum(grad_shard * grad_shard), ("mod", "dp"))
    grad_norm = jnp.sqrt(square_sum)
    clip_scale = jnp.minimum(1.0, 0.25 / (grad_norm + 1e-06))
    clipped = grad_shard * clip_scale
    new_first = 0.5 * first_moment + 0.5 * clipped
    new_second = 0.6 * second_moment + 0.4 * clipped * clipped
    direction = new_first / (1.0 - 0.5**STEP) / (jnp.sqrt(new_second / (1.0 - 0.6**STEP)) + 1e-08)
    new_master = master - 0.04 * (direction + 0.01 * master)
    new_average = 0.5 * average + 0.5 * new_master
    return (
        result_rows,
        grad_rows,
        grad_norm,
        new_master,
        new_first,
        new_second,
        new_average,
        new_master.astype(jnp.bfloat16),
    )


def solution(mesh):
    placed = (
        P("mod", "dp", None, None),
        P("mod", "dp", None, None),
        P(("mod", "dp")),
        P(("mod", "dp")),
        P(("mod", "dp")),
        P(("mod", "dp")),
        P("dp"),
        P(),
    )
    return jax.shard_map(
        on_device,
        mesh=mesh,
        in_specs=placed,
        out_specs=(
            P("mod", "dp", None, None),
            P("mod", "dp", None, None),
            P(),
            P(("mod", "dp")),
            P(("mod", "dp")),
            P(("mod", "dp")),
            P(("mod", "dp")),
            P(("mod", "dp")),
        ),
        check_vma=False,
    )
```

```python
import functools
import jax
import jax.numpy as jnp
from jax import lax
from jax.experimental import pallas as pl
from jax.experimental.pallas import tpu as pltpu
from jax.sharding import PartitionSpec as P

D = 768
H = 12
HD = 64
FF = 3072
NB = 63
P_SIZE = 196
STEP = 5


HALF = D // 2
BLOCK = 144
PHASE_ROWS = 32 * BLOCK
BF = jnp.bfloat16
F32 = jnp.float32
DP = 16
EDGE = 17664
PAD = 208
KEYS = 512
HALF_KEYS = KEYS // 2
PAIR = 2 * HD
LIGHT = pl.CostEstimate(flops=1, bytes_accessed=1, transcendentals=0)


def x_swap():
    return [(i, i ^ 1) for i in range(DP)]


def y_swap():
    return [(i, i ^ 2) for i in range(DP)]


def z_turn(step):
    return [(i, (i // 4 + step) % 4 * 4 + i % 4) for i in range(DP)]


def send_dp(block, route):
    return lax.ppermute(block, "dp", route)


def send_mod(block):
    return lax.ppermute(block, "mod", [(0, 1), (1, 0)])


def pack_shard(own, side, place):
    lead = 8832 * side + 552 * place
    count = BLOCK * D
    lent = lax.dynamic_slice(own, (count - lead,), (count,))
    given = send_mod(lent)
    nxt = [(i, i + 1) for i in range(2 * DP - 1)]
    edge = lax.ppermute(own[own.shape[0] - EDGE :], ("mod", "dp"), nxt)
    kept = lax.dynamic_slice(jnp.concatenate([edge, own[:count]]), (EDGE - lead,), (count,))
    kept = kept.reshape(BLOCK, D)
    given = given.reshape(BLOCK, D)
    return jnp.where(side == 0, kept, given), jnp.where(side == 0, given, kept)


def unpack_sends(first, second, side):
    even = jnp.where(side == 0, first, second).reshape(-1)
    lent = jnp.where(side == 0, second, first)
    odd = send_mod(lent)
    back = [(i + 1, i) for i in range(2 * DP - 1)]
    return even, odd, lax.ppermute(even[:EDGE], ("mod", "dp"), back)


def unpack_shard(even, odd, edge, vec, side, place):
    lead = 8832 * side + 552 * place
    is_last = jnp.logical_and(side == 1, place == DP - 1)
    edge = jnp.where(is_last, vec.reshape(-1)[:EDGE], edge)
    return lax.dynamic_slice(jnp.concatenate([even, odd.reshape(-1), edge]), (lead,), (221736,))


def sum_all_small(part):
    part = part + send_dp(part, x_swap())
    part = part + send_dp(part, y_swap())
    part = sum_z_small(part)
    return part + send_mod(part)


def sum_z_small(part):
    part = part + send_dp(part, z_turn(2))
    return part + send_dp(part, [(i, i ^ 4) for i in range(DP)])


def sum_rest_small(part):
    part = part + send_dp(part, x_swap())
    part = part + send_dp(part, y_swap())
    return part + send_mod(part)


def xy_swap():
    return [(i, i ^ 3) for i in range(DP)]


def sum_scalar(value, side, place, beside):
    slots = lax.broadcasted_iota(jnp.int32, (8, 128), 0) * 128
    slots = slots + lax.broadcasted_iota(jnp.int32, (8, 128), 1)
    own = jnp.where(slots == side * DP + place, value, 0.0)
    for routes in ([z_turn(1), z_turn(2), z_turn(3)], [x_swap(), y_swap(), xy_swap()]):
        got = [send_dp(own, route) for route in routes]
        own = own + got[0] + got[1] + got[2]
        own, beside = lax.optimization_barrier((own, beside))
    return jnp.sum(own + send_mod(own)), beside


def gather_z(block):
    return [block] + [send_dp(block, z_turn(step)) for step in (1, 2, 3)]


def gather_near(stack):
    left, right = stack[:, :, :HALF], stack[:, :, HALF:]
    got = send_dp(left, x_swap()), send_dp(right, y_swap())
    return (left, right), got


def gather_far(near, got):
    left = jnp.stack([near[0], got[0]])
    right = jnp.stack([near[1], got[1]])
    far = send_dp(left, y_swap()), send_dp(right, x_swap())
    mine = [left, right, *far]
    return mine + [send_mod(piece) for piece in mine]


def coords():
    side = lax.axis_index("mod")
    place = lax.axis_index("dp")
    return jnp.stack([side, place // 4, place // 2 % 2, place % 2]).astype(jnp.int32)


def assemble_body(phase, spot, *refs):
    pieces, out, sem = refs[:8], refs[-2], refs[-1]
    side, z, y, x = spot[0], spot[1], spot[2], spot[3]
    copies = []
    for index in range(16):
        other, half, yr, xr = index // 8, index // 4 % 2, index // 2 % 2, index % 2
        owner = side ^ other
        parity = owner if phase == 0 else 1 - owner
        source = pieces[other * 4 + (yr if half == 0 else xr) * 2 + half]
        for turn in range(4):
            home = ((z - turn) & 3) * 4 + (y ^ yr) * 2 + (x ^ xr)
            copies.append(
                pltpu.make_async_copy(
                    source.at[xr if half == 0 else yr, turn],
                    out.at[home * 2 + parity, :, pl.ds(half * HALF, HALF)],
                    sem.at[index * 4 + turn],
                )
            )
    for copy in copies:
        copy.start()
    for copy in copies:
        copy.wait()


def assemble(phase, spot, pieces, after=()):
    return pl.pallas_call(
        functools.partial(assemble_body, phase),
        out_shape=jax.ShapeDtypeStruct((32, BLOCK, D), BF),
        in_specs=[pl.BlockSpec(memory_space=pltpu.SMEM)] + [pl.BlockSpec(memory_space=pl.ANY)] * (8 + len(after)),
        out_specs=pl.BlockSpec(memory_space=pltpu.VMEM),
        scratch_shapes=[pltpu.SemaphoreType.DMA((64,))],
        cost_estimate=LIGHT,
        name="assemble",
    )(spot, *pieces, *after).reshape(PHASE_ROWS, D)


def scatter_body(phase, pieces, spot, *refs):
    sources, kept, lent, sem = refs[:-3], refs[-3], refs[-2], refs[-1]
    side, z, y, x = spot[0], spot[1], spot[2], spot[3]
    copies = []
    for block in range(32):
        home, parity = block // 2, block % 2
        owner = parity if phase == 0 else 1 - parity
        turn = (home // 4 - z) & 3
        yr = (home // 2 % 2) ^ y
        xr = (home % 2) ^ x
        for index, source_row, block_row, count in pieces[block]:
            for half in range(2):
                stay, leave = [
                    pltpu.make_async_copy(
                        sources[index].at[pl.ds(source_row, count), pl.ds(half * HALF, HALF)],
                        target.at[half, yr, xr, turn, pl.ds(block_row, count), :],
                        sem.at[len(copies)],
                    )
                    for target in (kept, lent)
                ]
                pl.when(side == owner)(stay.start)
                pl.when(side != owner)(leave.start)
                copies.append(stay)
    for copy in copies:
        copy.wait()


def scatter(phase, spot, tables, after=()):
    starts = [0]
    for rows in (D, D, D, D, FF, FF):
        starts.append(starts[-1] + rows)
    pieces = []
    for block in range(32):
        low = phase * PHASE_ROWS + block * BLOCK
        parts = []
        for index in range(len(tables)):
            first, last = max(low, starts[index]), min(low + BLOCK, starts[index + 1])
            if first < last:
                parts.append((index, first - starts[index], first - low, last - first))
        pieces.append(parts)
    used = sorted({part[0] for parts in pieces for part in parts})
    pieces = [[(used.index(part[0]),) + part[1:] for part in parts] for parts in pieces]
    count = 2 * sum(len(parts) for parts in pieces)
    return pl.pallas_call(
        functools.partial(scatter_body, phase, pieces),
        out_shape=(jax.ShapeDtypeStruct((2, 2, 2, 4, BLOCK, HALF), BF),) * 2,
        in_specs=[pl.BlockSpec(memory_space=pltpu.SMEM)]
        + [pl.BlockSpec(memory_space=pltpu.VMEM)] * len(used)
        + [pl.BlockSpec(memory_space=pl.ANY)] * len(after),
        out_specs=(pl.BlockSpec(memory_space=pl.ANY),) * 2,
        scratch_shapes=[pltpu.SemaphoreType.DMA((count,))],
        cost_estimate=LIGHT,
        name="scatter",
    )(spot, *[tables[index] for index in used], *after)


def plus(left, right):
    return (left.astype(F32) + right.astype(F32)).astype(BF)


def outs_body(*refs):
    left_mine, left_theirs, right_mine, right_theirs, left, right = refs[:4] + refs[-2:]
    index = pl.program_id(0)

    @pl.when(index < 2)
    def _():
        left[0] = plus(left_mine[0, 0, 0], left_theirs[0, 0, 0])

    @pl.when(index >= 2)
    def _():
        right[0] = plus(right_mine[0, 0, 0], right_theirs[0, 0, 0])


def reduce_outs(mine, theirs, after=()):
    block = (1, 1, 1, 4, BLOCK, HALF)
    left = pl.BlockSpec(block, lambda i: (0, jnp.minimum(i, 1), 1, 0, 0, 0))
    right = pl.BlockSpec(block, lambda i: (1, 1, jnp.maximum(i - 2, 0), 0, 0, 0))
    return pl.pallas_call(
        outs_body,
        grid=(4,),
        out_shape=(jax.ShapeDtypeStruct((2, 4, BLOCK, HALF), BF),) * 2,
        in_specs=[left, left, right, right] + [pl.BlockSpec(memory_space=pl.ANY)] * len(after),
        out_specs=(
            pl.BlockSpec((1, 4, BLOCK, HALF), lambda i: (jnp.minimum(i, 1), 0, 0, 0)),
            pl.BlockSpec((1, 4, BLOCK, HALF), lambda i: (jnp.maximum(i - 2, 0), 0, 0, 0)),
        ),
        cost_estimate=LIGHT,
        name="reduce_outs",
    )(mine, theirs, mine, theirs, *after)


def reduce_sends(outs):
    return send_dp(outs[0], x_swap()), send_dp(outs[1], y_swap())


def reduce_ins(mine, theirs):
    return plus(mine[0, :, 0], theirs[0, :, 0]), plus(mine[1, 0], theirs[1, 0])


def reduce_next(sent, ins):
    left_next = send_dp(plus(ins[0][1], sent[0][1]), y_swap())
    right_next = send_dp(plus(ins[1][1], sent[1][1]), x_swap())
    return left_next, right_next


def reduce_both(sent, ins, nexts):
    left, right = [
        ins[k][0].astype(F32) + sent[k][0].astype(F32) + nexts[k].astype(F32) for k in range(2)
    ]
    both = jnp.concatenate([left, right], axis=-1)
    return both[0], both.astype(BF)


def reduce_z(low):
    return [send_dp(low[step], z_turn(step)) for step in (1, 2, 3)]


def reduce_total(own, turns):
    return own + turns[0].astype(F32) + turns[1].astype(F32) + turns[2].astype(F32)


def dot_f32(left, right, dims):
    return lax.dot_general(left, right, (dims, ((), ())), preferred_element_type=F32)


NN = ((1,), (0,))
NT = ((1,), (1,))
TN = ((0,), (0,))


def bias_of(table_ref, ids_ref, head):
    entry = jnp.broadcast_to(table_ref[pl.ds(head, 1), :], (PAD, 128))
    return [
        jnp.take_along_axis(
            entry, ids_ref[:, c * 128 : (c + 1) * 128], axis=1, mode="promise_in_bounds"
        )
        for c in range(KEYS // 128)
    ]


def joint_keys(own_ref, other_ref, seq):
    rows = pl.ds(seq * PAD, PAD)
    gap = jnp.zeros((HALF_KEYS - PAD, PAIR), BF)
    return jnp.concatenate([own_ref[rows, :], gap, other_ref[rows, :], gap], axis=0)


def key_mask(counts_ref, seq):
    lane = lax.broadcasted_iota(jnp.int32, (1, KEYS), 1)
    own, other = counts_ref[seq], counts_ref[2 + seq]
    return jnp.logical_or(
        lane < own, jnp.logical_and(lane >= HALF_KEYS, lane < HALF_KEYS + other)
    )


def half_only(values, part):
    lane = lax.broadcasted_iota(jnp.int32, values.shape, 1)
    keep = lane < HD if part == 0 else lane >= HD
    return jnp.where(keep, values, jnp.zeros((), values.dtype))


def attend_body(counts, ids, table, query, key_own, key_other, value_own, value_other, *refs):
    out, logs = refs[-2:]
    pair = pl.program_id(0)
    keys = [joint_keys(key_own, key_other, seq) for seq in range(2)]
    values = [joint_keys(value_own, value_other, seq) for seq in range(2)]
    masks = [key_mask(counts, seq) for seq in range(2)]
    lane = lax.broadcasted_iota(jnp.int32, (PAD, 128), 1)
    done = [None, None]
    for part in range(2):
        head = 2 * pair + part
        bias = jnp.concatenate(bias_of(table, ids, head), axis=1)
        for seq in range(2):
            rows = pl.ds(seq * PAD, PAD)
            scores = dot_f32(half_only(query[rows, :], part), keys[seq], NT) * 0.125 + bias
            scores = jnp.where(masks[seq], scores, -1e30)
            top = jnp.max(scores, axis=1, keepdims=True)
            powers = jnp.exp(scores - top)
            total = jnp.sum(powers, axis=1, keepdims=True)
            probs = (powers * (1.0 / total)).astype(BF)
            got = dot_f32(probs, values[seq], NN)
            done[seq] = got if part == 0 else jnp.where(lane < HD, done[seq], got)
            logs[rows, :] = jnp.where(lane == head, top + jnp.log(total), logs[rows, :])
    for seq in range(2):
        out[pl.ds(seq * PAD, PAD), :] = done[seq]


def fixed(shape):
    return pl.BlockSpec(shape, lambda i: (0,) * len(shape))


def by_pair():
    return pl.BlockSpec((2 * PAD, PAIR), lambda i: (0, i))


def attend(counts, ids, table, query, key_own, key_other, value_own, value_other, after):
    return pl.pallas_call(
        attend_body,
        grid=(H // 2,),
        out_shape=(
            jax.ShapeDtypeStruct((2 * PAD, D), F32),
            jax.ShapeDtypeStruct((2 * PAD, 128), F32),
        ),
        in_specs=[pl.BlockSpec(memory_space=pltpu.SMEM), fixed((PAD, KEYS)), fixed((16, 128))]
        + [by_pair()] * 5
        + [pl.BlockSpec(memory_space=pl.ANY)] * len(after),
        out_specs=(by_pair(), fixed((2 * PAD, 128))),
        cost_estimate=LIGHT,
        name="attend",
    )(counts, ids, table, query, key_own, key_other, value_own, value_other, *after)


def attend_back_body(
    base, counts, ids, table, logs, query, key_own, key_other, value_own, value_other, grad, *refs
):
    grad_query, grad_key_own, grad_value_own, grad_key_other, grad_value_other, terms = refs[-6:]
    pair = pl.program_id(0) + base
    keys = [joint_keys(key_own, key_other, seq) for seq in range(2)]
    values = [joint_keys(value_own, value_other, seq) for seq in range(2)]
    masks = [key_mask(counts, seq) for seq in range(2)]
    lane = lax.broadcasted_iota(jnp.int32, (PAD, 128), 1)
    to_query, to_key, to_value = [0.0, 0.0], [0.0, 0.0], [0.0, 0.0]
    for part in range(2):
        head = 2 * pair + part
        bias = jnp.concatenate(bias_of(table, ids, head), axis=1)
        both = 0.0
        for seq in range(2):
            rows = pl.ds(seq * PAD, PAD)
            asked = half_only(query[rows, :], part)
            into = half_only(grad[rows, :], part)
            scores = dot_f32(asked, keys[seq], NT) * 0.125 + bias
            scores = jnp.where(masks[seq], scores, -1e30)
            log = jnp.sum(jnp.where(lane == head, logs[rows, :], 0.0), axis=1, keepdims=True)
            probs = jnp.exp(scores - log)
            grad_probs = dot_f32(into, values[seq], NT)
            mean = jnp.sum(probs * grad_probs, axis=1, keepdims=True)
            grad_scores = (probs * (grad_probs - mean)).astype(BF)
            both = both + grad_scores.astype(F32)
            to_value[seq] = to_value[seq] + dot_f32(probs.astype(BF), into, TN)
            to_query[seq] = to_query[seq] + dot_f32(grad_scores, half_only(keys[seq], part), NN)
            to_key[seq] = to_key[seq] + dot_f32(grad_scores, asked, TN)
        for c in range(KEYS // 128):
            terms[c, pl.ds(head - 2 * base, PAD, stride=8), :] = both[:, c * 128 : (c + 1) * 128]
    for seq in range(2):
        rows = pl.ds(seq * PAD, PAD)
        grad_query[rows, :] = (to_query[seq] * 0.125).astype(BF)
        grad_key_own[rows, :] = to_key[seq][:PAD] * 0.125
        grad_key_other[rows, :] = (to_key[seq][HALF_KEYS : HALF_KEYS + PAD] * 0.125).astype(BF)
        grad_value_own[rows, :] = to_value[seq][:PAD]
        grad_value_other[rows, :] = to_value[seq][HALF_KEYS : HALF_KEYS + PAD].astype(BF)


def attend_back(base, counts, ids, table, logs, query, keys, values, grad, before=(), after=()):
    def rows_of(kind):
        return jax.ShapeDtypeStruct((2 * PAD, D), kind)

    columns = pl.BlockSpec((2 * PAD, PAIR), lambda i: (0, i + base))
    any_ref = pl.BlockSpec(memory_space=pl.ANY)
    return pl.pallas_call(
        functools.partial(attend_back_body, base),
        grid=(H // 4,),
        out_shape=(
            rows_of(BF),
            rows_of(F32),
            rows_of(F32),
            rows_of(BF),
            rows_of(BF),
            jax.ShapeDtypeStruct((KEYS // 128, PAD * 8, 128), F32),
        ),
        in_specs=[
            pl.BlockSpec(memory_space=pltpu.SMEM),
            fixed((PAD, KEYS)),
            fixed((16, 128)),
            fixed((2 * PAD, 128)),
        ]
        + [columns] * 6
        + [any_ref] * (len(before) + len(after)),
        out_specs=(columns,) * 5 + (fixed((KEYS // 128, PAD * 8, 128)),),
        input_output_aliases={10 + i: i for i in range(len(before))},
        cost_estimate=LIGHT,
        name="attend_back",
    )(counts, ids, table, logs, query, *keys, *values, grad, *before, *after)


GROUP = 4


def table_body(ids, early, late, *refs):
    out = refs[-1]
    bucket = lax.broadcasted_iota(jnp.int32, (NB + 1, KEYS), 0)

    def step(index, totals):
        fresh = []
        for lane_group in range(GROUP):
            row = index * GROUP + lane_group
            hot = jnp.where(ids[pl.ds(row, 1), :] == bucket, 1.0, 0.0).astype(BF)
            span = pl.ds(pl.multiple_of(row * 8, 8), 8)
            term = jnp.concatenate(
                [
                    jnp.concatenate([terms[c, span, :] for c in range(KEYS // 128)], axis=1)
                    for terms in (early, late)
                ],
                axis=0,
            )
            high = term.astype(BF)
            low = (term - high.astype(F32)).astype(BF)
            both = jnp.concatenate([high, low], axis=0)
            fresh.append(totals[lane_group] + dot_f32(hot, both, NT))
        return tuple(fresh)

    zero = jnp.zeros((NB + 1, 32), F32)
    totals = lax.fori_loop(0, P_SIZE // GROUP, step, (zero,) * GROUP)
    total = totals[0] + totals[1] + totals[2] + totals[3]
    out[...] = total


def table_grad(ids, terms, after=()):
    whole = pl.BlockSpec(memory_space=pltpu.VMEM)
    both = pl.pallas_call(
        table_body,
        out_shape=jax.ShapeDtypeStruct((NB + 1, 32), F32),
        in_specs=[whole] * 3 + [pl.BlockSpec(memory_space=pl.ANY)] * len(after),
        out_specs=whole,
        cost_estimate=LIGHT,
        name="table_grad",
    )(ids, *terms, *after)
    both = both[:NB, :16] + both[:NB, 16:]
    return jnp.concatenate([both[:, : H // 2], both[:, 8 : 8 + H // 2]], axis=1)


CUT = PHASE_ROWS - 4 * D


def spread_body(half, table, *refs):
    out, held = refs[-2], refs[-1]
    start = 4 * D if half == 0 else 0
    for c in range(D // 128):
        held[...] = table[pl.ds(start, CUT), pl.ds(c * 128, 128)].astype(F32)
        for part in range(4):
            out[:, pl.ds(part * D + c * 128, 128)] = held[
                pl.ds(part, CUT // 4, stride=4), :
            ].astype(BF)


def spread(half, table, before=None):
    whole = pl.BlockSpec(memory_space=pltpu.VMEM)
    extra = () if before is None else (before,)
    return pl.pallas_call(
        functools.partial(spread_body, half),
        grid=(1,),
        out_shape=jax.ShapeDtypeStruct((D, FF), BF),
        in_specs=[whole] + [pl.BlockSpec(memory_space=pl.ANY)] * len(extra),
        out_specs=pl.BlockSpec((CUT // 4, FF), lambda i: (half, 0)),
        scratch_shapes=[pltpu.VMEM((CUT, 128), F32)],
        input_output_aliases={1: 0} if extra else {},
        cost_estimate=LIGHT,
        name="spread",
    )(table, *extra)


def inner_grad_body(share, left, right, out, turned, held):
    chunk = pl.program_id(0)

    @pl.when(chunk == 0)
    def _():
        gap = jnp.zeros((KEYS - 2 * PAD, D), BF)
        turned[...] = jnp.concatenate([left[...], gap], axis=0).T

    gap = jnp.zeros((KEYS - 2 * PAD, 256), BF)
    for part in range(4):
        start = pl.multiple_of(part * D + chunk * 256, 256)
        block = jnp.concatenate([right[:, pl.ds(start, 256)], gap], axis=0)
        value = dot_f32(turned[...], block, NN) * share
        for c in range(2):
            held[c, pl.ds(part, D, stride=4), :] = value[:, c * 128 : (c + 1) * 128]
    out[...] = jnp.concatenate([held[0], held[1]], axis=1).astype(BF)


def inner_grad(left, right, share):
    return pl.pallas_call(
        functools.partial(inner_grad_body, share),
        grid=(D // 256,),
        out_shape=jax.ShapeDtypeStruct((FF, D), BF),
        in_specs=[fixed((2 * PAD, D)), fixed((2 * PAD, FF))],
        out_specs=pl.BlockSpec((FF, 256), lambda i: (0, i)),
        scratch_shapes=[pltpu.VMEM((D, KEYS), BF), pltpu.VMEM((2, FF, 128), F32)],
        cost_estimate=LIGHT,
        name="inner_grad",
    )(left, right)


def from_partner(block, axis, bit):
    count = lax.axis_size(axis)
    route = []
    for low in range(count):
        high = low | 1 << bit
        if high != low and high < count:
            route += [(low, high), (high, low)]
    return lax.ppermute(block, axis, route)


def layer_norm(values, gain, shift):
    center = values - jnp.mean(values, axis=-1, keepdims=True)
    spread = jnp.mean(center * center, axis=-1, keepdims=True)
    return center * lax.rsqrt(spread + 1e-05) * gain + shift


def norm_back(values, gain, shift, grad_after):
    _, pullback = jax.vjp(layer_norm, values, gain, shift)
    return pullback(grad_after)


def matmul(left, right):
    return jnp.dot(left, right, preferred_element_type=jnp.float32)


def matmul_tn(left, right):
    return lax.dot_general(
        left, right, (((0,), (0,)), ((), ())), preferred_element_type=jnp.float32
    )


def matmul_nt(left, right):
    return lax.dot_general(
        left, right, (((1,), (1,)), ((), ())), preferred_element_type=jnp.float32
    )


def exact_gelu(values):
    return jax.nn.gelu(values, approximate=False)


def unpack(flat):
    pairs = [(D, D), (D, D), (D, D), (D, D), (D, FF), (FF, D), (10, D), (3, FF), (NB + 1, H)]
    pieces = []
    offset = 0
    for dims_pair in pairs:
        extent = dims_pair[0] * dims_pair[1]
        pieces.append(flat[offset : offset + extent].reshape(dims_pair))
        offset += extent
    return pieces


def widen(values):
    return jnp.pad(values, ((0, 0), (0, PAD - P_SIZE), (0, 0))).reshape(2 * PAD, D)


def narrow(values):
    return values.reshape(1, 2, PAD, D)[:, :, :P_SIZE]


def on_device(rows, cotangent, master, first_moment, second_moment, average, lengths, buckets):
    side = lax.axis_index("mod")
    place = lax.axis_index("dp")
    fast = lax.axis_size("dp") == DP
    own_copy = master.astype(jnp.bfloat16)
    if fast:
        spot = coords()
        first, second = pack_shard(own_copy, side, place)
        is_last = jnp.logical_and(side == 1, place == DP - 1)
        vec = jnp.where(is_last, own_copy[-EDGE:], jnp.zeros((), BF))
        vec = jnp.pad(vec, (0, D)).reshape(24, D)
        vec, first = lax.optimization_barrier((vec, first))
        vec = sum_all_small(vec)
        first_stack, second = lax.optimization_barrier((gather_z(first), second))
        second_stack = gather_z(second)
        first_near, first_got = gather_near(jnp.stack(first_stack))
        first_got, second_stack[1], second_stack[3] = lax.optimization_barrier(
            (first_got, second_stack[1], second_stack[3])
        )
        first_pieces = gather_far(first_near, first_got)
        second_stack = jnp.stack(second_stack)
        first_table = assemble(0, spot, first_pieces, (second_stack,))
        second_near, second_got = gather_near(second_stack)
        square = [first_table[i * D : (i + 1) * D] for i in range(4)]
        vec_model, vec_inner = vec[:10], vec[10:22].reshape(3, FF)
        head_table = vec[22].reshape(NB + 1, H)
    else:
        weights = unpack(lax.all_gather(own_copy, ("mod", "dp"), axis=0, tiled=True))
        square, (w_inner, w_outer, vec_model, vec_inner, head_table) = weights[:4], weights[4:]
    w_query, w_key, w_value, w_out = square
    model_vec = vec_model.astype(jnp.float32)
    inner_vec = vec_inner.astype(jnp.float32)
    head_vals = head_table.astype(jnp.float32)
    scale_row = jnp.repeat(head_vals[NB], HD)
    table = jnp.pad(head_vals.T, ((0, 16 - H), (0, 128 - NB - 1)))
    full = jnp.full_like(lengths, P_SIZE)
    own_count = jnp.where(side == 0, full, lengths)
    other_count = jnp.where(side == 0, lengths, full)
    counts = jnp.concatenate([own_count, other_count]).astype(jnp.int32)
    slots = jnp.arange(PAD, dtype=jnp.int32)
    own_valid = (slots[None, :] < own_count[:, None]).astype(F32).reshape(2 * PAD, 1)
    near = lax.dynamic_slice(buckets, (side * P_SIZE, side * P_SIZE), (P_SIZE, P_SIZE))
    far = lax.dynamic_slice(buckets, (side * P_SIZE, (1 - side) * P_SIZE), (P_SIZE, P_SIZE))
    room = ((0, PAD - P_SIZE), (0, HALF_KEYS - P_SIZE))
    ids = jnp.concatenate([jnp.pad(near, room), jnp.pad(far, room)], axis=1)

    inputs = widen(rows[0]).astype(F32)
    normed = layer_norm(inputs, model_vec[0], model_vec[1])
    normed_low = normed.astype(BF)
    keys_own = matmul(normed_low, w_key).astype(BF)
    values_own = (matmul(normed_low, w_value) + model_vec[3]).astype(BF)
    keys_other, values_other = from_partner((keys_own, values_own), "mod", 0)
    asking = normed_low
    if fast:
        asking, second_got = lax.optimization_barrier((asking, second_got))
        second_pieces = gather_far(second_near, second_got)
        sent_early = tuple(second_pieces[:2])
    query = (matmul(asking, w_query) + model_vec[2]).astype(BF)
    keys_both, values_both = (keys_own, keys_other), (values_own, values_other)
    sent_early = sent_early if fast else ()
    attended, logs = attend(counts, ids, table, query, *keys_both, *values_both, sent_early)

    if fast:
        w_inner = spread(0, first_table)
        second_table = assemble(1, spot, second_pieces, (attended, w_inner))
        w_inner = spread(1, second_table, w_inner)
        w_outer = second_table[CUT:]
    scaled = attended * scale_row
    mixed = layer_norm(scaled, model_vec[4], model_vec[5])
    mixed_low = mixed.astype(BF)
    middle = inputs + (matmul(mixed_low, w_out) + model_vec[6])
    normed_two = layer_norm(middle, model_vec[7], model_vec[8])
    normed_two_low = normed_two.astype(BF)
    inner = matmul(normed_two_low, w_inner) + inner_vec[0]
    activated = exact_gelu(inner)
    inner_normed = layer_norm(activated, inner_vec[1], inner_vec[2])
    inner_low = inner_normed.astype(BF)

    tokens_all = 2 * rows.shape[1] * P_SIZE * lax.axis_size("dp")
    share = 1.0 / tokens_all

    def weight_grad(left, right):
        value = matmul_tn(left, right) * share
        return value.astype(BF) if fast else value

    grad_out = widen(cotangent[0]).astype(F32) * own_valid
    grad_branch = grad_out.astype(BF)
    grad_w_outer = weight_grad(inner_low, grad_branch)
    grad_b_outer = jnp.sum(grad_branch.astype(F32), axis=0)
    grad_inner_normed = matmul_nt(grad_branch, w_outer)
    grad_activated, grad_gain_ff, grad_shift_ff = norm_back(
        activated, inner_vec[1], inner_vec[2], grad_inner_normed
    )
    _, gelu_pull = jax.vjp(exact_gelu, inner)
    grad_inner_low = gelu_pull(grad_activated)[0].astype(BF)
    if fast:
        grad_w_inner = inner_grad(normed_two_low, grad_inner_low, share)
    else:
        grad_w_inner = weight_grad(normed_two_low, grad_inner_low).reshape(FF, D)
    grad_b_inner = jnp.sum(grad_inner_low.astype(F32), axis=0)
    grad_normed_two = matmul_nt(grad_inner_low, w_inner)
    grad_mid_part, grad_gain_two, grad_shift_two = norm_back(
        middle, model_vec[7], model_vec[8], grad_normed_two
    )
    grad_middle = grad_out + grad_mid_part
    grad_attn_low = grad_middle.astype(BF)
    grad_w_out = weight_grad(mixed_low, grad_attn_low)
    grad_b_out = jnp.sum(grad_attn_low.astype(F32), axis=0)
    grad_mixed = matmul_nt(grad_attn_low, w_out)
    grad_scaled, grad_gain_attn, grad_shift_attn = norm_back(
        scaled, model_vec[4], model_vec[5], grad_mixed
    )
    grad_head_scale = jnp.sum(jnp.sum(grad_scaled * attended, axis=0).reshape(H, HD), axis=1)
    grad_attended = (grad_scaled * scale_row).astype(BF)
    parts = (counts, ids, table, logs, query, keys_both, values_both, grad_attended)
    if fast:
        kept, lent = scatter(1, spot, [None] * 4 + [grad_w_inner, grad_w_outer])
        early = attend_back(0, *parts, after=(kept,))
        got = send_mod(lent)
        late_outs, late_ins = reduce_outs(kept, got), reduce_ins(kept, got)
        late = attend_back(H // 4, *parts, before=early[:5], after=late_outs)
    else:
        early = attend_back(0, *parts)
        late = attend_back(H // 4, *parts, before=early[:5])
    grad_query, key_kept, value_kept, key_sent, value_sent, late_terms = late
    terms = (early[5], late_terms)
    back_keys, back_values = from_partner((key_sent, value_sent), "mod", 0)
    if fast:
        back_keys, back_values, late_sent = lax.optimization_barrier(
            (back_keys, back_values, reduce_sends(late_outs))
        )
    grad_key = (key_kept + back_keys.astype(F32)).astype(BF)
    grad_value = (value_kept + back_values.astype(F32)).astype(BF)
    grad_w_query = weight_grad(normed_low, grad_query)
    grad_w_key = weight_grad(normed_low, grad_key)
    grad_w_value = weight_grad(normed_low, grad_value)
    matrices = [grad_w_query, grad_w_key, grad_w_value, grad_w_out, grad_w_inner, grad_w_outer]
    if fast:
        late_next = reduce_next(late_sent, late_ins)
        kept, lent = scatter(0, spot, matrices, late_next)
        got = send_mod(lent)
        first_outs = reduce_outs(kept, got)
        late_both, late_low = reduce_both(late_sent, late_ins, late_next)
        grad_table = table_grad(ids, terms, first_outs)
        late_turns, first_sent, grad_table = lax.optimization_barrier(
            (reduce_z(late_low), reduce_sends(first_outs), grad_table)
        )
    else:
        grad_table = table_grad(ids, terms)
    result = middle + (matmul(inner_low, w_outer) + model_vec[9])
    result_rows = narrow(result.astype(BF))
    grad_b_query = jnp.sum(grad_query.astype(F32), axis=0)
    grad_b_value = jnp.sum(grad_value.astype(F32), axis=0)
    grad_normed = (
        matmul_nt(grad_query, w_query) + matmul_nt(grad_key, w_key) + matmul_nt(grad_value, w_value)
    )
    grad_in_part, grad_gain_one, grad_shift_one = norm_back(
        inputs, model_vec[0], model_vec[1], grad_normed
    )
    grad_rows = narrow(grad_middle + grad_in_part)
    grad_model_vec = jnp.stack(
        [
            grad_gain_one,
            grad_shift_one,
            grad_b_query,
            grad_b_value,
            grad_gain_attn,
            grad_shift_attn,
            grad_b_out,
            grad_gain_two,
            grad_shift_two,
            grad_b_outer,
        ]
    )
    grad_inner_vec = jnp.stack([grad_b_inner, grad_gain_ff, grad_shift_ff])
    grad_heads = jnp.concatenate([grad_table, grad_head_scale[None, :]], axis=0)
    vec_grad = (
        jnp.concatenate(
            [grad_model_vec, grad_inner_vec.reshape(12, D), grad_heads.reshape(1, D)], axis=0
        )
        * share
    )
    if fast:
        second = reduce_total(late_both, late_turns)
        first_ins = reduce_ins(kept, got)
        first_next = reduce_next(first_sent, first_ins)
        first_both, first_low = reduce_both(first_sent, first_ins, first_next)
        vec_grad, result_rows = lax.optimization_barrier((vec_grad, result_rows))
        vec_grad = sum_z_small(jnp.pad(vec_grad, ((0, 1), (0, 0))))
        vec_grad, first_low = lax.optimization_barrier((vec_grad, first_low))
        first = reduce_total(first_both, reduce_z(first_low))
        vec_grad = sum_rest_small(vec_grad)
        square = jnp.sum(first * first) + jnp.sum(second * second)
        square = square + jnp.where(is_last, jnp.sum(vec_grad * vec_grad), 0.0)
        sent = unpack_sends(first, second, side)
        square_sum, sent = sum_scalar(square, side, place, sent)
        grad_shard = unpack_shard(*sent, vec_grad, side, place)
    else:
        local_grad = jnp.concatenate([part.reshape(-1) for part in matrices + [vec_grad]])
        half_size = local_grad.shape[0] // 2
        own_half = lax.dynamic_slice_in_dim(local_grad, side * half_size, half_size)
        other_half = lax.dynamic_slice_in_dim(local_grad, (1 - side) * half_size, half_size)
        partner_half = from_partner(other_half.astype(BF), "mod", 0).astype(F32)
        grad_shard = lax.psum_scatter(own_half + partner_half, "dp", scatter_dimension=0, tiled=True)
        square_sum = lax.psum(jnp.sum(grad_shard * grad_shard), ("mod", "dp"))
    grad_norm = jnp.sqrt(square_sum)
    clip_scale = jnp.minimum(1.0, 0.25 / (grad_norm + 1e-06))
    clipped = grad_shard * clip_scale
    new_first = 0.5 * first_moment + 0.5 * clipped
    new_second = 0.6 * second_moment + 0.4 * clipped * clipped
    direction = new_first / (1.0 - 0.5**STEP) / (jnp.sqrt(new_second / (1.0 - 0.6**STEP)) + 1e-08)
    new_master = master - 0.04 * (direction + 0.01 * master)
    new_average = 0.5 * average + 0.5 * new_master
    return (
        result_rows,
        grad_rows,
        grad_norm,
        new_master,
        new_first,
        new_second,
        new_average,
        new_master.astype(jnp.bfloat16),
    )


def solution(mesh):
    placed = (
        P("mod", "dp", None, None),
        P("mod", "dp", None, None),
        P(("mod", "dp")),
        P(("mod", "dp")),
        P(("mod", "dp")),
        P(("mod", "dp")),
        P("dp"),
        P(),
    )
    return jax.shard_map(
        on_device,
        mesh=mesh,
        in_specs=placed,
        out_specs=(
            P("mod", "dp", None, None),
            P("mod", "dp", None, None),
            P(),
            P(("mod", "dp")),
            P(("mod", "dp")),
            P(("mod", "dp")),
            P(("mod", "dp")),
            P(("mod", "dp")),
        ),
        check_vma=False,
    )
```

```python
import functools
import jax
import jax.numpy as jnp
from jax import lax
from jax.experimental import pallas as pl
from jax.experimental.pallas import tpu as pltpu
from jax.sharding import PartitionSpec as P

D = 768
H = 12
HD = 64
FF = 3072
NB = 63
P_SIZE = 196
STEP = 5


HALF = D // 2
BLOCK = 144
PHASE_ROWS = 32 * BLOCK
BF = jnp.bfloat16
F32 = jnp.float32
DP = 16
EDGE = 17664
PAD = 208
KEYS = 512
HALF_KEYS = KEYS // 2
PAIR = 2 * HD
LIGHT = pl.CostEstimate(flops=1, bytes_accessed=1, transcendentals=0)


def x_swap():
    return [(i, i ^ 1) for i in range(DP)]


def y_swap():
    return [(i, i ^ 2) for i in range(DP)]


def z_turn(step):
    return [(i, (i // 4 + step) % 4 * 4 + i % 4) for i in range(DP)]


def send_dp(block, route):
    return lax.ppermute(block, "dp", route)


def send_mod(block):
    return lax.ppermute(block, "mod", [(0, 1), (1, 0)])


def pack_shard(own, side, place):
    lead = 8832 * side + 552 * place
    count = BLOCK * D
    lent = lax.dynamic_slice(own, (count - lead,), (count,))
    given = send_mod(lent)
    nxt = [(i, i + 1) for i in range(2 * DP - 1)]
    edge = lax.ppermute(own[own.shape[0] - EDGE :], ("mod", "dp"), nxt)
    kept = lax.dynamic_slice(jnp.concatenate([edge, own[:count]]), (EDGE - lead,), (count,))
    kept = kept.reshape(BLOCK, D)
    given = given.reshape(BLOCK, D)
    return jnp.where(side == 0, kept, given), jnp.where(side == 0, given, kept)


def unpack_sends(first, second, side):
    even = jnp.where(side == 0, first, second).reshape(-1)
    lent = jnp.where(side == 0, second, first)
    odd = send_mod(lent)
    back = [(i + 1, i) for i in range(2 * DP - 1)]
    return even, odd, lax.ppermute(even[:EDGE], ("mod", "dp"), back)


def unpack_shard(even, odd, edge, vec, side, place):
    lead = 8832 * side + 552 * place
    is_last = jnp.logical_and(side == 1, place == DP - 1)
    edge = jnp.where(is_last, vec.reshape(-1)[:EDGE], edge)
    return lax.dynamic_slice(jnp.concatenate([even, odd.reshape(-1), edge]), (lead,), (221736,))


def sum_round(part, routes):
    got = [send_dp(part, route) for route in routes]
    return part + got[0] + got[1] + got[2]


def sum_z_small(part):
    part = part + send_dp(part, z_turn(2))
    return part + send_dp(part, [(i, i ^ 4) for i in range(DP)])


def sum_rest_small(part):
    part = part + send_dp(part, x_swap())
    part = part + send_dp(part, y_swap())
    return part + send_mod(part)


def xy_swap():
    return [(i, i ^ 3) for i in range(DP)]


def sum_scalar(value, side, place, beside):
    slots = lax.broadcasted_iota(jnp.int32, (8, 128), 0) * 128
    slots = slots + lax.broadcasted_iota(jnp.int32, (8, 128), 1)
    own = jnp.where(slots == side * DP + place, value, 0.0)
    for routes in ([z_turn(1), z_turn(2), z_turn(3)], [x_swap(), y_swap(), xy_swap()]):
        got = [send_dp(own, route) for route in routes]
        own = own + got[0] + got[1] + got[2]
        own, beside = lax.optimization_barrier((own, beside))
    return jnp.sum(own + send_mod(own)), beside


def gather_z(block):
    return [block] + [send_dp(block, z_turn(step)) for step in (1, 2, 3)]


def gather_near(stack):
    left, right = stack[:, :, :HALF], stack[:, :, HALF:]
    got = send_dp(left, x_swap()), send_dp(right, y_swap())
    return (left, right), got


def gather_far(near, got):
    left = jnp.stack([near[0], got[0]])
    right = jnp.stack([near[1], got[1]])
    far = send_dp(left, y_swap()), send_dp(right, x_swap())
    mine = [left, right, *far]
    return mine + [send_mod(piece) for piece in mine]


def coords():
    side = lax.axis_index("mod")
    place = lax.axis_index("dp")
    return jnp.stack([side, place // 4, place // 2 % 2, place % 2]).astype(jnp.int32)


def assemble_body(phase, spot, *refs):
    pieces, out, sem = refs[:8], refs[-2], refs[-1]
    side, z, y, x = spot[0], spot[1], spot[2], spot[3]
    copies = []
    for index in range(16):
        other, half, yr, xr = index // 8, index // 4 % 2, index // 2 % 2, index % 2
        owner = side ^ other
        parity = owner if phase == 0 else 1 - owner
        source = pieces[other * 4 + (yr if half == 0 else xr) * 2 + half]
        for turn in range(4):
            home = ((z - turn) & 3) * 4 + (y ^ yr) * 2 + (x ^ xr)
            copies.append(
                pltpu.make_async_copy(
                    source.at[xr if half == 0 else yr, turn],
                    out.at[home * 2 + parity, :, pl.ds(half * HALF, HALF)],
                    sem.at[index * 4 + turn],
                )
            )
    for copy in copies:
        copy.start()
    for copy in copies:
        copy.wait()


def assemble(phase, spot, pieces, after=()):
    return pl.pallas_call(
        functools.partial(assemble_body, phase),
        out_shape=jax.ShapeDtypeStruct((32, BLOCK, D), BF),
        in_specs=[pl.BlockSpec(memory_space=pltpu.SMEM)] + [pl.BlockSpec(memory_space=pl.ANY)] * (8 + len(after)),
        out_specs=pl.BlockSpec(memory_space=pltpu.VMEM),
        scratch_shapes=[pltpu.SemaphoreType.DMA((64,))],
        cost_estimate=LIGHT,
        name="assemble",
    )(spot, *pieces, *after).reshape(PHASE_ROWS, D)


def scatter_body(phase, pieces, spot, *refs):
    sources, kept, lent, sem = refs[:-3], refs[-3], refs[-2], refs[-1]
    side, z, y, x = spot[0], spot[1], spot[2], spot[3]
    copies = []
    for block in range(32):
        home, parity = block // 2, block % 2
        owner = parity if phase == 0 else 1 - parity
        turn = (home // 4 - z) & 3
        yr = (home // 2 % 2) ^ y
        xr = (home % 2) ^ x
        for index, source_row, block_row, count in pieces[block]:
            for half in range(2):
                stay, leave = [
                    pltpu.make_async_copy(
                        sources[index].at[pl.ds(source_row, count), pl.ds(half * HALF, HALF)],
                        target.at[half, yr, xr, turn, pl.ds(block_row, count), :],
                        sem.at[len(copies)],
                    )
                    for target in (kept, lent)
                ]
                pl.when(side == owner)(stay.start)
                pl.when(side != owner)(leave.start)
                copies.append(stay)
    for copy in copies:
        copy.wait()


def scatter(phase, spot, tables, after=()):
    starts = [0]
    for rows in (D, D, D, D, FF, FF):
        starts.append(starts[-1] + rows)
    pieces = []
    for block in range(32):
        low = phase * PHASE_ROWS + block * BLOCK
        parts = []
        for index in range(len(tables)):
            first, last = max(low, starts[index]), min(low + BLOCK, starts[index + 1])
            if first < last:
                parts.append((index, first - starts[index], first - low, last - first))
        pieces.append(parts)
    used = sorted({part[0] for parts in pieces for part in parts})
    pieces = [[(used.index(part[0]),) + part[1:] for part in parts] for parts in pieces]
    count = 2 * sum(len(parts) for parts in pieces)
    return pl.pallas_call(
        functools.partial(scatter_body, phase, pieces),
        out_shape=(jax.ShapeDtypeStruct((2, 2, 2, 4, BLOCK, HALF), BF),) * 2,
        in_specs=[pl.BlockSpec(memory_space=pltpu.SMEM)]
        + [pl.BlockSpec(memory_space=pltpu.VMEM)] * len(used)
        + [pl.BlockSpec(memory_space=pl.ANY)] * len(after),
        out_specs=(pl.BlockSpec(memory_space=pl.ANY),) * 2,
        scratch_shapes=[pltpu.SemaphoreType.DMA((count,))],
        cost_estimate=LIGHT,
        name="scatter",
    )(spot, *[tables[index] for index in used], *after)


def plus(left, right):
    return (left.astype(F32) + right.astype(F32)).astype(BF)


def outs_body(*refs):
    left_mine, left_theirs, right_mine, right_theirs, left, right = refs[:4] + refs[-2:]
    index = pl.program_id(0)

    @pl.when(index < 2)
    def _():
        left[0] = plus(left_mine[0, 0, 0], left_theirs[0, 0, 0])

    @pl.when(index >= 2)
    def _():
        right[0] = plus(right_mine[0, 0, 0], right_theirs[0, 0, 0])


def reduce_outs(mine, theirs, after=()):
    block = (1, 1, 1, 4, BLOCK, HALF)
    left = pl.BlockSpec(block, lambda i: (0, jnp.minimum(i, 1), 1, 0, 0, 0))
    right = pl.BlockSpec(block, lambda i: (1, 1, jnp.maximum(i - 2, 0), 0, 0, 0))
    return pl.pallas_call(
        outs_body,
        grid=(4,),
        out_shape=(jax.ShapeDtypeStruct((2, 4, BLOCK, HALF), BF),) * 2,
        in_specs=[left, left, right, right] + [pl.BlockSpec(memory_space=pl.ANY)] * len(after),
        out_specs=(
            pl.BlockSpec((1, 4, BLOCK, HALF), lambda i: (jnp.minimum(i, 1), 0, 0, 0)),
            pl.BlockSpec((1, 4, BLOCK, HALF), lambda i: (jnp.maximum(i - 2, 0), 0, 0, 0)),
        ),
        cost_estimate=LIGHT,
        name="reduce_outs",
    )(mine, theirs, mine, theirs, *after)


def reduce_sends(outs):
    return send_dp(outs[0], x_swap()), send_dp(outs[1], y_swap())


def reduce_ins(mine, theirs):
    return plus(mine[0, :, 0], theirs[0, :, 0]), plus(mine[1, 0], theirs[1, 0])


def reduce_next(sent, ins):
    left_next = send_dp(plus(ins[0][1], sent[0][1]), y_swap())
    right_next = send_dp(plus(ins[1][1], sent[1][1]), x_swap())
    return left_next, right_next


def reduce_both(sent, ins, nexts):
    left, right = [
        ins[k][0].astype(F32) + sent[k][0].astype(F32) + nexts[k].astype(F32) for k in range(2)
    ]
    both = jnp.concatenate([left, right], axis=-1)
    return both[0], both.astype(BF)


def reduce_z(low):
    return [send_dp(low[step], z_turn(step)) for step in (1, 2, 3)]


def reduce_total(own, turns):
    return own + turns[0].astype(F32) + turns[1].astype(F32) + turns[2].astype(F32)


def dot_f32(left, right, dims):
    return lax.dot_general(left, right, (dims, ((), ())), preferred_element_type=F32)


NN = ((1,), (0,))
NT = ((1,), (1,))
TN = ((0,), (0,))


def bias_of(table_ref, ids_ref, head):
    entry = jnp.broadcast_to(table_ref[pl.ds(head, 1), :], (PAD, 128))
    return [
        jnp.take_along_axis(
            entry, ids_ref[:, c * 128 : (c + 1) * 128], axis=1, mode="promise_in_bounds"
        )
        for c in range(KEYS // 128)
    ]


def joint_keys(own_ref, other_ref, seq):
    rows = pl.ds(seq * PAD, PAD)
    gap = jnp.zeros((HALF_KEYS - PAD, PAIR), BF)
    return jnp.concatenate([own_ref[rows, :], gap, other_ref[rows, :], gap], axis=0)


def key_mask(counts_ref, seq):
    lane = lax.broadcasted_iota(jnp.int32, (1, KEYS), 1)
    own, other = counts_ref[seq], counts_ref[2 + seq]
    return jnp.logical_or(
        lane < own, jnp.logical_and(lane >= HALF_KEYS, lane < HALF_KEYS + other)
    )


def half_only(values, part):
    lane = lax.broadcasted_iota(jnp.int32, values.shape, 1)
    keep = lane < HD if part == 0 else lane >= HD
    return jnp.where(keep, values, jnp.zeros((), values.dtype))


def attend_body(counts, ids, table, query, key_own, key_other, value_own, value_other, *refs):
    out, logs = refs[-2:]
    pair = pl.program_id(0)
    keys = [joint_keys(key_own, key_other, seq) for seq in range(2)]
    values = [joint_keys(value_own, value_other, seq) for seq in range(2)]
    masks = [key_mask(counts, seq) for seq in range(2)]
    lane = lax.broadcasted_iota(jnp.int32, (PAD, 128), 1)
    done = [None, None]
    for part in range(2):
        head = 2 * pair + part
        bias = jnp.concatenate(bias_of(table, ids, head), axis=1)
        for seq in range(2):
            rows = pl.ds(seq * PAD, PAD)
            scores = dot_f32(half_only(query[rows, :], part), keys[seq], NT) * 0.125 + bias
            scores = jnp.where(masks[seq], scores, -1e30)
            top = jnp.max(scores, axis=1, keepdims=True)
            powers = jnp.exp(scores - top)
            total = jnp.sum(powers, axis=1, keepdims=True)
            probs = (powers * (1.0 / total)).astype(BF)
            got = dot_f32(probs, values[seq], NN)
            done[seq] = got if part == 0 else jnp.where(lane < HD, done[seq], got)
            logs[rows, :] = jnp.where(lane == head, top + jnp.log(total), logs[rows, :])
    for seq in range(2):
        out[pl.ds(seq * PAD, PAD), :] = done[seq]


def fixed(shape):
    return pl.BlockSpec(shape, lambda i: (0,) * len(shape))


def by_pair():
    return pl.BlockSpec((2 * PAD, PAIR), lambda i: (0, i))


def attend(counts, ids, table, query, key_own, key_other, value_own, value_other, after):
    return pl.pallas_call(
        attend_body,
        grid=(H // 2,),
        out_shape=(
            jax.ShapeDtypeStruct((2 * PAD, D), F32),
            jax.ShapeDtypeStruct((2 * PAD, 128), F32),
        ),
        in_specs=[pl.BlockSpec(memory_space=pltpu.SMEM), fixed((PAD, KEYS)), fixed((16, 128))]
        + [by_pair()] * 5
        + [pl.BlockSpec(memory_space=pl.ANY)] * len(after),
        out_specs=(by_pair(), fixed((2 * PAD, 128))),
        cost_estimate=LIGHT,
        name="attend",
    )(counts, ids, table, query, key_own, key_other, value_own, value_other, *after)


def attend_back_body(
    base, counts, ids, table, logs, query, key_own, key_other, value_own, value_other, grad, *refs
):
    grad_query, grad_key_own, grad_value_own, grad_key_other, grad_value_other, terms = refs[-6:]
    pair = pl.program_id(0) + base
    keys = [joint_keys(key_own, key_other, seq) for seq in range(2)]
    values = [joint_keys(value_own, value_other, seq) for seq in range(2)]
    masks = [key_mask(counts, seq) for seq in range(2)]
    lane = lax.broadcasted_iota(jnp.int32, (PAD, 128), 1)
    to_query, to_key, to_value = [0.0, 0.0], [0.0, 0.0], [0.0, 0.0]
    for part in range(2):
        head = 2 * pair + part
        bias = jnp.concatenate(bias_of(table, ids, head), axis=1)
        both = 0.0
        for seq in range(2):
            rows = pl.ds(seq * PAD, PAD)
            asked = half_only(query[rows, :], part)
            into = half_only(grad[rows, :], part)
            scores = dot_f32(asked, keys[seq], NT) * 0.125 + bias
            scores = jnp.where(masks[seq], scores, -1e30)
            log = jnp.sum(jnp.where(lane == head, logs[rows, :], 0.0), axis=1, keepdims=True)
            probs = jnp.exp(scores - log)
            grad_probs = dot_f32(into, values[seq], NT)
            mean = jnp.sum(probs * grad_probs, axis=1, keepdims=True)
            grad_scores = (probs * (grad_probs - mean)).astype(BF)
            both = both + grad_scores.astype(F32)
            to_value[seq] = to_value[seq] + dot_f32(probs.astype(BF), into, TN)
            to_query[seq] = to_query[seq] + dot_f32(grad_scores, half_only(keys[seq], part), NN)
            to_key[seq] = to_key[seq] + dot_f32(grad_scores, asked, TN)
        for c in range(KEYS // 128):
            terms[c, pl.ds(head - 2 * base, PAD, stride=8), :] = both[:, c * 128 : (c + 1) * 128]
    for seq in range(2):
        rows = pl.ds(seq * PAD, PAD)
        grad_query[rows, :] = (to_query[seq] * 0.125).astype(BF)
        grad_key_own[rows, :] = to_key[seq][:PAD] * 0.125
        grad_key_other[rows, :] = (to_key[seq][HALF_KEYS : HALF_KEYS + PAD] * 0.125).astype(BF)
        grad_value_own[rows, :] = to_value[seq][:PAD]
        grad_value_other[rows, :] = to_value[seq][HALF_KEYS : HALF_KEYS + PAD].astype(BF)


def attend_back(base, counts, ids, table, logs, query, keys, values, grad, before=(), after=()):
    def rows_of(kind):
        return jax.ShapeDtypeStruct((2 * PAD, D), kind)

    columns = pl.BlockSpec((2 * PAD, PAIR), lambda i: (0, i + base))
    any_ref = pl.BlockSpec(memory_space=pl.ANY)
    return pl.pallas_call(
        functools.partial(attend_back_body, base),
        grid=(H // 4,),
        out_shape=(
            rows_of(BF),
            rows_of(F32),
            rows_of(F32),
            rows_of(BF),
            rows_of(BF),
            jax.ShapeDtypeStruct((KEYS // 128, PAD * 8, 128), F32),
        ),
        in_specs=[
            pl.BlockSpec(memory_space=pltpu.SMEM),
            fixed((PAD, KEYS)),
            fixed((16, 128)),
            fixed((2 * PAD, 128)),
        ]
        + [columns] * 6
        + [any_ref] * (len(before) + len(after)),
        out_specs=(columns,) * 5 + (fixed((KEYS // 128, PAD * 8, 128)),),
        input_output_aliases={10 + i: i for i in range(len(before))},
        cost_estimate=LIGHT,
        name="attend_back",
    )(counts, ids, table, logs, query, *keys, *values, grad, *before, *after)


GROUP = 4


def table_body(ids, early, late, *refs):
    out = refs[-1]
    bucket = lax.broadcasted_iota(jnp.int32, (NB + 1, KEYS), 0)

    def step(index, totals):
        fresh = []
        for lane_group in range(GROUP):
            row = index * GROUP + lane_group
            hot = jnp.where(ids[pl.ds(row, 1), :] == bucket, 1.0, 0.0).astype(BF)
            span = pl.ds(pl.multiple_of(row * 8, 8), 8)
            term = jnp.concatenate(
                [
                    jnp.concatenate([terms[c, span, :] for c in range(KEYS // 128)], axis=1)
                    for terms in (early, late)
                ],
                axis=0,
            )
            high = term.astype(BF)
            low = (term - high.astype(F32)).astype(BF)
            both = jnp.concatenate([high, low], axis=0)
            fresh.append(totals[lane_group] + dot_f32(hot, both, NT))
        return tuple(fresh)

    zero = jnp.zeros((NB + 1, 32), F32)
    totals = lax.fori_loop(0, P_SIZE // GROUP, step, (zero,) * GROUP)
    total = totals[0] + totals[1] + totals[2] + totals[3]
    out[...] = total


def table_grad(ids, terms, after=()):
    whole = pl.BlockSpec(memory_space=pltpu.VMEM)
    both = pl.pallas_call(
        table_body,
        out_shape=jax.ShapeDtypeStruct((NB + 1, 32), F32),
        in_specs=[whole] * 3 + [pl.BlockSpec(memory_space=pl.ANY)] * len(after),
        out_specs=whole,
        cost_estimate=LIGHT,
        name="table_grad",
    )(ids, *terms, *after)
    both = both[:NB, :16] + both[:NB, 16:]
    return jnp.concatenate([both[:, : H // 2], both[:, 8 : 8 + H // 2]], axis=1)


CUT = PHASE_ROWS - 4 * D


def spread_body(half, table, *refs):
    out, held = refs[-2], refs[-1]
    start = 4 * D if half == 0 else 0
    for c in range(D // 128):
        held[...] = table[pl.ds(start, CUT), pl.ds(c * 128, 128)].astype(F32)
        for part in range(4):
            out[:, pl.ds(part * D + c * 128, 128)] = held[
                pl.ds(part, CUT // 4, stride=4), :
            ].astype(BF)


def spread(half, table, before=None):
    whole = pl.BlockSpec(memory_space=pltpu.VMEM)
    extra = () if before is None else (before,)
    return pl.pallas_call(
        functools.partial(spread_body, half),
        grid=(1,),
        out_shape=jax.ShapeDtypeStruct((D, FF), BF),
        in_specs=[whole] + [pl.BlockSpec(memory_space=pl.ANY)] * len(extra),
        out_specs=pl.BlockSpec((CUT // 4, FF), lambda i: (half, 0)),
        scratch_shapes=[pltpu.VMEM((CUT, 128), F32)],
        input_output_aliases={1: 0} if extra else {},
        cost_estimate=LIGHT,
        name="spread",
    )(table, *extra)


def inner_grad_body(share, left, right, out, turned, held):
    chunk = pl.program_id(0)

    @pl.when(chunk == 0)
    def _():
        gap = jnp.zeros((KEYS - 2 * PAD, D), BF)
        turned[...] = jnp.concatenate([left[...], gap], axis=0).T

    gap = jnp.zeros((KEYS - 2 * PAD, 256), BF)
    for part in range(4):
        start = pl.multiple_of(part * D + chunk * 256, 256)
        block = jnp.concatenate([right[:, pl.ds(start, 256)], gap], axis=0)
        value = dot_f32(turned[...], block, NN) * share
        for c in range(2):
            held[c, pl.ds(part, D, stride=4), :] = value[:, c * 128 : (c + 1) * 128]
    out[...] = jnp.concatenate([held[0], held[1]], axis=1).astype(BF)


def inner_grad(left, right, share):
    return pl.pallas_call(
        functools.partial(inner_grad_body, share),
        grid=(D // 256,),
        out_shape=jax.ShapeDtypeStruct((FF, D), BF),
        in_specs=[fixed((2 * PAD, D)), fixed((2 * PAD, FF))],
        out_specs=pl.BlockSpec((FF, 256), lambda i: (0, i)),
        scratch_shapes=[pltpu.VMEM((D, KEYS), BF), pltpu.VMEM((2, FF, 128), F32)],
        cost_estimate=LIGHT,
        name="inner_grad",
    )(left, right)


def from_partner(block, axis, bit):
    count = lax.axis_size(axis)
    route = []
    for low in range(count):
        high = low | 1 << bit
        if high != low and high < count:
            route += [(low, high), (high, low)]
    return lax.ppermute(block, axis, route)


def layer_norm(values, gain, shift):
    center = values - jnp.mean(values, axis=-1, keepdims=True)
    spread = jnp.mean(center * center, axis=-1, keepdims=True)
    return center * lax.rsqrt(spread + 1e-05) * gain + shift


def norm_back(values, gain, shift, grad_after):
    _, pullback = jax.vjp(layer_norm, values, gain, shift)
    return pullback(grad_after)


def matmul(left, right):
    return jnp.dot(left, right, preferred_element_type=jnp.float32)


def matmul_tn(left, right):
    return lax.dot_general(
        left, right, (((0,), (0,)), ((), ())), preferred_element_type=jnp.float32
    )


def matmul_nt(left, right):
    return lax.dot_general(
        left, right, (((1,), (1,)), ((), ())), preferred_element_type=jnp.float32
    )


def exact_gelu(values):
    return jax.nn.gelu(values, approximate=False)


def unpack(flat):
    pairs = [(D, D), (D, D), (D, D), (D, D), (D, FF), (FF, D), (10, D), (3, FF), (NB + 1, H)]
    pieces = []
    offset = 0
    for dims_pair in pairs:
        extent = dims_pair[0] * dims_pair[1]
        pieces.append(flat[offset : offset + extent].reshape(dims_pair))
        offset += extent
    return pieces


def widen(values):
    return jnp.pad(values, ((0, 0), (0, PAD - P_SIZE), (0, 0))).reshape(2 * PAD, D)


def narrow(values):
    return values.reshape(1, 2, PAD, D)[:, :, :P_SIZE]


def on_device(rows, cotangent, master, first_moment, second_moment, average, lengths, buckets):
    side = lax.axis_index("mod")
    place = lax.axis_index("dp")
    fast = lax.axis_size("dp") == DP
    own_copy = master.astype(jnp.bfloat16)
    if fast:
        spot = coords()
        first, second = pack_shard(own_copy, side, place)
        is_last = jnp.logical_and(side == 1, place == DP - 1)
        vec = jnp.where(is_last, own_copy[-EDGE:], jnp.zeros((), BF))
        vec = jnp.pad(vec, (0, D)).reshape(24, D)
        vec = sum_round(vec, [z_turn(1), z_turn(2), z_turn(3)])
        vec = sum_round(vec, [x_swap(), y_swap(), xy_swap()])
        vec, first = lax.optimization_barrier((vec, first))
        vec = vec + send_mod(vec)
        first_stack, second = lax.optimization_barrier((gather_z(first), second))
        second_stack = gather_z(second)
        first_near, first_got = gather_near(jnp.stack(first_stack))
        first_got, second_stack = lax.optimization_barrier((first_got, second_stack))
        first_pieces = gather_far(first_near, first_got)
        second_stack, swapped = lax.optimization_barrier((second_stack, first_pieces[4:6]))
        first_pieces[4:6] = swapped
        second_near, second_got = gather_near(jnp.stack(second_stack))
        first_table = assemble(0, spot, first_pieces)
        square = [first_table[i * D : (i + 1) * D] for i in range(4)]
        vec_model, vec_inner = vec[:10], vec[10:22].reshape(3, FF)
        head_table = vec[22].reshape(NB + 1, H)
    else:
        weights = unpack(lax.all_gather(own_copy, ("mod", "dp"), axis=0, tiled=True))
        square, (w_inner, w_outer, vec_model, vec_inner, head_table) = weights[:4], weights[4:]
    w_query, w_key, w_value, w_out = square
    model_vec = vec_model.astype(jnp.float32)
    inner_vec = vec_inner.astype(jnp.float32)
    head_vals = head_table.astype(jnp.float32)
    scale_row = jnp.repeat(head_vals[NB], HD)
    table = jnp.pad(head_vals.T, ((0, 16 - H), (0, 128 - NB - 1)))
    full = jnp.full_like(lengths, P_SIZE)
    own_count = jnp.where(side == 0, full, lengths)
    other_count = jnp.where(side == 0, lengths, full)
    counts = jnp.concatenate([own_count, other_count]).astype(jnp.int32)
    slots = jnp.arange(PAD, dtype=jnp.int32)
    own_valid = (slots[None, :] < own_count[:, None]).astype(F32).reshape(2 * PAD, 1)
    near = lax.dynamic_slice(buckets, (side * P_SIZE, side * P_SIZE), (P_SIZE, P_SIZE))
    far = lax.dynamic_slice(buckets, (side * P_SIZE, (1 - side) * P_SIZE), (P_SIZE, P_SIZE))
    room = ((0, PAD - P_SIZE), (0, HALF_KEYS - P_SIZE))
    ids = jnp.concatenate([jnp.pad(near, room), jnp.pad(far, room)], axis=1)

    inputs = widen(rows[0]).astype(F32)
    normed = layer_norm(inputs, model_vec[0], model_vec[1])
    normed_low = normed.astype(BF)
    keys_own = matmul(normed_low, w_key).astype(BF)
    values_own = (matmul(normed_low, w_value) + model_vec[3]).astype(BF)
    keys_other, values_other = from_partner((keys_own, values_own), "mod", 0)
    asking = normed_low
    if fast:
        asking, second_got = lax.optimization_barrier((asking, second_got))
        second_pieces = gather_far(second_near, second_got)
        sent_early = tuple(second_pieces[:2])
    query = (matmul(asking, w_query) + model_vec[2]).astype(BF)
    keys_both, values_both = (keys_own, keys_other), (values_own, values_other)
    sent_early = sent_early if fast else ()
    attended, logs = attend(counts, ids, table, query, *keys_both, *values_both, sent_early)

    if fast:
        w_inner = spread(0, first_table)
        second_table = assemble(1, spot, second_pieces, (attended, w_inner))
        w_inner = spread(1, second_table, w_inner)
        w_outer = second_table[CUT:]
    scaled = attended * scale_row
    mixed = layer_norm(scaled, model_vec[4], model_vec[5])
    mixed_low = mixed.astype(BF)
    middle = inputs + (matmul(mixed_low, w_out) + model_vec[6])
    normed_two = layer_norm(middle, model_vec[7], model_vec[8])
    normed_two_low = normed_two.astype(BF)
    inner = matmul(normed_two_low, w_inner) + inner_vec[0]
    activated = exact_gelu(inner)
    inner_normed = layer_norm(activated, inner_vec[1], inner_vec[2])
    inner_low = inner_normed.astype(BF)

    tokens_all = 2 * rows.shape[1] * P_SIZE * lax.axis_size("dp")
    share = 1.0 / tokens_all

    def weight_grad(left, right):
        value = matmul_tn(left, right) * share
        return value.astype(BF) if fast else value

    grad_out = widen(cotangent[0]).astype(F32) * own_valid
    grad_branch = grad_out.astype(BF)
    grad_w_outer = weight_grad(inner_low, grad_branch)
    grad_b_outer = jnp.sum(grad_branch.astype(F32), axis=0)
    grad_inner_normed = matmul_nt(grad_branch, w_outer)
    grad_activated, grad_gain_ff, grad_shift_ff = norm_back(
        activated, inner_vec[1], inner_vec[2], grad_inner_normed
    )
    _, gelu_pull = jax.vjp(exact_gelu, inner)
    grad_inner_low = gelu_pull(grad_activated)[0].astype(BF)
    if fast:
        grad_w_inner = inner_grad(normed_two_low, grad_inner_low, share)
    else:
        grad_w_inner = weight_grad(normed_two_low, grad_inner_low).reshape(FF, D)
    grad_b_inner = jnp.sum(grad_inner_low.astype(F32), axis=0)
    grad_normed_two = matmul_nt(grad_inner_low, w_inner)
    grad_mid_part, grad_gain_two, grad_shift_two = norm_back(
        middle, model_vec[7], model_vec[8], grad_normed_two
    )
    grad_middle = grad_out + grad_mid_part
    grad_attn_low = grad_middle.astype(BF)
    grad_w_out = weight_grad(mixed_low, grad_attn_low)
    grad_b_out = jnp.sum(grad_attn_low.astype(F32), axis=0)
    grad_mixed = matmul_nt(grad_attn_low, w_out)
    grad_scaled, grad_gain_attn, grad_shift_attn = norm_back(
        scaled, model_vec[4], model_vec[5], grad_mixed
    )
    grad_head_scale = jnp.sum(jnp.sum(grad_scaled * attended, axis=0).reshape(H, HD), axis=1)
    grad_attended = (grad_scaled * scale_row).astype(BF)
    parts = (counts, ids, table, logs, query, keys_both, values_both, grad_attended)
    if fast:
        kept, lent = scatter(1, spot, [None] * 4 + [grad_w_inner, grad_w_outer])
        early = attend_back(0, *parts, after=(kept,))
        got = send_mod(lent)
        late_outs, late_ins = reduce_outs(kept, got), reduce_ins(kept, got)
        late = attend_back(H // 4, *parts, before=early[:5], after=late_outs)
    else:
        early = attend_back(0, *parts)
        late = attend_back(H // 4, *parts, before=early[:5])
    grad_query, key_kept, value_kept, key_sent, value_sent, late_terms = late
    terms = (early[5], late_terms)
    back_keys, back_values = from_partner((key_sent, value_sent), "mod", 0)
    if fast:
        back_keys, back_values, late_sent = lax.optimization_barrier(
            (back_keys, back_values, reduce_sends(late_outs))
        )
    grad_key = (key_kept + back_keys.astype(F32)).astype(BF)
    grad_value = (value_kept + back_values.astype(F32)).astype(BF)
    grad_w_query = weight_grad(normed_low, grad_query)
    grad_w_key = weight_grad(normed_low, grad_key)
    grad_w_value = weight_grad(normed_low, grad_value)
    matrices = [grad_w_query, grad_w_key, grad_w_value, grad_w_out, grad_w_inner, grad_w_outer]
    if fast:
        late_next = reduce_next(late_sent, late_ins)
        kept, lent = scatter(0, spot, matrices, late_next)
        got = send_mod(lent)
        first_outs = reduce_outs(kept, got)
        late_both, late_low = reduce_both(late_sent, late_ins, late_next)
        grad_table = table_grad(ids, terms, first_outs)
        late_turns, first_sent, grad_table = lax.optimization_barrier(
            (reduce_z(late_low), reduce_sends(first_outs), grad_table)
        )
    else:
        grad_table = table_grad(ids, terms)
    if fast:
        inner_low, grad_query, grad_key, grad_value, _ = lax.optimization_barrier(
            (inner_low, grad_query, grad_key, grad_value, first_outs)
        )
    result = middle + (matmul(inner_low, w_outer) + model_vec[9])
    result_rows = narrow(result.astype(BF))
    grad_b_query = jnp.sum(grad_query.astype(F32), axis=0)
    grad_b_value = jnp.sum(grad_value.astype(F32), axis=0)
    grad_normed = (
        matmul_nt(grad_query, w_query) + matmul_nt(grad_key, w_key) + matmul_nt(grad_value, w_value)
    )
    grad_in_part, grad_gain_one, grad_shift_one = norm_back(
        inputs, model_vec[0], model_vec[1], grad_normed
    )
    grad_rows = narrow(grad_middle + grad_in_part)
    grad_model_vec = jnp.stack(
        [
            grad_gain_one,
            grad_shift_one,
            grad_b_query,
            grad_b_value,
            grad_gain_attn,
            grad_shift_attn,
            grad_b_out,
            grad_gain_two,
            grad_shift_two,
            grad_b_outer,
        ]
    )
    grad_inner_vec = jnp.stack([grad_b_inner, grad_gain_ff, grad_shift_ff])
    grad_heads = jnp.concatenate([grad_table, grad_head_scale[None, :]], axis=0)
    vec_grad = (
        jnp.concatenate(
            [grad_model_vec, grad_inner_vec.reshape(12, D), grad_heads.reshape(1, D)], axis=0
        )
        * share
    )
    if fast:
        second = reduce_total(late_both, late_turns)
        first_ins = reduce_ins(kept, got)
        first_next = reduce_next(first_sent, first_ins)
        first_both, first_low = reduce_both(first_sent, first_ins, first_next)
        vec_grad, result_rows = lax.optimization_barrier((vec_grad, result_rows))
        vec_grad = sum_z_small(jnp.pad(vec_grad, ((0, 1), (0, 0))))
        vec_grad, first_low = lax.optimization_barrier((vec_grad, first_low))
        first = reduce_total(first_both, reduce_z(first_low))
        vec_grad = sum_rest_small(vec_grad)
        square = jnp.sum(first * first) + jnp.sum(second * second)
        square = square + jnp.where(is_last, jnp.sum(vec_grad * vec_grad), 0.0)
        first, second, square = lax.optimization_barrier((first, second, square))
        sent = unpack_sends(first, second, side)
        square_sum, sent = sum_scalar(square, side, place, sent)
        grad_shard = unpack_shard(*sent, vec_grad, side, place)
    else:
        local_grad = jnp.concatenate([part.reshape(-1) for part in matrices + [vec_grad]])
        half_size = local_grad.shape[0] // 2
        own_half = lax.dynamic_slice_in_dim(local_grad, side * half_size, half_size)
        other_half = lax.dynamic_slice_in_dim(local_grad, (1 - side) * half_size, half_size)
        partner_half = from_partner(other_half.astype(BF), "mod", 0).astype(F32)
        grad_shard = lax.psum_scatter(own_half + partner_half, "dp", scatter_dimension=0, tiled=True)
        square_sum = lax.psum(jnp.sum(grad_shard * grad_shard), ("mod", "dp"))
    grad_norm = jnp.sqrt(square_sum)
    clip_scale = jnp.minimum(1.0, 0.25 / (grad_norm + 1e-06))
    clipped = grad_shard * clip_scale
    new_first = 0.5 * first_moment + 0.5 * clipped
    new_second = 0.6 * second_moment + 0.4 * clipped * clipped
    direction = new_first / (1.0 - 0.5**STEP) / (jnp.sqrt(new_second / (1.0 - 0.6**STEP)) + 1e-08)
    new_master = master - 0.04 * (direction + 0.01 * master)
    new_average = 0.5 * average + 0.5 * new_master
    return (
        result_rows,
        grad_rows,
        grad_norm,
        new_master,
        new_first,
        new_second,
        new_average,
        new_master.astype(jnp.bfloat16),
    )


def solution(mesh):
    placed = (
        P("mod", "dp", None, None),
        P("mod", "dp", None, None),
        P(("mod", "dp")),
        P(("mod", "dp")),
        P(("mod", "dp")),
        P(("mod", "dp")),
        P("dp"),
        P(),
    )
    return jax.shard_map(
        on_device,
        mesh=mesh,
        in_specs=placed,
        out_specs=(
            P("mod", "dp", None, None),
            P("mod", "dp", None, None),
            P(),
            P(("mod", "dp")),
            P(("mod", "dp")),
            P(("mod", "dp")),
            P(("mod", "dp")),
            P(("mod", "dp")),
        ),
        check_vma=False,
    )
```

```python
import functools
import jax
import jax.numpy as jnp
from jax import lax
from jax.experimental import pallas as pl
from jax.experimental.pallas import tpu as pltpu
from jax.sharding import PartitionSpec as P

D = 768
H = 12
HD = 64
FF = 3072
NB = 63
P_SIZE = 196
STEP = 5


HALF = D // 2
BLOCK = 144
PHASE_ROWS = 32 * BLOCK
BF = jnp.bfloat16
F32 = jnp.float32
DP = 16
EDGE = 17664
PAD = 208
KEYS = 512
HALF_KEYS = KEYS // 2
PAIR = 2 * HD
LIGHT = pl.CostEstimate(flops=1, bytes_accessed=1, transcendentals=0)


def x_swap():
    return [(i, i ^ 1) for i in range(DP)]


def y_swap():
    return [(i, i ^ 2) for i in range(DP)]


def z_turn(step):
    return [(i, (i // 4 + step) % 4 * 4 + i % 4) for i in range(DP)]


def send_dp(block, route):
    return lax.ppermute(block, "dp", route)


def send_mod(block):
    return lax.ppermute(block, "mod", [(0, 1), (1, 0)])


def pack_shard(own, side, place):
    lead = 8832 * side + 552 * place
    count = BLOCK * D
    lent = lax.dynamic_slice(own, (count - lead,), (count,))
    given = send_mod(lent)
    nxt = [(i, i + 1) for i in range(2 * DP - 1)]
    edge = lax.ppermute(own[own.shape[0] - EDGE :], ("mod", "dp"), nxt)
    kept = lax.dynamic_slice(jnp.concatenate([edge, own[:count]]), (EDGE - lead,), (count,))
    kept = kept.reshape(BLOCK, D)
    given = given.reshape(BLOCK, D)
    return jnp.where(side == 0, kept, given), jnp.where(side == 0, given, kept)


def unpack_sends(first, second, side):
    even = jnp.where(side == 0, first, second).reshape(-1)
    lent = jnp.where(side == 0, second, first)
    odd = send_mod(lent)
    back = [(i + 1, i) for i in range(2 * DP - 1)]
    return even, odd, lax.ppermute(even[:EDGE], ("mod", "dp"), back)


def unpack_shard(even, odd, edge, vec, side, place):
    lead = 8832 * side + 552 * place
    is_last = jnp.logical_and(side == 1, place == DP - 1)
    edge = jnp.where(is_last, vec.reshape(-1)[:EDGE], edge)
    return lax.dynamic_slice(jnp.concatenate([even, odd.reshape(-1), edge]), (lead,), (221736,))


def sum_round(part, routes):
    got = [send_dp(part, route) for route in routes]
    return part + got[0] + got[1] + got[2]


def sum_z_small(part):
    part = part + send_dp(part, z_turn(2))
    return part + send_dp(part, [(i, i ^ 4) for i in range(DP)])


def sum_rest_small(part):
    part = part + send_dp(part, x_swap())
    part = part + send_dp(part, y_swap())
    return part + send_mod(part)


def xy_swap():
    return [(i, i ^ 3) for i in range(DP)]


def sum_scalar(value, side, place, beside):
    slots = lax.broadcasted_iota(jnp.int32, (8, 128), 0) * 128
    slots = slots + lax.broadcasted_iota(jnp.int32, (8, 128), 1)
    own = jnp.where(slots == side * DP + place, value, 0.0)
    for routes in ([z_turn(1), z_turn(2), z_turn(3)], [x_swap(), y_swap(), xy_swap()]):
        got = [send_dp(own, route) for route in routes]
        own = own + got[0] + got[1] + got[2]
        own, beside = lax.optimization_barrier((own, beside))
    return jnp.sum(own + send_mod(own)), beside


def gather_z(block):
    return [block] + [send_dp(block, z_turn(step)) for step in (1, 2, 3)]


def gather_near(stack):
    left, right = stack[:, :, :HALF], stack[:, :, HALF:]
    got = send_dp(left, x_swap()), send_dp(right, y_swap())
    return (left, right), got


def gather_far(near, got):
    left = jnp.stack([near[0], got[0]])
    right = jnp.stack([near[1], got[1]])
    return left, right, send_dp(left, y_swap()), send_dp(right, x_swap())


def coords():
    side = lax.axis_index("mod")
    place = lax.axis_index("dp")
    return jnp.stack([side, place // 4, place // 2 % 2, place % 2]).astype(jnp.int32)


def assemble_body(phase, spot, *refs):
    pieces, out, sem = refs[:8], refs[-2], refs[-1]
    side, z, y, x = spot[0], spot[1], spot[2], spot[3]
    copies = []
    for index in range(16):
        other, half, yr, xr = index // 8, index // 4 % 2, index // 2 % 2, index % 2
        owner = side ^ other
        parity = owner if phase == 0 else 1 - owner
        source = pieces[other * 4 + (yr if half == 0 else xr) * 2 + half]
        for turn in range(4):
            home = ((z - turn) & 3) * 4 + (y ^ yr) * 2 + (x ^ xr)
            copies.append(
                pltpu.make_async_copy(
                    source.at[xr if half == 0 else yr, turn],
                    out.at[home * 2 + parity, :, pl.ds(half * HALF, HALF)],
                    sem.at[index * 4 + turn],
                )
            )
    for copy in copies:
        copy.start()
    for copy in copies:
        copy.wait()


def assemble(phase, spot, pieces, after=()):
    return pl.pallas_call(
        functools.partial(assemble_body, phase),
        out_shape=jax.ShapeDtypeStruct((32, BLOCK, D), BF),
        in_specs=[pl.BlockSpec(memory_space=pltpu.SMEM)] + [pl.BlockSpec(memory_space=pl.ANY)] * (8 + len(after)),
        out_specs=pl.BlockSpec(memory_space=pltpu.VMEM),
        scratch_shapes=[pltpu.SemaphoreType.DMA((64,))],
        cost_estimate=LIGHT,
        name="assemble",
    )(spot, *pieces, *after).reshape(PHASE_ROWS, D)


def scatter_body(phase, pieces, spot, *refs):
    sources, kept, lent, sem = refs[:-3], refs[-3], refs[-2], refs[-1]
    side, z, y, x = spot[0], spot[1], spot[2], spot[3]
    copies = []
    for block in range(32):
        home, parity = block // 2, block % 2
        owner = parity if phase == 0 else 1 - parity
        turn = (home // 4 - z) & 3
        yr = (home // 2 % 2) ^ y
        xr = (home % 2) ^ x
        for index, source_row, block_row, count in pieces[block]:
            for half in range(2):
                stay, leave = [
                    pltpu.make_async_copy(
                        sources[index].at[pl.ds(source_row, count), pl.ds(half * HALF, HALF)],
                        target.at[half, yr, xr, turn, pl.ds(block_row, count), :],
                        sem.at[len(copies)],
                    )
                    for target in (kept, lent)
                ]
                pl.when(side == owner)(stay.start)
                pl.when(side != owner)(leave.start)
                copies.append(stay)
    for copy in copies:
        copy.wait()


def scatter(phase, spot, tables, after=()):
    starts = [0]
    for rows in (D, D, D, D, FF, FF):
        starts.append(starts[-1] + rows)
    pieces = []
    for block in range(32):
        low = phase * PHASE_ROWS + block * BLOCK
        parts = []
        for index in range(len(tables)):
            first, last = max(low, starts[index]), min(low + BLOCK, starts[index + 1])
            if first < last:
                parts.append((index, first - starts[index], first - low, last - first))
        pieces.append(parts)
    used = sorted({part[0] for parts in pieces for part in parts})
    pieces = [[(used.index(part[0]),) + part[1:] for part in parts] for parts in pieces]
    count = 2 * sum(len(parts) for parts in pieces)
    return pl.pallas_call(
        functools.partial(scatter_body, phase, pieces),
        out_shape=(jax.ShapeDtypeStruct((2, 2, 2, 4, BLOCK, HALF), BF),) * 2,
        in_specs=[pl.BlockSpec(memory_space=pltpu.SMEM)]
        + [pl.BlockSpec(memory_space=pltpu.VMEM)] * len(used)
        + [pl.BlockSpec(memory_space=pl.ANY)] * len(after),
        out_specs=(pl.BlockSpec(memory_space=pl.ANY),) * 2,
        scratch_shapes=[pltpu.SemaphoreType.DMA((count,))],
        cost_estimate=LIGHT,
        name="scatter",
    )(spot, *[tables[index] for index in used], *after)


def plus(left, right):
    return (left.astype(F32) + right.astype(F32)).astype(BF)


def outs_body(*refs):
    left_mine, left_theirs, right_mine, right_theirs, left, right = refs[:4] + refs[-2:]
    index = pl.program_id(0)

    @pl.when(index < 2)
    def _():
        left[0] = plus(left_mine[0, 0, 0], left_theirs[0, 0, 0])

    @pl.when(index >= 2)
    def _():
        right[0] = plus(right_mine[0, 0, 0], right_theirs[0, 0, 0])


def reduce_outs(mine, theirs, after=()):
    block = (1, 1, 1, 4, BLOCK, HALF)
    left = pl.BlockSpec(block, lambda i: (0, jnp.minimum(i, 1), 1, 0, 0, 0))
    right = pl.BlockSpec(block, lambda i: (1, 1, jnp.maximum(i - 2, 0), 0, 0, 0))
    return pl.pallas_call(
        outs_body,
        grid=(4,),
        out_shape=(jax.ShapeDtypeStruct((2, 4, BLOCK, HALF), BF),) * 2,
        in_specs=[left, left, right, right] + [pl.BlockSpec(memory_space=pl.ANY)] * len(after),
        out_specs=(
            pl.BlockSpec((1, 4, BLOCK, HALF), lambda i: (jnp.minimum(i, 1), 0, 0, 0)),
            pl.BlockSpec((1, 4, BLOCK, HALF), lambda i: (jnp.maximum(i - 2, 0), 0, 0, 0)),
        ),
        cost_estimate=LIGHT,
        name="reduce_outs",
    )(mine, theirs, mine, theirs, *after)


def reduce_sends(outs):
    return send_dp(outs[0], x_swap()), send_dp(outs[1], y_swap())


def reduce_ins(mine, theirs):
    return plus(mine[0, :, 0], theirs[0, :, 0]), plus(mine[1, 0], theirs[1, 0])


def reduce_next(sent, ins):
    left_next = send_dp(plus(ins[0][1], sent[0][1]), y_swap())
    right_next = send_dp(plus(ins[1][1], sent[1][1]), x_swap())
    return left_next, right_next


def reduce_both(sent, ins, nexts):
    left, right = [
        ins[k][0].astype(F32) + sent[k][0].astype(F32) + nexts[k].astype(F32) for k in range(2)
    ]
    both = jnp.concatenate([left, right], axis=-1)
    return both[0], both.astype(BF)


def reduce_z(low):
    return [send_dp(low[step], z_turn(step)) for step in (1, 2, 3)]


def reduce_total(own, turns):
    return own + turns[0].astype(F32) + turns[1].astype(F32) + turns[2].astype(F32)


def dot_f32(left, right, dims):
    return lax.dot_general(left, right, (dims, ((), ())), preferred_element_type=F32)


NN = ((1,), (0,))
NT = ((1,), (1,))
TN = ((0,), (0,))


def bias_of(table_ref, ids_ref, head):
    entry = jnp.broadcast_to(table_ref[pl.ds(head, 1), :], (PAD, 128))
    return [
        jnp.take_along_axis(
            entry, ids_ref[:, c * 128 : (c + 1) * 128], axis=1, mode="promise_in_bounds"
        )
        for c in range(KEYS // 128)
    ]


def joint_keys(own_ref, other_ref, seq):
    rows = pl.ds(seq * PAD, PAD)
    gap = jnp.zeros((HALF_KEYS - PAD, PAIR), BF)
    return jnp.concatenate([own_ref[rows, :], gap, other_ref[rows, :], gap], axis=0)


def key_mask(counts_ref, seq):
    lane = lax.broadcasted_iota(jnp.int32, (1, KEYS), 1)
    own, other = counts_ref[seq], counts_ref[2 + seq]
    return jnp.logical_or(
        lane < own, jnp.logical_and(lane >= HALF_KEYS, lane < HALF_KEYS + other)
    )


def half_only(values, part):
    lane = lax.broadcasted_iota(jnp.int32, values.shape, 1)
    keep = lane < HD if part == 0 else lane >= HD
    return jnp.where(keep, values, jnp.zeros((), values.dtype))


def attend_body(counts, ids, table, query, key_own, key_other, value_own, value_other, *refs):
    out, logs = refs[-2:]
    pair = pl.program_id(0)
    keys = [joint_keys(key_own, key_other, seq) for seq in range(2)]
    values = [joint_keys(value_own, value_other, seq) for seq in range(2)]
    masks = [key_mask(counts, seq) for seq in range(2)]
    lane = lax.broadcasted_iota(jnp.int32, (PAD, 128), 1)
    done = [None, None]
    for part in range(2):
        head = 2 * pair + part
        bias = jnp.concatenate(bias_of(table, ids, head), axis=1)
        for seq in range(2):
            rows = pl.ds(seq * PAD, PAD)
            scores = dot_f32(half_only(query[rows, :], part), keys[seq], NT) * 0.125 + bias
            scores = jnp.where(masks[seq], scores, -1e30)
            top = jnp.max(scores, axis=1, keepdims=True)
            powers = jnp.exp(scores - top)
            total = jnp.sum(powers, axis=1, keepdims=True)
            probs = (powers * (1.0 / total)).astype(BF)
            got = dot_f32(probs, values[seq], NN)
            done[seq] = got if part == 0 else jnp.where(lane < HD, done[seq], got)
            logs[rows, :] = jnp.where(lane == head, top + jnp.log(total), logs[rows, :])
    for seq in range(2):
        out[pl.ds(seq * PAD, PAD), :] = done[seq]


def fixed(shape):
    return pl.BlockSpec(shape, lambda i: (0,) * len(shape))


def by_pair():
    return pl.BlockSpec((2 * PAD, PAIR), lambda i: (0, i))


def attend(counts, ids, table, query, key_own, key_other, value_own, value_other, after):
    return pl.pallas_call(
        attend_body,
        grid=(H // 2,),
        out_shape=(
            jax.ShapeDtypeStruct((2 * PAD, D), F32),
            jax.ShapeDtypeStruct((2 * PAD, 128), F32),
        ),
        in_specs=[pl.BlockSpec(memory_space=pltpu.SMEM), fixed((PAD, KEYS)), fixed((16, 128))]
        + [by_pair()] * 5
        + [pl.BlockSpec(memory_space=pl.ANY)] * len(after),
        out_specs=(by_pair(), fixed((2 * PAD, 128))),
        cost_estimate=LIGHT,
        name="attend",
    )(counts, ids, table, query, key_own, key_other, value_own, value_other, *after)


def attend_back_body(
    base, counts, ids, table, logs, query, key_own, key_other, value_own, value_other, grad, *refs
):
    grad_query, grad_key_own, grad_value_own, grad_key_other, grad_value_other, terms = refs[-6:]
    pair = pl.program_id(0) + base
    keys = [joint_keys(key_own, key_other, seq) for seq in range(2)]
    values = [joint_keys(value_own, value_other, seq) for seq in range(2)]
    masks = [key_mask(counts, seq) for seq in range(2)]
    lane = lax.broadcasted_iota(jnp.int32, (PAD, 128), 1)
    to_query, to_key, to_value = [0.0, 0.0], [0.0, 0.0], [0.0, 0.0]
    for part in range(2):
        head = 2 * pair + part
        bias = jnp.concatenate(bias_of(table, ids, head), axis=1)
        both = 0.0
        for seq in range(2):
            rows = pl.ds(seq * PAD, PAD)
            asked = half_only(query[rows, :], part)
            into = half_only(grad[rows, :], part)
            scores = dot_f32(asked, keys[seq], NT) * 0.125 + bias
            scores = jnp.where(masks[seq], scores, -1e30)
            log = jnp.sum(jnp.where(lane == head, logs[rows, :], 0.0), axis=1, keepdims=True)
            probs = jnp.exp(scores - log)
            grad_probs = dot_f32(into, values[seq], NT)
            mean = jnp.sum(probs * grad_probs, axis=1, keepdims=True)
            grad_scores = (probs * (grad_probs - mean)).astype(BF)
            both = both + grad_scores.astype(F32)
            to_value[seq] = to_value[seq] + dot_f32(probs.astype(BF), into, TN)
            to_query[seq] = to_query[seq] + dot_f32(grad_scores, half_only(keys[seq], part), NN)
            to_key[seq] = to_key[seq] + dot_f32(grad_scores, asked, TN)
        for c in range(KEYS // 128):
            terms[c, pl.ds(head - 2 * base, PAD, stride=8), :] = both[:, c * 128 : (c + 1) * 128]
    for seq in range(2):
        rows = pl.ds(seq * PAD, PAD)
        grad_query[rows, :] = (to_query[seq] * 0.125).astype(BF)
        grad_key_own[rows, :] = to_key[seq][:PAD] * 0.125
        grad_key_other[rows, :] = (to_key[seq][HALF_KEYS : HALF_KEYS + PAD] * 0.125).astype(BF)
        grad_value_own[rows, :] = to_value[seq][:PAD]
        grad_value_other[rows, :] = to_value[seq][HALF_KEYS : HALF_KEYS + PAD].astype(BF)


def attend_back(base, counts, ids, table, logs, query, keys, values, grad, before=(), after=()):
    def rows_of(kind):
        return jax.ShapeDtypeStruct((2 * PAD, D), kind)

    columns = pl.BlockSpec((2 * PAD, PAIR), lambda i: (0, i + base))
    any_ref = pl.BlockSpec(memory_space=pl.ANY)
    return pl.pallas_call(
        functools.partial(attend_back_body, base),
        grid=(H // 4,),
        out_shape=(
            rows_of(BF),
            rows_of(F32),
            rows_of(F32),
            rows_of(BF),
            rows_of(BF),
            jax.ShapeDtypeStruct((KEYS // 128, PAD * 8, 128), F32),
        ),
        in_specs=[
            pl.BlockSpec(memory_space=pltpu.SMEM),
            fixed((PAD, KEYS)),
            fixed((16, 128)),
            fixed((2 * PAD, 128)),
        ]
        + [columns] * 6
        + [any_ref] * (len(before) + len(after)),
        out_specs=(columns,) * 5 + (fixed((KEYS // 128, PAD * 8, 128)),),
        input_output_aliases={10 + i: i for i in range(len(before))},
        cost_estimate=LIGHT,
        name="attend_back",
    )(counts, ids, table, logs, query, *keys, *values, grad, *before, *after)


GROUP = 4


def table_body(ids, early, late, *refs):
    out = refs[-1]
    bucket = lax.broadcasted_iota(jnp.int32, (NB + 1, KEYS), 0)

    def step(index, totals):
        fresh = []
        for lane_group in range(GROUP):
            row = index * GROUP + lane_group
            hot = jnp.where(ids[pl.ds(row, 1), :] == bucket, 1.0, 0.0).astype(BF)
            span = pl.ds(pl.multiple_of(row * 8, 8), 8)
            term = jnp.concatenate(
                [
                    jnp.concatenate([terms[c, span, :] for c in range(KEYS // 128)], axis=1)
                    for terms in (early, late)
                ],
                axis=0,
            )
            high = term.astype(BF)
            low = (term - high.astype(F32)).astype(BF)
            both = jnp.concatenate([high, low], axis=0)
            fresh.append(totals[lane_group] + dot_f32(hot, both, NT))
        return tuple(fresh)

    zero = jnp.zeros((NB + 1, 32), F32)
    totals = lax.fori_loop(0, P_SIZE // GROUP, step, (zero,) * GROUP)
    total = totals[0] + totals[1] + totals[2] + totals[3]
    out[...] = total


def table_grad(ids, terms, after=()):
    whole = pl.BlockSpec(memory_space=pltpu.VMEM)
    both = pl.pallas_call(
        table_body,
        out_shape=jax.ShapeDtypeStruct((NB + 1, 32), F32),
        in_specs=[whole] * 3 + [pl.BlockSpec(memory_space=pl.ANY)] * len(after),
        out_specs=whole,
        cost_estimate=LIGHT,
        name="table_grad",
    )(ids, *terms, *after)
    both = both[:NB, :16] + both[:NB, 16:]
    return jnp.concatenate([both[:, : H // 2], both[:, 8 : 8 + H // 2]], axis=1)


CUT = PHASE_ROWS - 4 * D


def spread_body(half, table, *refs):
    out, held = refs[-2], refs[-1]
    start = 4 * D if half == 0 else 0
    for c in range(D // 128):
        held[...] = table[pl.ds(start, CUT), pl.ds(c * 128, 128)].astype(F32)
        for part in range(4):
            out[:, pl.ds(part * D + c * 128, 128)] = held[
                pl.ds(part, CUT // 4, stride=4), :
            ].astype(BF)


def spread(half, table, before=None):
    whole = pl.BlockSpec(memory_space=pltpu.VMEM)
    extra = () if before is None else (before,)
    return pl.pallas_call(
        functools.partial(spread_body, half),
        grid=(1,),
        out_shape=jax.ShapeDtypeStruct((D, FF), BF),
        in_specs=[whole] + [pl.BlockSpec(memory_space=pl.ANY)] * len(extra),
        out_specs=pl.BlockSpec((CUT // 4, FF), lambda i: (half, 0)),
        scratch_shapes=[pltpu.VMEM((CUT, 128), F32)],
        input_output_aliases={1: 0} if extra else {},
        cost_estimate=LIGHT,
        name="spread",
    )(table, *extra)


def inner_grad_body(share, left, right, out, turned, held):
    chunk = pl.program_id(0)

    @pl.when(chunk == 0)
    def _():
        gap = jnp.zeros((KEYS - 2 * PAD, D), BF)
        turned[...] = jnp.concatenate([left[...], gap], axis=0).T

    gap = jnp.zeros((KEYS - 2 * PAD, 256), BF)
    for part in range(4):
        start = pl.multiple_of(part * D + chunk * 256, 256)
        block = jnp.concatenate([right[:, pl.ds(start, 256)], gap], axis=0)
        value = dot_f32(turned[...], block, NN) * share
        for c in range(2):
            held[c, pl.ds(part, D, stride=4), :] = value[:, c * 128 : (c + 1) * 128]
    out[...] = jnp.concatenate([held[0], held[1]], axis=1).astype(BF)


def inner_grad(left, right, share):
    return pl.pallas_call(
        functools.partial(inner_grad_body, share),
        grid=(D // 256,),
        out_shape=jax.ShapeDtypeStruct((FF, D), BF),
        in_specs=[fixed((2 * PAD, D)), fixed((2 * PAD, FF))],
        out_specs=pl.BlockSpec((FF, 256), lambda i: (0, i)),
        scratch_shapes=[pltpu.VMEM((D, KEYS), BF), pltpu.VMEM((2, FF, 128), F32)],
        cost_estimate=LIGHT,
        name="inner_grad",
    )(left, right)


def from_partner(block, axis, bit):
    count = lax.axis_size(axis)
    route = []
    for low in range(count):
        high = low | 1 << bit
        if high != low and high < count:
            route += [(low, high), (high, low)]
    return lax.ppermute(block, axis, route)


def layer_norm(values, gain, shift):
    center = values - jnp.mean(values, axis=-1, keepdims=True)
    spread = jnp.mean(center * center, axis=-1, keepdims=True)
    return center * lax.rsqrt(spread + 1e-05) * gain + shift


def norm_back(values, gain, shift, grad_after):
    _, pullback = jax.vjp(layer_norm, values, gain, shift)
    return pullback(grad_after)


def matmul(left, right):
    return jnp.dot(left, right, preferred_element_type=jnp.float32)


def matmul_tn(left, right):
    return lax.dot_general(
        left, right, (((0,), (0,)), ((), ())), preferred_element_type=jnp.float32
    )


def matmul_nt(left, right):
    return lax.dot_general(
        left, right, (((1,), (1,)), ((), ())), preferred_element_type=jnp.float32
    )


def exact_gelu(values):
    return jax.nn.gelu(values, approximate=False)


def unpack(flat):
    pairs = [(D, D), (D, D), (D, D), (D, D), (D, FF), (FF, D), (10, D), (3, FF), (NB + 1, H)]
    pieces = []
    offset = 0
    for dims_pair in pairs:
        extent = dims_pair[0] * dims_pair[1]
        pieces.append(flat[offset : offset + extent].reshape(dims_pair))
        offset += extent
    return pieces


def widen(values):
    return jnp.pad(values, ((0, 0), (0, PAD - P_SIZE), (0, 0))).reshape(2 * PAD, D)


def narrow(values):
    return values.reshape(1, 2, PAD, D)[:, :, :P_SIZE]


def on_device(rows, cotangent, master, first_moment, second_moment, average, lengths, buckets):
    side = lax.axis_index("mod")
    place = lax.axis_index("dp")
    fast = lax.axis_size("dp") == DP
    own_copy = master.astype(jnp.bfloat16)
    if fast:
        spot = coords()
        first, second = pack_shard(own_copy, side, place)
        is_last = jnp.logical_and(side == 1, place == DP - 1)
        vec = jnp.where(is_last, own_copy[-EDGE:], jnp.zeros((), BF))
        vec = jnp.pad(vec, (0, D)).reshape(24, D)
        vec = sum_round(vec, [z_turn(1), z_turn(2), z_turn(3)])
        vec, first = lax.optimization_barrier((vec, first))
        vec = sum_round(vec, [x_swap(), y_swap(), xy_swap()])
        vec, first_stack, second = lax.optimization_barrier((vec, gather_z(first), second))
        vec = vec + send_mod(vec)
        second_stack = gather_z(second)
        first_pieces = gather_far(*gather_near(jnp.stack(first_stack)))
        near_pieces, second_stack = lax.optimization_barrier((first_pieces[:2], second_stack))
        swapped = [send_mod(piece) for piece in near_pieces]
        second_stack, swapped = lax.optimization_barrier((second_stack, swapped))
        swapped += [send_mod(piece) for piece in first_pieces[2:]]
        second_near, second_got = gather_near(jnp.stack(second_stack))
        first_table = assemble(0, spot, [*first_pieces, *swapped])
        _, second_near, second_got = lax.optimization_barrier(
            (first_table, second_near, second_got)
        )
        second_pieces = gather_far(second_near, second_got)
        second_pieces = [*second_pieces, *[send_mod(piece) for piece in second_pieces]]
        square = [first_table[i * D : (i + 1) * D] for i in range(4)]
        vec_model, vec_inner = vec[:10], vec[10:22].reshape(3, FF)
        head_table = vec[22].reshape(NB + 1, H)
    else:
        weights = unpack(lax.all_gather(own_copy, ("mod", "dp"), axis=0, tiled=True))
        square, (w_inner, w_outer, vec_model, vec_inner, head_table) = weights[:4], weights[4:]
    w_query, w_key, w_value, w_out = square
    model_vec = vec_model.astype(jnp.float32)
    inner_vec = vec_inner.astype(jnp.float32)
    head_vals = head_table.astype(jnp.float32)
    scale_row = jnp.repeat(head_vals[NB], HD)
    table = jnp.pad(head_vals.T, ((0, 16 - H), (0, 128 - NB - 1)))
    full = jnp.full_like(lengths, P_SIZE)
    own_count = jnp.where(side == 0, full, lengths)
    other_count = jnp.where(side == 0, lengths, full)
    counts = jnp.concatenate([own_count, other_count]).astype(jnp.int32)
    slots = jnp.arange(PAD, dtype=jnp.int32)
    own_valid = (slots[None, :] < own_count[:, None]).astype(F32).reshape(2 * PAD, 1)
    near = lax.dynamic_slice(buckets, (side * P_SIZE, side * P_SIZE), (P_SIZE, P_SIZE))
    far = lax.dynamic_slice(buckets, (side * P_SIZE, (1 - side) * P_SIZE), (P_SIZE, P_SIZE))
    room = ((0, PAD - P_SIZE), (0, HALF_KEYS - P_SIZE))
    ids = jnp.concatenate([jnp.pad(near, room), jnp.pad(far, room)], axis=1)

    inputs = widen(rows[0]).astype(F32)
    normed = layer_norm(inputs, model_vec[0], model_vec[1])
    normed_low = normed.astype(BF)
    keys_own = matmul(normed_low, w_key).astype(BF)
    values_own = (matmul(normed_low, w_value) + model_vec[3]).astype(BF)
    keys_other, values_other = from_partner((keys_own, values_own), "mod", 0)
    if fast:
        sent_early = tuple(second_pieces[:2])
    query = (matmul(normed_low, w_query) + model_vec[2]).astype(BF)
    keys_both, values_both = (keys_own, keys_other), (values_own, values_other)
    sent_early = sent_early if fast else ()
    attended, logs = attend(counts, ids, table, query, *keys_both, *values_both, sent_early)

    if fast:
        w_inner = spread(0, first_table)
        second_table = assemble(1, spot, second_pieces, (attended, w_inner))
        w_inner = spread(1, second_table, w_inner)
        w_outer = second_table[CUT:]
    scaled = attended * scale_row
    mixed = layer_norm(scaled, model_vec[4], model_vec[5])
    mixed_low = mixed.astype(BF)
    middle = inputs + (matmul(mixed_low, w_out) + model_vec[6])
    normed_two = layer_norm(middle, model_vec[7], model_vec[8])
    normed_two_low = normed_two.astype(BF)
    inner = matmul(normed_two_low, w_inner) + inner_vec[0]
    activated = exact_gelu(inner)
    inner_normed = layer_norm(activated, inner_vec[1], inner_vec[2])
    inner_low = inner_normed.astype(BF)

    tokens_all = 2 * rows.shape[1] * P_SIZE * lax.axis_size("dp")
    share = 1.0 / tokens_all

    def weight_grad(left, right):
        value = matmul_tn(left, right) * share
        return value.astype(BF) if fast else value

    grad_out = widen(cotangent[0]).astype(F32) * own_valid
    grad_branch = grad_out.astype(BF)
    grad_w_outer = weight_grad(inner_low, grad_branch)
    grad_b_outer = jnp.sum(grad_branch.astype(F32), axis=0)
    grad_inner_normed = matmul_nt(grad_branch, w_outer)
    grad_activated, grad_gain_ff, grad_shift_ff = norm_back(
        activated, inner_vec[1], inner_vec[2], grad_inner_normed
    )
    _, gelu_pull = jax.vjp(exact_gelu, inner)
    grad_inner_low = gelu_pull(grad_activated)[0].astype(BF)
    if fast:
        grad_w_inner = inner_grad(normed_two_low, grad_inner_low, share)
    else:
        grad_w_inner = weight_grad(normed_two_low, grad_inner_low).reshape(FF, D)
    grad_b_inner = jnp.sum(grad_inner_low.astype(F32), axis=0)
    grad_normed_two = matmul_nt(grad_inner_low, w_inner)
    grad_mid_part, grad_gain_two, grad_shift_two = norm_back(
        middle, model_vec[7], model_vec[8], grad_normed_two
    )
    grad_middle = grad_out + grad_mid_part
    grad_attn_low = grad_middle.astype(BF)
    grad_w_out = weight_grad(mixed_low, grad_attn_low)
    grad_b_out = jnp.sum(grad_attn_low.astype(F32), axis=0)
    grad_mixed = matmul_nt(grad_attn_low, w_out)
    grad_scaled, grad_gain_attn, grad_shift_attn = norm_back(
        scaled, model_vec[4], model_vec[5], grad_mixed
    )
    grad_head_scale = jnp.sum(jnp.sum(grad_scaled * attended, axis=0).reshape(H, HD), axis=1)
    grad_attended = (grad_scaled * scale_row).astype(BF)
    parts = (counts, ids, table, logs, query, keys_both, values_both, grad_attended)
    if fast:
        kept, lent = scatter(1, spot, [None] * 4 + [grad_w_inner, grad_w_outer])
        early = attend_back(0, *parts, after=(kept,))
        got = send_mod(lent)
        late_outs, late_ins = reduce_outs(kept, got), reduce_ins(kept, got)
        late = attend_back(H // 4, *parts, before=early[:5], after=late_outs)
    else:
        early = attend_back(0, *parts)
        late = attend_back(H // 4, *parts, before=early[:5])
    grad_query, key_kept, value_kept, key_sent, value_sent, late_terms = late
    terms = (early[5], late_terms)
    back_keys, back_values = from_partner((key_sent, value_sent), "mod", 0)
    if fast:
        back_keys, back_values, late_sent = lax.optimization_barrier(
            (back_keys, back_values, reduce_sends(late_outs))
        )
    grad_key = (key_kept + back_keys.astype(F32)).astype(BF)
    grad_value = (value_kept + back_values.astype(F32)).astype(BF)
    grad_w_query = weight_grad(normed_low, grad_query)
    grad_w_key = weight_grad(normed_low, grad_key)
    grad_w_value = weight_grad(normed_low, grad_value)
    matrices = [grad_w_query, grad_w_key, grad_w_value, grad_w_out, grad_w_inner, grad_w_outer]
    if fast:
        late_next = reduce_next(late_sent, late_ins)
        kept, lent = scatter(0, spot, matrices, late_next)
        got = send_mod(lent)
        first_outs = reduce_outs(kept, got)
        late_both, late_low = reduce_both(late_sent, late_ins, late_next)
        grad_table = table_grad(ids, terms, first_outs)
        late_turns, first_sent, grad_table = lax.optimization_barrier(
            (reduce_z(late_low), reduce_sends(first_outs), grad_table)
        )
    else:
        grad_table = table_grad(ids, terms)
    if fast:
        inner_low, grad_query, grad_key, grad_value, _ = lax.optimization_barrier(
            (inner_low, grad_query, grad_key, grad_value, first_outs)
        )
    result = middle + (matmul(inner_low, w_outer) + model_vec[9])
    result_rows = narrow(result.astype(BF))
    grad_b_query = jnp.sum(grad_query.astype(F32), axis=0)
    grad_b_value = jnp.sum(grad_value.astype(F32), axis=0)
    grad_normed = (
        matmul_nt(grad_query, w_query) + matmul_nt(grad_key, w_key) + matmul_nt(grad_value, w_value)
    )
    grad_in_part, grad_gain_one, grad_shift_one = norm_back(
        inputs, model_vec[0], model_vec[1], grad_normed
    )
    grad_rows = narrow(grad_middle + grad_in_part)
    grad_model_vec = jnp.stack(
        [
            grad_gain_one,
            grad_shift_one,
            grad_b_query,
            grad_b_value,
            grad_gain_attn,
            grad_shift_attn,
            grad_b_out,
            grad_gain_two,
            grad_shift_two,
            grad_b_outer,
        ]
    )
    grad_inner_vec = jnp.stack([grad_b_inner, grad_gain_ff, grad_shift_ff])
    grad_heads = jnp.concatenate([grad_table, grad_head_scale[None, :]], axis=0)
    vec_grad = (
        jnp.concatenate(
            [grad_model_vec, grad_inner_vec.reshape(12, D), grad_heads.reshape(1, D)], axis=0
        )
        * share
    )
    if fast:
        second = reduce_total(late_both, late_turns)
        first_ins = reduce_ins(kept, got)
        first_next = reduce_next(first_sent, first_ins)
        first_both, first_low = reduce_both(first_sent, first_ins, first_next)
        vec_grad, result_rows = lax.optimization_barrier((vec_grad, result_rows))
        vec_grad = sum_z_small(jnp.pad(vec_grad, ((0, 1), (0, 0))))
        vec_grad, first_low = lax.optimization_barrier((vec_grad, first_low))
        first = reduce_total(first_both, reduce_z(first_low))
        vec_grad = sum_rest_small(vec_grad)
        square = jnp.sum(first * first) + jnp.sum(second * second)
        square = square + jnp.where(is_last, jnp.sum(vec_grad * vec_grad), 0.0)
        first, second, square = lax.optimization_barrier((first, second, square))
        sent = unpack_sends(first, second, side)
        square_sum, sent = sum_scalar(square, side, place, sent)
        grad_shard = unpack_shard(*sent, vec_grad, side, place)
    else:
        local_grad = jnp.concatenate([part.reshape(-1) for part in matrices + [vec_grad]])
        half_size = local_grad.shape[0] // 2
        own_half = lax.dynamic_slice_in_dim(local_grad, side * half_size, half_size)
        other_half = lax.dynamic_slice_in_dim(local_grad, (1 - side) * half_size, half_size)
        partner_half = from_partner(other_half.astype(BF), "mod", 0).astype(F32)
        grad_shard = lax.psum_scatter(own_half + partner_half, "dp", scatter_dimension=0, tiled=True)
        square_sum = lax.psum(jnp.sum(grad_shard * grad_shard), ("mod", "dp"))
    grad_norm = jnp.sqrt(square_sum)
    clip_scale = jnp.minimum(1.0, 0.25 / (grad_norm + 1e-06))
    clipped = grad_shard * clip_scale
    new_first = 0.5 * first_moment + 0.5 * clipped
    new_second = 0.6 * second_moment + 0.4 * clipped * clipped
    direction = new_first / (1.0 - 0.5**STEP) / (jnp.sqrt(new_second / (1.0 - 0.6**STEP)) + 1e-08)
    new_master = master - 0.04 * (direction + 0.01 * master)
    new_average = 0.5 * average + 0.5 * new_master
    return (
        result_rows,
        grad_rows,
        grad_norm,
        new_master,
        new_first,
        new_second,
        new_average,
        new_master.astype(jnp.bfloat16),
    )


def solution(mesh):
    placed = (
        P("mod", "dp", None, None),
        P("mod", "dp", None, None),
        P(("mod", "dp")),
        P(("mod", "dp")),
        P(("mod", "dp")),
        P(("mod", "dp")),
        P("dp"),
        P(),
    )
    return jax.shard_map(
        on_device,
        mesh=mesh,
        in_specs=placed,
        out_specs=(
            P("mod", "dp", None, None),
            P("mod", "dp", None, None),
            P(),
            P(("mod", "dp")),
            P(("mod", "dp")),
            P(("mod", "dp")),
            P(("mod", "dp")),
            P(("mod", "dp")),
        ),
        check_vma=False,
    )
```

```python
import functools
import jax
import jax.numpy as jnp
from jax import lax
from jax.experimental import pallas as pl
from jax.experimental.pallas import tpu as pltpu
from jax.sharding import PartitionSpec as P

D = 768
H = 12
HD = 64
FF = 3072
NB = 63
P_SIZE = 196
STEP = 5


HALF = D // 2
BLOCK = 144
PHASE_ROWS = 32 * BLOCK
BF = jnp.bfloat16
F32 = jnp.float32
DP = 16
EDGE = 17664
PAD = 208
KEYS = 512
HALF_KEYS = KEYS // 2
PAIR = 2 * HD
LIGHT = pl.CostEstimate(flops=1, bytes_accessed=1, transcendentals=0)


def x_swap():
    return [(i, i ^ 1) for i in range(DP)]


def y_swap():
    return [(i, i ^ 2) for i in range(DP)]


def z_turn(step):
    return [(i, (i // 4 + step) % 4 * 4 + i % 4) for i in range(DP)]


def send_dp(block, route):
    return lax.ppermute(block, "dp", route)


def send_mod(block):
    return lax.ppermute(block, "mod", [(0, 1), (1, 0)])


def pack_shard(own, side, place):
    lead = 8832 * side + 552 * place
    count = BLOCK * D
    lent = lax.dynamic_slice(own, (count - lead,), (count,))
    given = send_mod(lent)
    nxt = [(i, i + 1) for i in range(2 * DP - 1)]
    edge = lax.ppermute(own[own.shape[0] - EDGE :], ("mod", "dp"), nxt)
    kept = lax.dynamic_slice(jnp.concatenate([edge, own[:count]]), (EDGE - lead,), (count,))
    kept = kept.reshape(BLOCK, D)
    given = given.reshape(BLOCK, D)
    return jnp.where(side == 0, kept, given), jnp.where(side == 0, given, kept)


def unpack_sends(first, second, side):
    even = jnp.where(side == 0, first, second).reshape(-1)
    lent = jnp.where(side == 0, second, first)
    odd = send_mod(lent)
    back = [(i + 1, i) for i in range(2 * DP - 1)]
    return even, odd, lax.ppermute(even[:EDGE], ("mod", "dp"), back)


def unpack_shard(even, odd, edge, vec, side, place):
    lead = 8832 * side + 552 * place
    is_last = jnp.logical_and(side == 1, place == DP - 1)
    edge = jnp.where(is_last, vec.reshape(-1)[:EDGE], edge)
    return lax.dynamic_slice(jnp.concatenate([even, odd.reshape(-1), edge]), (lead,), (221736,))


def sum_z_small(part):
    part = part + send_dp(part, z_turn(2))
    return part + send_dp(part, [(i, i ^ 4) for i in range(DP)])


def sum_rest_small(part):
    part = part + send_dp(part, x_swap())
    part = part + send_dp(part, y_swap())
    return part + send_mod(part)


def xy_swap():
    return [(i, i ^ 3) for i in range(DP)]


def sum_scalar(value, side, place, beside):
    slots = lax.broadcasted_iota(jnp.int32, (8, 128), 0) * 128
    slots = slots + lax.broadcasted_iota(jnp.int32, (8, 128), 1)
    own = jnp.where(slots == side * DP + place, value, 0.0)
    for routes in ([z_turn(1), z_turn(2), z_turn(3)], [x_swap(), y_swap(), xy_swap()]):
        got = [send_dp(own, route) for route in routes]
        own = own + got[0] + got[1] + got[2]
        own, beside = lax.optimization_barrier((own, beside))
    return jnp.sum(own + send_mod(own)), beside


def gather_z(block):
    return [block] + [send_dp(block, z_turn(step)) for step in (1, 2, 3)]


def gather_near(stack):
    left, right = stack[:, :, :HALF], stack[:, :, HALF:]
    got = send_dp(left, x_swap()), send_dp(right, y_swap())
    return (left, right), got


def gather_far(near, got):
    left = jnp.stack([near[0], got[0]])
    right = jnp.stack([near[1], got[1]])
    return left, right, send_dp(left, y_swap()), send_dp(right, x_swap())


def coords():
    side = lax.axis_index("mod")
    place = lax.axis_index("dp")
    return jnp.stack([side, place // 4, place // 2 % 2, place % 2]).astype(jnp.int32)


def assemble_body(phase, spot, *refs):
    pieces, out, sem = refs[:8], refs[-2], refs[-1]
    side, z, y, x = spot[0], spot[1], spot[2], spot[3]
    copies = []
    for index in range(16):
        other, half, yr, xr = index // 8, index // 4 % 2, index // 2 % 2, index % 2
        owner = side ^ other
        parity = owner if phase == 0 else 1 - owner
        source = pieces[other * 4 + (yr if half == 0 else xr) * 2 + half]
        for turn in range(4):
            home = ((z - turn) & 3) * 4 + (y ^ yr) * 2 + (x ^ xr)
            copies.append(
                pltpu.make_async_copy(
                    source.at[xr if half == 0 else yr, turn, pl.ds(0, BLOCK), :],
                    out.at[home * 2 + parity, :, pl.ds(half * HALF, HALF)],
                    sem.at[index * 4 + turn],
                )
            )
    for copy in copies:
        copy.start()
    for copy in copies:
        copy.wait()


def assemble(phase, spot, pieces, after=()):
    return pl.pallas_call(
        functools.partial(assemble_body, phase),
        out_shape=jax.ShapeDtypeStruct((32, BLOCK, D), BF),
        in_specs=[pl.BlockSpec(memory_space=pltpu.SMEM)] + [pl.BlockSpec(memory_space=pl.ANY)] * (8 + len(after)),
        out_specs=pl.BlockSpec(memory_space=pltpu.VMEM),
        scratch_shapes=[pltpu.SemaphoreType.DMA((64,))],
        cost_estimate=LIGHT,
        name="assemble",
    )(spot, *pieces, *after).reshape(PHASE_ROWS, D)


def scatter_body(phase, pieces, spot, *refs):
    sources, kept, lent, sem = refs[:-3], refs[-3], refs[-2], refs[-1]
    side, z, y, x = spot[0], spot[1], spot[2], spot[3]
    copies = []
    for block in range(32):
        home, parity = block // 2, block % 2
        owner = parity if phase == 0 else 1 - parity
        turn = (home // 4 - z) & 3
        yr = (home // 2 % 2) ^ y
        xr = (home % 2) ^ x
        for index, source_row, block_row, count in pieces[block]:
            for half in range(2):
                stay, leave = [
                    pltpu.make_async_copy(
                        sources[index].at[pl.ds(source_row, count), pl.ds(half * HALF, HALF)],
                        target.at[half, yr, xr, turn, pl.ds(block_row, count), :],
                        sem.at[len(copies)],
                    )
                    for target in (kept, lent)
                ]
                pl.when(side == owner)(stay.start)
                pl.when(side != owner)(leave.start)
                copies.append(stay)
    for copy in copies:
        copy.wait()


def scatter(phase, spot, tables, after=()):
    starts = [0]
    for rows in (D, D, D, D, FF, FF):
        starts.append(starts[-1] + rows)
    pieces = []
    for block in range(32):
        low = phase * PHASE_ROWS + block * BLOCK
        parts = []
        for index in range(len(tables)):
            first, last = max(low, starts[index]), min(low + BLOCK, starts[index + 1])
            if first < last:
                parts.append((index, first - starts[index], first - low, last - first))
        pieces.append(parts)
    used = sorted({part[0] for parts in pieces for part in parts})
    pieces = [[(used.index(part[0]),) + part[1:] for part in parts] for parts in pieces]
    count = 2 * sum(len(parts) for parts in pieces)
    return pl.pallas_call(
        functools.partial(scatter_body, phase, pieces),
        out_shape=(jax.ShapeDtypeStruct((2, 2, 2, 4, BLOCK, HALF), BF),) * 2,
        in_specs=[pl.BlockSpec(memory_space=pltpu.SMEM)]
        + [pl.BlockSpec(memory_space=pltpu.VMEM)] * len(used)
        + [pl.BlockSpec(memory_space=pl.ANY)] * len(after),
        out_specs=(pl.BlockSpec(memory_space=pl.ANY),) * 2,
        scratch_shapes=[pltpu.SemaphoreType.DMA((count,))],
        cost_estimate=LIGHT,
        name="scatter",
    )(spot, *[tables[index] for index in used], *after)


def plus(left, right):
    return (left.astype(F32) + right.astype(F32)).astype(BF)


def outs_body(*refs):
    left_mine, left_theirs, right_mine, right_theirs, left, right = refs[:4] + refs[-2:]
    index = pl.program_id(0)

    @pl.when(index < 2)
    def _():
        left[0] = plus(left_mine[0, 0, 0], left_theirs[0, 0, 0])

    @pl.when(index >= 2)
    def _():
        right[0] = plus(right_mine[0, 0, 0], right_theirs[0, 0, 0])


def reduce_outs(mine, theirs, after=()):
    block = (1, 1, 1, 4, BLOCK, HALF)
    left = pl.BlockSpec(block, lambda i: (0, jnp.minimum(i, 1), 1, 0, 0, 0))
    right = pl.BlockSpec(block, lambda i: (1, 1, jnp.maximum(i - 2, 0), 0, 0, 0))
    return pl.pallas_call(
        outs_body,
        grid=(4,),
        out_shape=(jax.ShapeDtypeStruct((2, 4, BLOCK, HALF), BF),) * 2,
        in_specs=[left, left, right, right] + [pl.BlockSpec(memory_space=pl.ANY)] * len(after),
        out_specs=(
            pl.BlockSpec((1, 4, BLOCK, HALF), lambda i: (jnp.minimum(i, 1), 0, 0, 0)),
            pl.BlockSpec((1, 4, BLOCK, HALF), lambda i: (jnp.maximum(i - 2, 0), 0, 0, 0)),
        ),
        cost_estimate=LIGHT,
        name="reduce_outs",
    )(mine, theirs, mine, theirs, *after)


def reduce_sends(outs):
    return send_dp(outs[0], x_swap()), send_dp(outs[1], y_swap())


def reduce_ins(mine, theirs):
    return plus(mine[0, :, 0], theirs[0, :, 0]), plus(mine[1, 0], theirs[1, 0])


def reduce_next(sent, ins):
    left_next = send_dp(plus(ins[0][1], sent[0][1]), y_swap())
    right_next = send_dp(plus(ins[1][1], sent[1][1]), x_swap())
    return left_next, right_next


def reduce_both(sent, ins, nexts):
    left, right = [
        ins[k][0].astype(F32) + sent[k][0].astype(F32) + nexts[k].astype(F32) for k in range(2)
    ]
    both = jnp.concatenate([left, right], axis=-1)
    return both[0], both.astype(BF)


def reduce_z(low):
    return [send_dp(low[step], z_turn(step)) for step in (1, 2, 3)]


def reduce_total(own, turns):
    return own + turns[0].astype(F32) + turns[1].astype(F32) + turns[2].astype(F32)


def dot_f32(left, right, dims):
    return lax.dot_general(left, right, (dims, ((), ())), preferred_element_type=F32)


NN = ((1,), (0,))
NT = ((1,), (1,))
TN = ((0,), (0,))


def bias_of(table_ref, ids_ref, head):
    entry = jnp.broadcast_to(table_ref[pl.ds(head, 1), :], (PAD, 128))
    return [
        jnp.take_along_axis(
            entry, ids_ref[:, c * 128 : (c + 1) * 128], axis=1, mode="promise_in_bounds"
        )
        for c in range(KEYS // 128)
    ]


def joint_keys(own_ref, other_ref, seq):
    rows = pl.ds(seq * PAD, PAD)
    gap = jnp.zeros((HALF_KEYS - PAD, PAIR), BF)
    return jnp.concatenate([own_ref[rows, :], gap, other_ref[rows, :], gap], axis=0)


def key_mask(counts_ref, seq):
    lane = lax.broadcasted_iota(jnp.int32, (1, KEYS), 1)
    own, other = counts_ref[seq], counts_ref[2 + seq]
    return jnp.logical_or(
        lane < own, jnp.logical_and(lane >= HALF_KEYS, lane < HALF_KEYS + other)
    )


def half_only(values, part):
    lane = lax.broadcasted_iota(jnp.int32, values.shape, 1)
    keep = lane < HD if part == 0 else lane >= HD
    return jnp.where(keep, values, jnp.zeros((), values.dtype))


def attend_body(counts, ids, table, query, key_own, key_other, value_own, value_other, *refs):
    out, logs = refs[-2:]
    pair = pl.program_id(0)
    keys = [joint_keys(key_own, key_other, seq) for seq in range(2)]
    values = [joint_keys(value_own, value_other, seq) for seq in range(2)]
    masks = [key_mask(counts, seq) for seq in range(2)]
    lane = lax.broadcasted_iota(jnp.int32, (PAD, 128), 1)
    done = [None, None]
    for part in range(2):
        head = 2 * pair + part
        bias = jnp.concatenate(bias_of(table, ids, head), axis=1)
        for seq in range(2):
            rows = pl.ds(seq * PAD, PAD)
            scores = dot_f32(half_only(query[rows, :], part), keys[seq], NT) * 0.125 + bias
            scores = jnp.where(masks[seq], scores, -1e30)
            top = jnp.max(scores, axis=1, keepdims=True)
            powers = jnp.exp(scores - top)
            total = jnp.sum(powers, axis=1, keepdims=True)
            probs = (powers * (1.0 / total)).astype(BF)
            got = dot_f32(probs, values[seq], NN)
            done[seq] = got if part == 0 else jnp.where(lane < HD, done[seq], got)
            logs[rows, :] = jnp.where(lane == head, top + jnp.log(total), logs[rows, :])
    for seq in range(2):
        out[pl.ds(seq * PAD, PAD), :] = done[seq]


def fixed(shape):
    return pl.BlockSpec(shape, lambda i: (0,) * len(shape))


def by_pair():
    return pl.BlockSpec((2 * PAD, PAIR), lambda i: (0, i))


def attend(counts, ids, table, query, key_own, key_other, value_own, value_other, after):
    return pl.pallas_call(
        attend_body,
        grid=(H // 2,),
        out_shape=(
            jax.ShapeDtypeStruct((2 * PAD, D), F32),
            jax.ShapeDtypeStruct((2 * PAD, 128), F32),
        ),
        in_specs=[pl.BlockSpec(memory_space=pltpu.SMEM), fixed((PAD, KEYS)), fixed((16, 128))]
        + [by_pair()] * 5
        + [pl.BlockSpec(memory_space=pl.ANY)] * len(after),
        out_specs=(by_pair(), fixed((2 * PAD, 128))),
        cost_estimate=LIGHT,
        name="attend",
    )(counts, ids, table, query, key_own, key_other, value_own, value_other, *after)


def attend_back_body(
    base, counts, ids, table, logs, query, key_own, key_other, value_own, value_other, grad, *refs
):
    grad_query, grad_key_own, grad_value_own, grad_key_other, grad_value_other, terms = refs[-6:]
    pair = pl.program_id(0) + base
    keys = [joint_keys(key_own, key_other, seq) for seq in range(2)]
    values = [joint_keys(value_own, value_other, seq) for seq in range(2)]
    masks = [key_mask(counts, seq) for seq in range(2)]
    lane = lax.broadcasted_iota(jnp.int32, (PAD, 128), 1)
    to_query, to_key, to_value = [0.0, 0.0], [0.0, 0.0], [0.0, 0.0]
    for part in range(2):
        head = 2 * pair + part
        bias = jnp.concatenate(bias_of(table, ids, head), axis=1)
        both = 0.0
        for seq in range(2):
            rows = pl.ds(seq * PAD, PAD)
            asked = half_only(query[rows, :], part)
            into = half_only(grad[rows, :], part)
            scores = dot_f32(asked, keys[seq], NT) * 0.125 + bias
            scores = jnp.where(masks[seq], scores, -1e30)
            log = jnp.sum(jnp.where(lane == head, logs[rows, :], 0.0), axis=1, keepdims=True)
            probs = jnp.exp(scores - log)
            grad_probs = dot_f32(into, values[seq], NT)
            mean = jnp.sum(probs * grad_probs, axis=1, keepdims=True)
            grad_scores = (probs * (grad_probs - mean)).astype(BF)
            both = both + grad_scores.astype(F32)
            to_value[seq] = to_value[seq] + dot_f32(probs.astype(BF), into, TN)
            to_query[seq] = to_query[seq] + dot_f32(grad_scores, half_only(keys[seq], part), NN)
            to_key[seq] = to_key[seq] + dot_f32(grad_scores, asked, TN)
        for c in range(KEYS // 128):
            terms[c, pl.ds(head - 2 * base, PAD, stride=8), :] = both[:, c * 128 : (c + 1) * 128]
    for seq in range(2):
        rows = pl.ds(seq * PAD, PAD)
        grad_query[rows, :] = (to_query[seq] * 0.125).astype(BF)
        grad_key_own[rows, :] = to_key[seq][:PAD] * 0.125
        grad_key_other[rows, :] = (to_key[seq][HALF_KEYS : HALF_KEYS + PAD] * 0.125).astype(BF)
        grad_value_own[rows, :] = to_value[seq][:PAD]
        grad_value_other[rows, :] = to_value[seq][HALF_KEYS : HALF_KEYS + PAD].astype(BF)


def attend_back(base, counts, ids, table, logs, query, keys, values, grad, before=(), after=()):
    def rows_of(kind):
        return jax.ShapeDtypeStruct((2 * PAD, D), kind)

    columns = pl.BlockSpec((2 * PAD, PAIR), lambda i: (0, i + base))
    any_ref = pl.BlockSpec(memory_space=pl.ANY)
    return pl.pallas_call(
        functools.partial(attend_back_body, base),
        grid=(H // 4,),
        out_shape=(
            rows_of(BF),
            rows_of(F32),
            rows_of(F32),
            rows_of(BF),
            rows_of(BF),
            jax.ShapeDtypeStruct((KEYS // 128, PAD * 8, 128), F32),
        ),
        in_specs=[
            pl.BlockSpec(memory_space=pltpu.SMEM),
            fixed((PAD, KEYS)),
            fixed((16, 128)),
            fixed((2 * PAD, 128)),
        ]
        + [columns] * 6
        + [any_ref] * (len(before) + len(after)),
        out_specs=(columns,) * 5 + (fixed((KEYS // 128, PAD * 8, 128)),),
        input_output_aliases={10 + i: i for i in range(len(before))},
        cost_estimate=LIGHT,
        name="attend_back",
    )(counts, ids, table, logs, query, *keys, *values, grad, *before, *after)


GROUP = 7


def table_body(ids, early, late, *refs):
    out = refs[-1]
    bucket = lax.broadcasted_iota(jnp.int32, (NB + 1, KEYS), 0)

    def step(index, total):
        hots, terms = [], []
        for member in range(GROUP):
            row = index * GROUP + member
            hots.append(jnp.where(ids[pl.ds(row, 1), :] == bucket, 1.0, 0.0).astype(BF))
            span = pl.ds(pl.multiple_of(row * 8, 8), 8)
            terms.append(
                jnp.concatenate(
                    [
                        jnp.concatenate([part[c, span, :] for c in range(KEYS // 128)], axis=1)
                        for part in (early, late)
                    ],
                    axis=0,
                )
            )
        hot, term = jnp.concatenate(hots, axis=1), jnp.concatenate(terms, axis=1)
        high = term.astype(BF)
        low = (term - high.astype(F32)).astype(BF)
        return total + dot_f32(hot, jnp.concatenate([high, low], axis=0), NT)

    out[...] = lax.fori_loop(0, P_SIZE // GROUP, step, jnp.zeros((NB + 1, 32), F32))


def table_grad(ids, terms, after=()):
    whole = pl.BlockSpec(memory_space=pltpu.VMEM)
    both = pl.pallas_call(
        table_body,
        out_shape=jax.ShapeDtypeStruct((NB + 1, 32), F32),
        in_specs=[whole] * 3 + [pl.BlockSpec(memory_space=pl.ANY)] * len(after),
        out_specs=whole,
        cost_estimate=LIGHT,
        name="table_grad",
    )(ids, *terms, *after)
    both = both[:NB, :16] + both[:NB, 16:]
    return jnp.concatenate([both[:, : H // 2], both[:, 8 : 8 + H // 2]], axis=1)


CUT = PHASE_ROWS - 4 * D


def spread_body(half, table, *refs):
    out, held = refs[-2], refs[-1]
    start = 4 * D if half == 0 else 0
    for c in range(D // 128):
        held[...] = table[pl.ds(start, CUT), pl.ds(c * 128, 128)].astype(F32)
        for part in range(4):
            out[:, pl.ds(part * D + c * 128, 128)] = held[
                pl.ds(part, CUT // 4, stride=4), :
            ].astype(BF)


def spread(half, table, before=None):
    whole = pl.BlockSpec(memory_space=pltpu.VMEM)
    extra = () if before is None else (before,)
    return pl.pallas_call(
        functools.partial(spread_body, half),
        grid=(1,),
        out_shape=jax.ShapeDtypeStruct((D, FF), BF),
        in_specs=[whole] + [pl.BlockSpec(memory_space=pl.ANY)] * len(extra),
        out_specs=pl.BlockSpec((CUT // 4, FF), lambda i: (half, 0)),
        scratch_shapes=[pltpu.VMEM((CUT, 128), F32)],
        input_output_aliases={1: 0} if extra else {},
        cost_estimate=LIGHT,
        name="spread",
    )(table, *extra)


def inner_grad_body(share, left, right, out, turned, held):
    chunk = pl.program_id(0)

    @pl.when(chunk == 0)
    def _():
        gap = jnp.zeros((KEYS - 2 * PAD, D), BF)
        turned[...] = jnp.concatenate([left[...], gap], axis=0).T

    gap = jnp.zeros((KEYS - 2 * PAD, 256), BF)
    for part in range(4):
        start = pl.multiple_of(part * D + chunk * 256, 256)
        block = jnp.concatenate([right[:, pl.ds(start, 256)], gap], axis=0)
        value = dot_f32(turned[...], block, NN) * share
        for c in range(2):
            held[c, pl.ds(part, D, stride=4), :] = value[:, c * 128 : (c + 1) * 128]
    out[...] = jnp.concatenate([held[0], held[1]], axis=1).astype(BF)


def inner_grad(left, right, share):
    return pl.pallas_call(
        functools.partial(inner_grad_body, share),
        grid=(D // 256,),
        out_shape=jax.ShapeDtypeStruct((FF, D), BF),
        in_specs=[fixed((2 * PAD, D)), fixed((2 * PAD, FF))],
        out_specs=pl.BlockSpec((FF, 256), lambda i: (0, i)),
        scratch_shapes=[pltpu.VMEM((D, KEYS), BF), pltpu.VMEM((2, FF, 128), F32)],
        cost_estimate=LIGHT,
        name="inner_grad",
    )(left, right)


STRIP = 16
ROWS = 2 * PAD


def mean_of(values):
    return jnp.mean(values, axis=-1, keepdims=True)


def feed_body(
    base, middle, grad_out, w_first, w_second, model_vec, inner_vec,
    result, normed, hidden, grad_hidden, grad_middle, grad_wide, grad_narrow,
    acts, slopes, grads, total, center, wide,
):
    value = middle[...]
    value = value - mean_of(value)
    spread_two = lax.rsqrt(mean_of(value * value) + 1e-05)
    value = value * spread_two
    center[...] = value
    normed[...] = (value * model_vec[7:8, :] + model_vec[8:9, :]).astype(BF)

    def open_step(c, carry):
        lanes = pl.ds(pl.multiple_of(c * D, D), D)
        acts[:, lanes] = dot_f32(normed[...], w_first[:, lanes], NN) + inner_vec[0:1, lanes]
        return carry

    lax.fori_loop(0, 4, open_step, 0)

    def gelu_strip(index, carry):
        rows = pl.ds(pl.multiple_of(index * STRIP, STRIP), STRIP)
        summed = jnp.zeros((STRIP, 128), F32)
        for c in range(FF // 128):
            lanes = pl.ds(c * 128, 128)
            inner = acts[rows, lanes]
            half = 0.5 + 0.5 * lax.erf(inner * 0.7071067811865476)
            bell = jnp.exp(inner * inner * -0.5) * 0.3989422804014327
            slopes[rows, lanes] = half + inner * bell
            active = inner * half
            acts[rows, lanes] = active
            summed = summed + active
        mean = jnp.sum(summed, axis=1, keepdims=True) * (1.0 / FF)
        squares = jnp.zeros((STRIP, 128), F32)
        for c in range(FF // 128):
            away = acts[rows, pl.ds(c * 128, 128)] - mean
            squares = squares + away * away
        scale = lax.rsqrt(jnp.sum(squares, axis=1, keepdims=True) * (1.0 / FF) + 1e-05)
        for c in range(FF // 128):
            lanes = pl.ds(c * 128, 128)
            unit = (acts[rows, lanes] - mean) * scale
            acts[rows, lanes] = unit
            hidden[rows, lanes] = (unit * inner_vec[1:2, lanes] + inner_vec[2:3, lanes]).astype(BF)
            slopes[rows, lanes] = slopes[rows, lanes] * scale
        return carry

    lax.fori_loop(0, ROWS // STRIP, gelu_strip, 0)
    total[...] = middle[...] + model_vec[9:10, :]
    branch = grad_out[...].astype(BF)
    grad_narrow[...] = jnp.zeros_like(grad_narrow)
    grad_narrow[2:3, :] = jnp.sum(branch.astype(F32), axis=0, keepdims=True)

    def close_step(c, carry):
        lanes = pl.ds(pl.multiple_of(c * D, D), D)
        weight = w_second[pl.ds(pl.multiple_of(base + c * D, D), D), :]
        total[...] += dot_f32(hidden[:, lanes], weight, NN)
        grads[:, lanes] = dot_f32(branch, weight, NT)
        return carry

    lax.fori_loop(0, 4, close_step, 0)
    result[...] = total[...].astype(BF)
    wide[...] = jnp.zeros_like(wide)

    def back_strip(index, carry):
        rows = pl.ds(pl.multiple_of(index * STRIP, STRIP), STRIP)
        plain = jnp.zeros((STRIP, 128), F32)
        mixed = jnp.zeros((STRIP, 128), F32)
        for c in range(FF // 128):
            lanes = pl.ds(c * 128, 128)
            grad, unit = grads[rows, lanes], acts[rows, lanes]
            wide[1, :, lanes] += grad * unit
            wide[2, :, lanes] += grad
            grad = grad * inner_vec[1:2, lanes]
            grads[rows, lanes] = grad
            plain = plain + grad
            mixed = mixed + grad * unit
        plain = jnp.sum(plain, axis=1, keepdims=True) * (1.0 / FF)
        mixed = jnp.sum(mixed, axis=1, keepdims=True) * (1.0 / FF)
        for c in range(FF // 128):
            lanes = pl.ds(c * 128, 128)
            grad = grads[rows, lanes] - plain - acts[rows, lanes] * mixed
            low = (grad * slopes[rows, lanes]).astype(BF)
            grad_hidden[rows, lanes] = low
            wide[0, :, lanes] += low.astype(F32)
        return carry

    lax.fori_loop(0, ROWS // STRIP, back_strip, 0)
    grad_wide[...] = jnp.zeros_like(grad_wide)
    for k in range(3):
        grad_wide[k : k + 1, :] = jnp.sum(wide[k], axis=0, keepdims=True)
    total[...] = jnp.zeros_like(total)

    def last_step(c, carry):
        lanes = pl.ds(pl.multiple_of(c * D, D), D)
        total[...] += dot_f32(grad_hidden[:, lanes], w_first[:, lanes], NT)
        return carry

    lax.fori_loop(0, 4, last_step, 0)
    grad = total[...]
    unit = center[...]
    grad_narrow[0:1, :] = jnp.sum(grad * unit, axis=0, keepdims=True)
    grad_narrow[1:2, :] = jnp.sum(grad, axis=0, keepdims=True)
    grad = grad * model_vec[7:8, :]
    grad = spread_two * (grad - mean_of(grad) - unit * mean_of(grad * unit))
    grad_middle[...] = grad_out[...] + grad


def feed(base, middle, grad_out, w_first, w_second, model_vec, inner_vec):
    whole = pl.BlockSpec(memory_space=pltpu.VMEM)
    return pl.pallas_call(
        functools.partial(feed_body, base),
        out_shape=(
            jax.ShapeDtypeStruct((ROWS, D), BF),
            jax.ShapeDtypeStruct((ROWS, D), BF),
            jax.ShapeDtypeStruct((ROWS, FF), BF),
            jax.ShapeDtypeStruct((ROWS, FF), BF),
            jax.ShapeDtypeStruct((ROWS, D), F32),
            jax.ShapeDtypeStruct((8, FF), F32),
            jax.ShapeDtypeStruct((8, D), F32),
        ),
        in_specs=[whole] * 6,
        out_specs=(whole,) * 7,
        scratch_shapes=[
            pltpu.VMEM((ROWS, FF), F32),
            pltpu.VMEM((ROWS, FF), F32),
            pltpu.VMEM((ROWS, FF), F32),
            pltpu.VMEM((ROWS, D), F32),
            pltpu.VMEM((ROWS, D), F32),
            pltpu.VMEM((3, STRIP, FF), F32),
        ],
        cost_estimate=LIGHT,
        name="feed",
    )(middle, grad_out, w_first, w_second, model_vec, inner_vec)


def from_partner(block, axis, bit):
    count = lax.axis_size(axis)
    route = []
    for low in range(count):
        high = low | 1 << bit
        if high != low and high < count:
            route += [(low, high), (high, low)]
    return lax.ppermute(block, axis, route)


def layer_norm(values, gain, shift):
    center = values - jnp.mean(values, axis=-1, keepdims=True)
    spread = jnp.mean(center * center, axis=-1, keepdims=True)
    return center * lax.rsqrt(spread + 1e-05) * gain + shift


def norm_back(values, gain, shift, grad_after):
    _, pullback = jax.vjp(layer_norm, values, gain, shift)
    return pullback(grad_after)


def matmul(left, right):
    return jnp.dot(left, right, preferred_element_type=jnp.float32)


def matmul_tn(left, right):
    return lax.dot_general(
        left, right, (((0,), (0,)), ((), ())), preferred_element_type=jnp.float32
    )


def matmul_nt(left, right):
    return lax.dot_general(
        left, right, (((1,), (1,)), ((), ())), preferred_element_type=jnp.float32
    )


def exact_gelu(values):
    return jax.nn.gelu(values, approximate=False)


def unpack(flat):
    pairs = [(D, D), (D, D), (D, D), (D, D), (D, FF), (FF, D), (10, D), (3, FF), (NB + 1, H)]
    pieces = []
    offset = 0
    for dims_pair in pairs:
        extent = dims_pair[0] * dims_pair[1]
        pieces.append(flat[offset : offset + extent].reshape(dims_pair))
        offset += extent
    return pieces


def widen(values):
    return jnp.pad(values, ((0, 0), (0, PAD - P_SIZE), (0, 0))).reshape(2 * PAD, D)


def narrow(values):
    return values.reshape(1, 2, PAD, D)[:, :, :P_SIZE]


def on_device(rows, cotangent, master, first_moment, second_moment, average, lengths, buckets):
    side = lax.axis_index("mod")
    place = lax.axis_index("dp")
    fast = lax.axis_size("dp") == DP
    own_copy = master.astype(jnp.bfloat16)
    if fast:
        spot = coords()
        first, second = pack_shard(own_copy, side, place)
        is_last = jnp.logical_and(side == 1, place == DP - 1)
        vec = jnp.where(is_last, own_copy[-EDGE:], jnp.zeros((), BF))
        vec = jnp.pad(vec, (0, D)).reshape(24, D)
        riding = gather_z(jnp.concatenate([first, vec]))
        riding, second = lax.optimization_barrier((riding, second))
        first_stack = [piece[:BLOCK] for piece in riding]
        vec = riding[0][BLOCK:] + riding[1][BLOCK:] + riding[2][BLOCK:] + riding[3][BLOCK:]
        rider = jnp.pad(vec, ((0, 8), (0, 0))).reshape(4, 8, D)
        second_stack = gather_z(second)
        first_stack = jnp.concatenate([jnp.stack(first_stack), rider], axis=1)
        first_pieces = gather_far(*gather_near(first_stack))
        near_pieces, second_stack = lax.optimization_barrier((first_pieces[:2], second_stack))
        swapped = [send_mod(piece) for piece in near_pieces]
        second_stack, swapped = lax.optimization_barrier((second_stack, swapped))
        swapped += [send_mod(piece) for piece in first_pieces[2:]]
        second_near, second_got = gather_near(jnp.stack(second_stack))
        riders = [piece[:, :, BLOCK:] for piece in (*first_pieces, *swapped)]
        vec = jnp.concatenate(
            [
                jnp.sum(sum(piece.astype(F32) for piece in riders[half::2]), axis=0)
                for half in range(2)
            ],
            axis=-1,
        ).reshape(32, D)
        first_table = assemble(0, spot, [*first_pieces, *swapped])
        _, second_near, second_got = lax.optimization_barrier(
            (first_table, second_near, second_got)
        )
        second_pieces = list(gather_far(second_near, second_got))
        second_pieces = [*second_pieces, *[send_mod(piece) for piece in second_pieces]]
        square = [first_table[i * D : (i + 1) * D] for i in range(4)]
        vec_model, vec_inner = vec[:10], vec[10:22].reshape(3, FF)
        head_table = vec[22].reshape(NB + 1, H)
    else:
        weights = unpack(lax.all_gather(own_copy, ("mod", "dp"), axis=0, tiled=True))
        square, (w_inner, w_outer, vec_model, vec_inner, head_table) = weights[:4], weights[4:]
    w_query, w_key, w_value, w_out = square
    model_vec = vec_model.astype(jnp.float32)
    inner_vec = vec_inner.astype(jnp.float32)
    head_vals = head_table.astype(jnp.float32)
    scale_row = jnp.repeat(head_vals[NB], HD)
    table = jnp.pad(head_vals.T, ((0, 16 - H), (0, 128 - NB - 1)))
    full = jnp.full_like(lengths, P_SIZE)
    own_count = jnp.where(side == 0, full, lengths)
    other_count = jnp.where(side == 0, lengths, full)
    counts = jnp.concatenate([own_count, other_count]).astype(jnp.int32)
    slots = jnp.arange(PAD, dtype=jnp.int32)
    own_valid = (slots[None, :] < own_count[:, None]).astype(F32).reshape(2 * PAD, 1)
    near = lax.dynamic_slice(buckets, (side * P_SIZE, side * P_SIZE), (P_SIZE, P_SIZE))
    far = lax.dynamic_slice(buckets, (side * P_SIZE, (1 - side) * P_SIZE), (P_SIZE, P_SIZE))
    room = ((0, PAD - P_SIZE), (0, HALF_KEYS - P_SIZE))
    ids = jnp.concatenate([jnp.pad(near, room), jnp.pad(far, room)], axis=1)

    inputs = widen(rows[0]).astype(F32)
    normed = layer_norm(inputs, model_vec[0], model_vec[1])
    normed_low = normed.astype(BF)
    if fast:
        normed_low, second_pieces[:2] = lax.optimization_barrier((normed_low, second_pieces[:2]))
    keys_own = matmul(normed_low, w_key).astype(BF)
    values_own = (matmul(normed_low, w_value) + model_vec[3]).astype(BF)
    keys_other, values_other = from_partner((keys_own, values_own), "mod", 0)
    if fast:
        sent_early = tuple(second_pieces[:2])
    query = (matmul(normed_low, w_query) + model_vec[2]).astype(BF)
    keys_both, values_both = (keys_own, keys_other), (values_own, values_other)
    sent_early = sent_early if fast else ()
    attended, logs = attend(counts, ids, table, query, *keys_both, *values_both, sent_early)

    if fast:
        w_inner = spread(0, first_table)
        second_table = assemble(1, spot, second_pieces, (attended, w_inner))
        w_inner = spread(1, second_table, w_inner)
        w_outer, base = second_table, CUT
    else:
        base = 0
    scaled = attended * scale_row
    mixed = layer_norm(scaled, model_vec[4], model_vec[5])
    mixed_low = mixed.astype(BF)
    middle = inputs + (matmul(mixed_low, w_out) + model_vec[6])
    tokens_all = 2 * rows.shape[1] * P_SIZE * lax.axis_size("dp")
    share = 1.0 / tokens_all

    def weight_grad(left, right):
        value = matmul_tn(left, right) * share
        return value.astype(BF) if fast else value

    grad_out = widen(cotangent[0]).astype(F32) * own_valid
    result, normed_two_low, inner_low, grad_inner_low, grad_middle, grad_inner_vec, narrow_vec = feed(
        base, middle, grad_out, w_inner, w_outer, model_vec, inner_vec
    )
    result_rows = narrow(result)
    grad_inner_vec = grad_inner_vec[:3]
    grad_gain_two, grad_shift_two, grad_b_outer = narrow_vec[0], narrow_vec[1], narrow_vec[2]
    grad_w_outer = weight_grad(inner_low, grad_out.astype(BF))
    if fast:
        grad_w_inner = inner_grad(normed_two_low, grad_inner_low, share)
    else:
        grad_w_inner = weight_grad(normed_two_low, grad_inner_low).reshape(FF, D)
    grad_attn_low = grad_middle.astype(BF)
    grad_w_out = weight_grad(mixed_low, grad_attn_low)
    grad_b_out = jnp.sum(grad_attn_low.astype(F32), axis=0)
    grad_mixed = matmul_nt(grad_attn_low, w_out)
    grad_scaled, grad_gain_attn, grad_shift_attn = norm_back(
        scaled, model_vec[4], model_vec[5], grad_mixed
    )
    grad_head_scale = jnp.sum(jnp.sum(grad_scaled * attended, axis=0).reshape(H, HD), axis=1)
    grad_attended = (grad_scaled * scale_row).astype(BF)
    parts = (counts, ids, table, logs, query, keys_both, values_both, grad_attended)
    if fast:
        kept, lent = scatter(1, spot, [None] * 4 + [grad_w_inner, grad_w_outer])
        early = attend_back(0, *parts, after=(kept,))
        got = send_mod(lent)
        late_outs, late_ins = reduce_outs(kept, got), reduce_ins(kept, got)
        late = attend_back(H // 4, *parts, before=early[:5], after=late_outs)
    else:
        early = attend_back(0, *parts)
        late = attend_back(H // 4, *parts, before=early[:5])
    grad_query, key_kept, value_kept, key_sent, value_sent, late_terms = late
    terms = (early[5], late_terms)
    back_keys, back_values = from_partner((key_sent, value_sent), "mod", 0)
    if fast:
        back_keys, back_values, late_sent = lax.optimization_barrier(
            (back_keys, back_values, reduce_sends(late_outs))
        )
    grad_key = (key_kept + back_keys.astype(F32)).astype(BF)
    grad_value = (value_kept + back_values.astype(F32)).astype(BF)
    grad_w_query = weight_grad(normed_low, grad_query)
    grad_w_key = weight_grad(normed_low, grad_key)
    grad_w_value = weight_grad(normed_low, grad_value)
    matrices = [grad_w_query, grad_w_key, grad_w_value, grad_w_out, grad_w_inner, grad_w_outer]
    if fast:
        late_next = reduce_next(late_sent, late_ins)
        kept, lent = scatter(0, spot, matrices, late_next)
        got = send_mod(lent)
        first_outs = reduce_outs(kept, got)
        late_both, late_low = reduce_both(late_sent, late_ins, late_next)
        grad_table = table_grad(ids, terms, first_outs)
        late_turns, first_sent, grad_table = lax.optimization_barrier(
            (reduce_z(late_low), reduce_sends(first_outs), grad_table)
        )
    else:
        grad_table = table_grad(ids, terms)
    if fast:
        grad_query, grad_key, grad_value, _ = lax.optimization_barrier(
            (grad_query, grad_key, grad_value, first_outs)
        )
    grad_b_query = jnp.sum(grad_query.astype(F32), axis=0)
    grad_b_value = jnp.sum(grad_value.astype(F32), axis=0)
    grad_normed = (
        matmul_nt(grad_query, w_query) + matmul_nt(grad_key, w_key) + matmul_nt(grad_value, w_value)
    )
    grad_in_part, grad_gain_one, grad_shift_one = norm_back(
        inputs, model_vec[0], model_vec[1], grad_normed
    )
    grad_rows = narrow(grad_middle + grad_in_part)
    grad_model_vec = jnp.stack(
        [
            grad_gain_one,
            grad_shift_one,
            grad_b_query,
            grad_b_value,
            grad_gain_attn,
            grad_shift_attn,
            grad_b_out,
            grad_gain_two,
            grad_shift_two,
            grad_b_outer,
        ]
    )
    grad_heads = jnp.concatenate([grad_table, grad_head_scale[None, :]], axis=0)
    vec_grad = (
        jnp.concatenate(
            [grad_model_vec, grad_inner_vec.reshape(12, D), grad_heads.reshape(1, D)], axis=0
        )
        * share
    )
    if fast:
        second = reduce_total(late_both, late_turns)
        first_ins = reduce_ins(kept, got)
        first_next = reduce_next(first_sent, first_ins)
        first_both, first_low = reduce_both(first_sent, first_ins, first_next)
        vec_grad = sum_z_small(jnp.pad(vec_grad, ((0, 1), (0, 0))))
        vec_grad, first_low = lax.optimization_barrier((vec_grad, first_low))
        first = reduce_total(first_both, reduce_z(first_low))
        vec_grad = sum_rest_small(vec_grad)
        square = jnp.sum(first * first) + jnp.sum(second * second)
        square = square + jnp.where(is_last, jnp.sum(vec_grad * vec_grad), 0.0)
        first, second, square = lax.optimization_barrier((first, second, square))
        sent = unpack_sends(first, second, side)
        square_sum, sent = sum_scalar(square, side, place, sent)
        grad_shard = unpack_shard(*sent, vec_grad, side, place)
    else:
        local_grad = jnp.concatenate([part.reshape(-1) for part in matrices + [vec_grad]])
        half_size = local_grad.shape[0] // 2
        own_half = lax.dynamic_slice_in_dim(local_grad, side * half_size, half_size)
        other_half = lax.dynamic_slice_in_dim(local_grad, (1 - side) * half_size, half_size)
        partner_half = from_partner(other_half.astype(BF), "mod", 0).astype(F32)
        grad_shard = lax.psum_scatter(own_half + partner_half, "dp", scatter_dimension=0, tiled=True)
        square_sum = lax.psum(jnp.sum(grad_shard * grad_shard), ("mod", "dp"))
    grad_norm = jnp.sqrt(square_sum)
    clip_scale = jnp.minimum(1.0, 0.25 / (grad_norm + 1e-06))
    clipped = grad_shard * clip_scale
    new_first = 0.5 * first_moment + 0.5 * clipped
    new_second = 0.6 * second_moment + 0.4 * clipped * clipped
    direction = new_first / (1.0 - 0.5**STEP) / (jnp.sqrt(new_second / (1.0 - 0.6**STEP)) + 1e-08)
    new_master = master - 0.04 * (direction + 0.01 * master)
    new_average = 0.5 * average + 0.5 * new_master
    return (
        result_rows,
        grad_rows,
        grad_norm,
        new_master,
        new_first,
        new_second,
        new_average,
        new_master.astype(jnp.bfloat16),
    )


def solution(mesh):
    placed = (
        P("mod", "dp", None, None),
        P("mod", "dp", None, None),
        P(("mod", "dp")),
        P(("mod", "dp")),
        P(("mod", "dp")),
        P(("mod", "dp")),
        P("dp"),
        P(),
    )
    return jax.shard_map(
        on_device,
        mesh=mesh,
        in_specs=placed,
        out_specs=(
            P("mod", "dp", None, None),
            P("mod", "dp", None, None),
            P(),
            P(("mod", "dp")),
            P(("mod", "dp")),
            P(("mod", "dp")),
            P(("mod", "dp")),
            P(("mod", "dp")),
        ),
        check_vma=False,
    )
```

```python
import functools
import jax
import jax.numpy as jnp
from jax import lax
from jax.experimental import pallas as pl
from jax.experimental.pallas import tpu as pltpu
from jax.sharding import PartitionSpec as P

D = 768
H = 12
HD = 64
FF = 3072
NB = 63
P_SIZE = 196
STEP = 5


HALF = D // 2
BLOCK = 144
PHASE_ROWS = 32 * BLOCK
BF = jnp.bfloat16
F32 = jnp.float32
DP = 16
EDGE = 17664
PAD = 208
KEYS = 512
HALF_KEYS = KEYS // 2
PAIR = 2 * HD
LIGHT = pl.CostEstimate(flops=1, bytes_accessed=1, transcendentals=0)


def x_swap():
    return [(i, i ^ 1) for i in range(DP)]


def y_swap():
    return [(i, i ^ 2) for i in range(DP)]


def z_turn(step):
    return [(i, (i // 4 + step) % 4 * 4 + i % 4) for i in range(DP)]


def send_dp(block, route):
    return lax.ppermute(block, "dp", route)


def send_mod(block):
    return lax.ppermute(block, "mod", [(0, 1), (1, 0)])


def pack_shard(own, side, place):
    lead = 8832 * side + 552 * place
    count = BLOCK * D
    lent = lax.dynamic_slice(own, (count - lead,), (count,))
    given = send_mod(lent)
    nxt = [(i, i + 1) for i in range(2 * DP - 1)]
    edge = lax.ppermute(own[own.shape[0] - EDGE :], ("mod", "dp"), nxt)
    kept = lax.dynamic_slice(jnp.concatenate([edge, own[:count]]), (EDGE - lead,), (count,))
    kept = kept.reshape(BLOCK, D)
    given = given.reshape(BLOCK, D)
    return jnp.where(side == 0, kept, given), jnp.where(side == 0, given, kept)


def unpack_sends(first, second, side):
    even = jnp.where(side == 0, first, second).reshape(-1)
    lent = jnp.where(side == 0, second, first)
    odd = send_mod(lent)
    back = [(i + 1, i) for i in range(2 * DP - 1)]
    return even, odd, lax.ppermute(even[:EDGE], ("mod", "dp"), back)


def unpack_shard(even, odd, edge, vec, side, place):
    lead = 8832 * side + 552 * place
    is_last = jnp.logical_and(side == 1, place == DP - 1)
    edge = jnp.where(is_last, vec.reshape(-1)[:EDGE], edge)
    return lax.dynamic_slice(jnp.concatenate([even, odd.reshape(-1), edge]), (lead,), (221736,))


def sum_z_small(part):
    part = part + send_dp(part, z_turn(2))
    return part + send_dp(part, [(i, i ^ 4) for i in range(DP)])


def sum_rest_small(part):
    part = part + send_dp(part, x_swap())
    part = part + send_dp(part, y_swap())
    return part + send_mod(part)


def xy_swap():
    return [(i, i ^ 3) for i in range(DP)]


def sum_scalar(value, side, place, beside):
    slots = lax.broadcasted_iota(jnp.int32, (8, 128), 0) * 128
    slots = slots + lax.broadcasted_iota(jnp.int32, (8, 128), 1)
    own = jnp.where(slots == side * DP + place, value, 0.0)
    for routes in ([z_turn(1), z_turn(2), z_turn(3)], [x_swap(), y_swap(), xy_swap()]):
        got = [send_dp(own, route) for route in routes]
        own = own + got[0] + got[1] + got[2]
        own, beside = lax.optimization_barrier((own, beside))
    return jnp.sum(own + send_mod(own)), beside


def gather_z(block):
    return [block] + [send_dp(block, z_turn(step)) for step in (1, 2, 3)]


def gather_near(stack):
    left, right = stack[:, :, :HALF], stack[:, :, HALF:]
    got = send_dp(left, x_swap()), send_dp(right, y_swap())
    return (left, right), got


def gather_far(near, got):
    left = jnp.stack([near[0], got[0]])
    right = jnp.stack([near[1], got[1]])
    return left, right, send_dp(left, y_swap()), send_dp(right, x_swap())


def coords():
    side = lax.axis_index("mod")
    place = lax.axis_index("dp")
    return jnp.stack([side, place // 4, place // 2 % 2, place % 2]).astype(jnp.int32)


def assemble_body(phase, spot, *refs):
    pieces, out, sem = refs[:8], refs[-2], refs[-1]
    side, z, y, x = spot[0], spot[1], spot[2], spot[3]
    copies = []
    for index in range(16):
        other, half, yr, xr = index // 8, index // 4 % 2, index // 2 % 2, index % 2
        owner = side ^ other
        parity = owner if phase == 0 else 1 - owner
        source = pieces[other * 4 + (yr if half == 0 else xr) * 2 + half]
        for turn in range(4):
            home = ((z - turn) & 3) * 4 + (y ^ yr) * 2 + (x ^ xr)
            copies.append(
                pltpu.make_async_copy(
                    source.at[xr if half == 0 else yr, turn, pl.ds(0, BLOCK), :],
                    out.at[home * 2 + parity, :, pl.ds(half * HALF, HALF)],
                    sem.at[index * 4 + turn],
                )
            )
    for copy in copies:
        copy.start()
    for copy in copies:
        copy.wait()


def assemble(phase, spot, pieces, after=()):
    return pl.pallas_call(
        functools.partial(assemble_body, phase),
        out_shape=jax.ShapeDtypeStruct((32, BLOCK, D), BF),
        in_specs=[pl.BlockSpec(memory_space=pltpu.SMEM)] + [pl.BlockSpec(memory_space=pl.ANY)] * (8 + len(after)),
        out_specs=pl.BlockSpec(memory_space=pltpu.VMEM),
        scratch_shapes=[pltpu.SemaphoreType.DMA((64,))],
        cost_estimate=LIGHT,
        name="assemble",
    )(spot, *pieces, *after).reshape(PHASE_ROWS, D)


def scatter_copies(phase, pieces, spot, sources, kept, lent, sem):
    side, z, y, x = spot[0], spot[1], spot[2], spot[3]
    begun, waits = {}, []
    for block in range(32):
        home, parity = block // 2, block % 2
        owner = parity if phase == 0 else 1 - parity
        turn = (home // 4 - z) & 3
        yr = (home // 2 % 2) ^ y
        xr = (home % 2) ^ x
        for index, source_row, block_row, count in pieces[block]:
            for half in range(2):
                stay, leave = [
                    pltpu.make_async_copy(
                        sources[index].at[pl.ds(source_row, count), pl.ds(half * HALF, HALF)],
                        target.at[half, yr, xr, turn, pl.ds(block_row, count), :],
                        sem.at[len(waits)],
                    )
                    for target in (kept, lent)
                ]
                begun.setdefault(index, []).append((owner, stay, leave))
                waits.append(stay)

    def start(index):
        for owner, stay, leave in begun[index]:
            pl.when(side == owner)(stay.start)
            pl.when(side != owner)(leave.start)

    def wait():
        for copy in waits:
            copy.wait()

    return start, wait


def scatter_pieces(phase, present):
    starts = [0]
    for rows in (D, D, D, D, FF, FF):
        starts.append(starts[-1] + rows)
    pieces = []
    for block in range(32):
        low = phase * PHASE_ROWS + block * BLOCK
        parts = []
        for index in range(len(present)):
            first, last = max(low, starts[index]), min(low + BLOCK, starts[index + 1])
            if first < last:
                parts.append((index, first - starts[index], first - low, last - first))
        pieces.append(parts)
    used = sorted({part[0] for parts in pieces for part in parts})
    pieces = [[(used.index(part[0]),) + part[1:] for part in parts] for parts in pieces]
    return pieces, used, 2 * sum(len(parts) for parts in pieces)


def scatter_body(phase, pieces, number, spot, *refs):
    sources, kept, lent, sem = refs[:number], refs[-3], refs[-2], refs[-1]
    start, wait = scatter_copies(phase, pieces, spot, sources, kept, lent, sem)
    for index in range(number):
        start(index)
    wait()


def scatter(phase, spot, tables, after=()):
    pieces, used, count = scatter_pieces(phase, tables)
    return pl.pallas_call(
        functools.partial(scatter_body, phase, pieces, len(used)),
        out_shape=(jax.ShapeDtypeStruct((2, 2, 2, 4, BLOCK, HALF), BF),) * 2,
        in_specs=[pl.BlockSpec(memory_space=pltpu.SMEM)]
        + [pl.BlockSpec(memory_space=pltpu.VMEM)] * len(used)
        + [pl.BlockSpec(memory_space=pl.ANY)] * len(after),
        out_specs=(pl.BlockSpec(memory_space=pl.ANY),) * 2,
        scratch_shapes=[pltpu.SemaphoreType.DMA((count,))],
        cost_estimate=LIGHT,
        name="scatter",
    )(spot, *[tables[index] for index in used], *after)


def plus(left, right):
    return (left.astype(F32) + right.astype(F32)).astype(BF)


def outs_body(*refs):
    left_mine, left_theirs, right_mine, right_theirs, left, right = refs[:4] + refs[-2:]
    index = pl.program_id(0)

    @pl.when(index < 2)
    def _():
        left[0] = plus(left_mine[0, 0, 0], left_theirs[0, 0, 0])

    @pl.when(index >= 2)
    def _():
        right[0] = plus(right_mine[0, 0, 0], right_theirs[0, 0, 0])


def reduce_outs(mine, theirs, after=()):
    block = (1, 1, 1, 4, BLOCK, HALF)
    left = pl.BlockSpec(block, lambda i: (0, jnp.minimum(i, 1), 1, 0, 0, 0))
    right = pl.BlockSpec(block, lambda i: (1, 1, jnp.maximum(i - 2, 0), 0, 0, 0))
    return pl.pallas_call(
        outs_body,
        grid=(4,),
        out_shape=(jax.ShapeDtypeStruct((2, 4, BLOCK, HALF), BF),) * 2,
        in_specs=[left, left, right, right] + [pl.BlockSpec(memory_space=pl.ANY)] * len(after),
        out_specs=(
            pl.BlockSpec((1, 4, BLOCK, HALF), lambda i: (jnp.minimum(i, 1), 0, 0, 0)),
            pl.BlockSpec((1, 4, BLOCK, HALF), lambda i: (jnp.maximum(i - 2, 0), 0, 0, 0)),
        ),
        cost_estimate=LIGHT,
        name="reduce_outs",
    )(mine, theirs, mine, theirs, *after)


def reduce_sends(outs):
    return send_dp(outs[0], x_swap()), send_dp(outs[1], y_swap())


def reduce_ins(mine, theirs):
    return plus(mine[0, :, 0], theirs[0, :, 0]), plus(mine[1, 0], theirs[1, 0])


def reduce_next(sent, ins):
    left_next = send_dp(plus(ins[0][1], sent[0][1]), y_swap())
    right_next = send_dp(plus(ins[1][1], sent[1][1]), x_swap())
    return left_next, right_next


def reduce_both(sent, ins, nexts):
    left, right = [
        ins[k][0].astype(F32) + sent[k][0].astype(F32) + nexts[k].astype(F32) for k in range(2)
    ]
    both = jnp.concatenate([left, right], axis=-1)
    low = both.astype(BF)
    return both[0], [low[step] for step in (1, 2, 3)]


def reduce_z(low):
    return [send_dp(low[step - 1], z_turn(step)) for step in (1, 2, 3)]


def reduce_total(own, turns):
    return own + turns[0].astype(F32) + turns[1].astype(F32) + turns[2].astype(F32)


def dot_f32(left, right, dims):
    return lax.dot_general(left, right, (dims, ((), ())), preferred_element_type=F32)


NN = ((1,), (0,))
NT = ((1,), (1,))
TN = ((0,), (0,))


def bias_of(table_ref, ids_ref, head):
    entry = jnp.broadcast_to(table_ref[pl.ds(head, 1), :], (PAD, 128))
    return [
        jnp.take_along_axis(
            entry, ids_ref[:, c * 128 : (c + 1) * 128], axis=1, mode="promise_in_bounds"
        )
        for c in range(KEYS // 128)
    ]


def joint_keys(own_ref, other_ref, seq):
    rows = pl.ds(seq * PAD, PAD)
    gap = jnp.zeros((HALF_KEYS - PAD, PAIR), BF)
    return jnp.concatenate([own_ref[rows, :], gap, other_ref[rows, :], gap], axis=0)


def key_mask(counts_ref, seq):
    lane = lax.broadcasted_iota(jnp.int32, (1, KEYS), 1)
    own, other = counts_ref[seq], counts_ref[2 + seq]
    return jnp.logical_or(
        lane < own, jnp.logical_and(lane >= HALF_KEYS, lane < HALF_KEYS + other)
    )


def half_only(values, part):
    lane = lax.broadcasted_iota(jnp.int32, values.shape, 1)
    keep = lane < HD if part == 0 else lane >= HD
    return jnp.where(keep, values, jnp.zeros((), values.dtype))


def attend_body(counts, ids, table, query, key_own, key_other, value_own, value_other, *refs):
    out, logs = refs[-2:]
    pair = pl.program_id(0)
    keys = [joint_keys(key_own, key_other, seq) for seq in range(2)]
    values = [joint_keys(value_own, value_other, seq) for seq in range(2)]
    masks = [key_mask(counts, seq) for seq in range(2)]
    lane = lax.broadcasted_iota(jnp.int32, (PAD, 128), 1)
    done = [None, None]
    for part in range(2):
        head = 2 * pair + part
        bias = jnp.concatenate(bias_of(table, ids, head), axis=1)
        for seq in range(2):
            rows = pl.ds(seq * PAD, PAD)
            scores = dot_f32(half_only(query[rows, :], part), keys[seq], NT) * 0.125 + bias
            scores = jnp.where(masks[seq], scores, -1e30)
            top = jnp.max(scores, axis=1, keepdims=True)
            powers = jnp.exp(scores - top)
            total = jnp.sum(powers, axis=1, keepdims=True)
            probs = (powers * (1.0 / total)).astype(BF)
            got = dot_f32(probs, values[seq], NN)
            done[seq] = got if part == 0 else jnp.where(lane < HD, done[seq], got)
            logs[rows, :] = jnp.where(lane == head, top + jnp.log(total), logs[rows, :])
    for seq in range(2):
        out[pl.ds(seq * PAD, PAD), :] = done[seq]


def fixed(shape):
    return pl.BlockSpec(shape, lambda i: (0,) * len(shape))


def by_pair():
    return pl.BlockSpec((2 * PAD, PAIR), lambda i: (0, i))


def attend(counts, ids, table, query, key_own, key_other, value_own, value_other, after):
    return pl.pallas_call(
        attend_body,
        grid=(H // 2,),
        out_shape=(
            jax.ShapeDtypeStruct((2 * PAD, D), F32),
            jax.ShapeDtypeStruct((2 * PAD, 128), F32),
        ),
        in_specs=[pl.BlockSpec(memory_space=pltpu.SMEM), fixed((PAD, KEYS)), fixed((16, 128))]
        + [by_pair()] * 5
        + [pl.BlockSpec(memory_space=pl.ANY)] * len(after),
        out_specs=(by_pair(), fixed((2 * PAD, 128))),
        cost_estimate=LIGHT,
        name="attend",
    )(counts, ids, table, query, key_own, key_other, value_own, value_other, *after)


def attend_back_body(
    base, counts, ids, table, logs, query, key_own, key_other, value_own, value_other, grad, *refs
):
    grad_query, grad_key_own, grad_value_own, grad_key_other, grad_value_other, terms = refs[-6:]
    pair = pl.program_id(0) + base
    keys = [joint_keys(key_own, key_other, seq) for seq in range(2)]
    values = [joint_keys(value_own, value_other, seq) for seq in range(2)]
    masks = [key_mask(counts, seq) for seq in range(2)]
    lane = lax.broadcasted_iota(jnp.int32, (PAD, 128), 1)
    to_query, to_key, to_value = [0.0, 0.0], [0.0, 0.0], [0.0, 0.0]
    for part in range(2):
        head = 2 * pair + part
        bias = jnp.concatenate(bias_of(table, ids, head), axis=1)
        both = 0.0
        for seq in range(2):
            rows = pl.ds(seq * PAD, PAD)
            asked = half_only(query[rows, :], part)
            into = half_only(grad[rows, :], part)
            scores = dot_f32(asked, keys[seq], NT) * 0.125 + bias
            scores = jnp.where(masks[seq], scores, -1e30)
            log = jnp.sum(jnp.where(lane == head, logs[rows, :], 0.0), axis=1, keepdims=True)
            probs = jnp.exp(scores - log)
            grad_probs = dot_f32(into, values[seq], NT)
            mean = jnp.sum(probs * grad_probs, axis=1, keepdims=True)
            grad_scores = (probs * (grad_probs - mean)).astype(BF)
            both = both + grad_scores.astype(F32)
            to_value[seq] = to_value[seq] + dot_f32(probs.astype(BF), into, TN)
            to_query[seq] = to_query[seq] + dot_f32(grad_scores, half_only(keys[seq], part), NN)
            to_key[seq] = to_key[seq] + dot_f32(grad_scores, asked, TN)
        for c in range(KEYS // 128):
            terms[c, pl.ds(head - 2 * base, PAD, stride=8), :] = both[:, c * 128 : (c + 1) * 128]
    for seq in range(2):
        rows = pl.ds(seq * PAD, PAD)
        grad_query[rows, :] = (to_query[seq] * 0.125).astype(BF)
        grad_key_own[rows, :] = to_key[seq][:PAD] * 0.125
        grad_key_other[rows, :] = (to_key[seq][HALF_KEYS : HALF_KEYS + PAD] * 0.125).astype(BF)
        grad_value_own[rows, :] = to_value[seq][:PAD]
        grad_value_other[rows, :] = to_value[seq][HALF_KEYS : HALF_KEYS + PAD].astype(BF)


def attend_back(base, counts, ids, table, logs, query, keys, values, grad, before=(), after=()):
    def rows_of(kind):
        return jax.ShapeDtypeStruct((2 * PAD, D), kind)

    columns = pl.BlockSpec((2 * PAD, PAIR), lambda i: (0, i + base))
    any_ref = pl.BlockSpec(memory_space=pl.ANY)
    return pl.pallas_call(
        functools.partial(attend_back_body, base),
        grid=(H // 4,),
        out_shape=(
            rows_of(BF),
            rows_of(F32),
            rows_of(F32),
            rows_of(BF),
            rows_of(BF),
            jax.ShapeDtypeStruct((KEYS // 128, PAD * 8, 128), F32),
        ),
        in_specs=[
            pl.BlockSpec(memory_space=pltpu.SMEM),
            fixed((PAD, KEYS)),
            fixed((16, 128)),
            fixed((2 * PAD, 128)),
        ]
        + [columns] * 6
        + [any_ref] * (len(before) + len(after)),
        out_specs=(columns,) * 5 + (fixed((KEYS // 128, PAD * 8, 128)),),
        input_output_aliases={10 + i: i for i in range(len(before))},
        cost_estimate=LIGHT,
        name="attend_back",
    )(counts, ids, table, logs, query, *keys, *values, grad, *before, *after)


GROUP = 7


def table_body(ids, early, late, *refs):
    out = refs[-1]
    bucket = lax.broadcasted_iota(jnp.int32, (NB + 1, KEYS), 0)

    def step(index, total):
        hots, terms = [], []
        for member in range(GROUP):
            row = index * GROUP + member
            hots.append(jnp.where(ids[pl.ds(row, 1), :] == bucket, 1.0, 0.0).astype(BF))
            span = pl.ds(pl.multiple_of(row * 8, 8), 8)
            terms.append(
                jnp.concatenate(
                    [
                        jnp.concatenate([part[c, span, :] for c in range(KEYS // 128)], axis=1)
                        for part in (early, late)
                    ],
                    axis=0,
                )
            )
        hot, term = jnp.concatenate(hots, axis=1), jnp.concatenate(terms, axis=1)
        high = term.astype(BF)
        low = (term - high.astype(F32)).astype(BF)
        return total + dot_f32(hot, jnp.concatenate([high, low], axis=0), NT)

    out[...] = lax.fori_loop(0, P_SIZE // GROUP, step, jnp.zeros((NB + 1, 32), F32))


def table_grad(ids, terms, after=()):
    whole = pl.BlockSpec(memory_space=pltpu.VMEM)
    both = pl.pallas_call(
        table_body,
        out_shape=jax.ShapeDtypeStruct((NB + 1, 32), F32),
        in_specs=[whole] * 3 + [pl.BlockSpec(memory_space=pl.ANY)] * len(after),
        out_specs=whole,
        cost_estimate=LIGHT,
        name="table_grad",
    )(ids, *terms, *after)
    both = both[:NB, :16] + both[:NB, 16:]
    return jnp.concatenate([both[:, : H // 2], both[:, 8 : 8 + H // 2]], axis=1)


CUT = PHASE_ROWS - 4 * D


def spread_body(half, table, *refs):
    out, held = refs[-2], refs[-1]
    start = 4 * D if half == 0 else 0
    for c in range(D // 128):
        held[...] = table[pl.ds(start, CUT), pl.ds(c * 128, 128)].astype(F32)
        for part in range(4):
            out[:, pl.ds(part * D + c * 128, 128)] = held[
                pl.ds(part, CUT // 4, stride=4), :
            ].astype(BF)


def spread(half, table, before=None):
    whole = pl.BlockSpec(memory_space=pltpu.VMEM)
    extra = () if before is None else (before,)
    return pl.pallas_call(
        functools.partial(spread_body, half),
        grid=(1,),
        out_shape=jax.ShapeDtypeStruct((D, FF), BF),
        in_specs=[whole] + [pl.BlockSpec(memory_space=pl.ANY)] * len(extra),
        out_specs=pl.BlockSpec((CUT // 4, FF), lambda i: (half, 0)),
        scratch_shapes=[pltpu.VMEM((CUT, 128), F32)],
        input_output_aliases={1: 0} if extra else {},
        cost_estimate=LIGHT,
        name="spread",
    )(table, *extra)


def inner_grad_body(share, pieces, spot, outer, left, right, out, kept, lent, turned, held, sem):
    start, wait = scatter_copies(1, pieces, spot, (out, outer), kept, lent, sem)
    start(1)
    turned[...] = jnp.concatenate([left[...], jnp.zeros((KEYS - 2 * PAD, D), BF)], axis=0).T
    gap = jnp.zeros((KEYS - 2 * PAD, 256), BF)

    def step(chunk, carry):
        for part in range(4):
            begin = pl.multiple_of(part * D + chunk * 256, 256)
            block = jnp.concatenate([right[:, pl.ds(begin, 256)], gap], axis=0)
            value = dot_f32(turned[...], block, NN) * share
            for c in range(2):
                held[c, pl.ds(part, D, stride=4), :] = value[:, c * 128 : (c + 1) * 128]
        for c in range(2):
            lanes = pl.ds(pl.multiple_of(chunk * 256 + c * 128, 128), 128)
            out[:, lanes] = held[c].astype(BF)
        return carry

    lax.fori_loop(0, D // 256, step, 0)
    start(0)
    wait()


def inner_grad(spot, outer, left, right, share):
    pieces, used, count = scatter_pieces(1, (0, 0, 0, 0, 1, 1))
    whole = pl.BlockSpec(memory_space=pltpu.VMEM)
    return pl.pallas_call(
        functools.partial(inner_grad_body, share, pieces),
        out_shape=(jax.ShapeDtypeStruct((FF, D), BF),)
        + (jax.ShapeDtypeStruct((2, 2, 2, 4, BLOCK, HALF), BF),) * 2,
        in_specs=[pl.BlockSpec(memory_space=pltpu.SMEM)] + [whole] * 3,
        out_specs=(whole,) + (pl.BlockSpec(memory_space=pl.ANY),) * 2,
        scratch_shapes=[
            pltpu.VMEM((D, KEYS), BF),
            pltpu.VMEM((2, FF, 128), F32),
            pltpu.SemaphoreType.DMA((count,)),
        ],
        cost_estimate=LIGHT,
        name="inner_grad",
    )(spot, outer, left, right)


STRIP = 16
ROWS = 2 * PAD


def mean_of(values):
    return jnp.mean(values, axis=-1, keepdims=True)


def feed_body(
    base, middle, grad_out, w_first, w_second, model_vec, inner_vec,
    result, normed, hidden, grad_hidden, grad_middle, grad_wide, grad_narrow,
    acts, slopes, grads, total, center, wide,
):
    value = middle[...]
    value = value - mean_of(value)
    spread_two = lax.rsqrt(mean_of(value * value) + 1e-05)
    value = value * spread_two
    center[...] = value
    normed[...] = (value * model_vec[7:8, :] + model_vec[8:9, :]).astype(BF)

    def open_step(c, carry):
        lanes = pl.ds(pl.multiple_of(c * D, D), D)
        acts[:, lanes] = dot_f32(normed[...], w_first[:, lanes], NN) + inner_vec[0:1, lanes]
        return carry

    lax.fori_loop(0, 4, open_step, 0)

    def gelu_strip(index, carry):
        rows = pl.ds(pl.multiple_of(index * STRIP, STRIP), STRIP)
        summed = jnp.zeros((STRIP, 128), F32)
        for c in range(FF // 128):
            lanes = pl.ds(c * 128, 128)
            inner = acts[rows, lanes]
            half = 0.5 + 0.5 * lax.erf(inner * 0.7071067811865476)
            bell = jnp.exp(inner * inner * -0.5) * 0.3989422804014327
            slopes[rows, lanes] = half + inner * bell
            active = inner * half
            acts[rows, lanes] = active
            summed = summed + active
        mean = jnp.sum(summed, axis=1, keepdims=True) * (1.0 / FF)
        squares = jnp.zeros((STRIP, 128), F32)
        for c in range(FF // 128):
            away = acts[rows, pl.ds(c * 128, 128)] - mean
            squares = squares + away * away
        scale = lax.rsqrt(jnp.sum(squares, axis=1, keepdims=True) * (1.0 / FF) + 1e-05)
        for c in range(FF // 128):
            lanes = pl.ds(c * 128, 128)
            unit = (acts[rows, lanes] - mean) * scale
            acts[rows, lanes] = unit
            hidden[rows, lanes] = (unit * inner_vec[1:2, lanes] + inner_vec[2:3, lanes]).astype(BF)
            slopes[rows, lanes] = slopes[rows, lanes] * scale
        return carry

    lax.fori_loop(0, ROWS // STRIP, gelu_strip, 0)
    total[...] = middle[...] + model_vec[9:10, :]
    branch = grad_out[...].astype(BF)
    grad_narrow[...] = jnp.zeros_like(grad_narrow)
    grad_narrow[2:3, :] = jnp.sum(branch.astype(F32), axis=0, keepdims=True)

    def close_step(c, carry):
        lanes = pl.ds(pl.multiple_of(c * D, D), D)
        weight = w_second[pl.ds(pl.multiple_of(base + c * D, D), D), :]
        total[...] += dot_f32(hidden[:, lanes], weight, NN)
        grads[:, lanes] = dot_f32(branch, weight, NT)
        return carry

    lax.fori_loop(0, 4, close_step, 0)
    result[...] = total[...].astype(BF)
    wide[...] = jnp.zeros_like(wide)

    def back_strip(index, carry):
        rows = pl.ds(pl.multiple_of(index * STRIP, STRIP), STRIP)
        plain = jnp.zeros((STRIP, 128), F32)
        mixed = jnp.zeros((STRIP, 128), F32)
        for c in range(FF // 128):
            lanes = pl.ds(c * 128, 128)
            grad, unit = grads[rows, lanes], acts[rows, lanes]
            wide[1, :, lanes] += grad * unit
            wide[2, :, lanes] += grad
            grad = grad * inner_vec[1:2, lanes]
            grads[rows, lanes] = grad
            plain = plain + grad
            mixed = mixed + grad * unit
        plain = jnp.sum(plain, axis=1, keepdims=True) * (1.0 / FF)
        mixed = jnp.sum(mixed, axis=1, keepdims=True) * (1.0 / FF)
        for c in range(FF // 128):
            lanes = pl.ds(c * 128, 128)
            grad = grads[rows, lanes] - plain - acts[rows, lanes] * mixed
            low = (grad * slopes[rows, lanes]).astype(BF)
            grad_hidden[rows, lanes] = low
            wide[0, :, lanes] += low.astype(F32)
        return carry

    lax.fori_loop(0, ROWS // STRIP, back_strip, 0)
    grad_wide[...] = jnp.zeros_like(grad_wide)
    for k in range(3):
        grad_wide[k : k + 1, :] = jnp.sum(wide[k], axis=0, keepdims=True)
    total[...] = jnp.zeros_like(total)

    def last_step(c, carry):
        lanes = pl.ds(pl.multiple_of(c * D, D), D)
        total[...] += dot_f32(grad_hidden[:, lanes], w_first[:, lanes], NT)
        return carry

    lax.fori_loop(0, 4, last_step, 0)
    grad = total[...]
    unit = center[...]
    grad_narrow[0:1, :] = jnp.sum(grad * unit, axis=0, keepdims=True)
    grad_narrow[1:2, :] = jnp.sum(grad, axis=0, keepdims=True)
    grad = grad * model_vec[7:8, :]
    grad = spread_two * (grad - mean_of(grad) - unit * mean_of(grad * unit))
    grad_middle[...] = grad_out[...] + grad


def feed(base, middle, grad_out, w_first, w_second, model_vec, inner_vec):
    whole = pl.BlockSpec(memory_space=pltpu.VMEM)
    return pl.pallas_call(
        functools.partial(feed_body, base),
        out_shape=(
            jax.ShapeDtypeStruct((ROWS, D), BF),
            jax.ShapeDtypeStruct((ROWS, D), BF),
            jax.ShapeDtypeStruct((ROWS, FF), BF),
            jax.ShapeDtypeStruct((ROWS, FF), BF),
            jax.ShapeDtypeStruct((ROWS, D), F32),
            jax.ShapeDtypeStruct((8, FF), F32),
            jax.ShapeDtypeStruct((8, D), F32),
        ),
        in_specs=[whole] * 6,
        out_specs=(whole,) * 7,
        scratch_shapes=[
            pltpu.VMEM((ROWS, FF), F32),
            pltpu.VMEM((ROWS, FF), F32),
            pltpu.VMEM((ROWS, FF), F32),
            pltpu.VMEM((ROWS, D), F32),
            pltpu.VMEM((ROWS, D), F32),
            pltpu.VMEM((3, STRIP, FF), F32),
        ],
        cost_estimate=LIGHT,
        name="feed",
    )(middle, grad_out, w_first, w_second, model_vec, inner_vec)


def from_partner(block, axis, bit):
    count = lax.axis_size(axis)
    route = []
    for low in range(count):
        high = low | 1 << bit
        if high != low and high < count:
            route += [(low, high), (high, low)]
    return lax.ppermute(block, axis, route)


def layer_norm(values, gain, shift):
    center = values - jnp.mean(values, axis=-1, keepdims=True)
    spread = jnp.mean(center * center, axis=-1, keepdims=True)
    return center * lax.rsqrt(spread + 1e-05) * gain + shift


def norm_back(values, gain, shift, grad_after):
    _, pullback = jax.vjp(layer_norm, values, gain, shift)
    return pullback(grad_after)


def matmul(left, right):
    return jnp.dot(left, right, preferred_element_type=jnp.float32)


def matmul_tn(left, right):
    return lax.dot_general(
        left, right, (((0,), (0,)), ((), ())), preferred_element_type=jnp.float32
    )


def matmul_nt(left, right):
    return lax.dot_general(
        left, right, (((1,), (1,)), ((), ())), preferred_element_type=jnp.float32
    )


def exact_gelu(values):
    return jax.nn.gelu(values, approximate=False)


def unpack(flat):
    pairs = [(D, D), (D, D), (D, D), (D, D), (D, FF), (FF, D), (10, D), (3, FF), (NB + 1, H)]
    pieces = []
    offset = 0
    for dims_pair in pairs:
        extent = dims_pair[0] * dims_pair[1]
        pieces.append(flat[offset : offset + extent].reshape(dims_pair))
        offset += extent
    return pieces


def widen(values):
    return jnp.pad(values, ((0, 0), (0, PAD - P_SIZE), (0, 0))).reshape(2 * PAD, D)


def narrow(values):
    return values.reshape(1, 2, PAD, D)[:, :, :P_SIZE]


def on_device(rows, cotangent, master, first_moment, second_moment, average, lengths, buckets):
    side = lax.axis_index("mod")
    place = lax.axis_index("dp")
    fast = lax.axis_size("dp") == DP
    own_copy = master.astype(jnp.bfloat16)
    if fast:
        spot = coords()
        first, second = pack_shard(own_copy, side, place)
        is_last = jnp.logical_and(side == 1, place == DP - 1)
        vec = jnp.where(is_last, own_copy[-EDGE:], jnp.zeros((), BF))
        vec = jnp.pad(vec, (0, D)).reshape(24, D)
        riding = gather_z(jnp.concatenate([first, vec]))
        riding, second = lax.optimization_barrier((riding, second))
        first_stack = [piece[:BLOCK] for piece in riding]
        vec = riding[0][BLOCK:] + riding[1][BLOCK:] + riding[2][BLOCK:] + riding[3][BLOCK:]
        rider = jnp.pad(vec, ((0, 8), (0, 0))).reshape(4, 8, D)
        second_stack = gather_z(second)
        first_stack = jnp.concatenate([jnp.stack(first_stack), rider], axis=1)
        first_pieces = gather_far(*gather_near(first_stack))
        near_pieces, second_stack = lax.optimization_barrier((first_pieces[:2], second_stack))
        swapped = [send_mod(piece) for piece in near_pieces]
        second_stack, swapped = lax.optimization_barrier((second_stack, swapped))
        swapped += [send_mod(piece) for piece in first_pieces[2:]]
        second_near, second_got = gather_near(jnp.stack(second_stack))
        riders = [piece[:, :, BLOCK:] for piece in (*first_pieces, *swapped)]
        vec = jnp.concatenate(
            [
                jnp.sum(sum(piece.astype(F32) for piece in riders[half::2]), axis=0)
                for half in range(2)
            ],
            axis=-1,
        ).reshape(32, D)
        first_table = assemble(0, spot, [*first_pieces, *swapped])
        _, second_near, second_got = lax.optimization_barrier(
            (first_table, second_near, second_got)
        )
        second_pieces = list(gather_far(second_near, second_got))
        second_pieces = [*second_pieces, *[send_mod(piece) for piece in second_pieces]]
        square = [first_table[i * D : (i + 1) * D] for i in range(4)]
        vec_model, vec_inner = vec[:10], vec[10:22].reshape(3, FF)
        head_table = vec[22].reshape(NB + 1, H)
    else:
        weights = unpack(lax.all_gather(own_copy, ("mod", "dp"), axis=0, tiled=True))
        square, (w_inner, w_outer, vec_model, vec_inner, head_table) = weights[:4], weights[4:]
    w_query, w_key, w_value, w_out = square
    model_vec = vec_model.astype(jnp.float32)
    inner_vec = vec_inner.astype(jnp.float32)
    head_vals = head_table.astype(jnp.float32)
    scale_row = jnp.repeat(head_vals[NB], HD)
    table = jnp.pad(head_vals.T, ((0, 16 - H), (0, 128 - NB - 1)))
    full = jnp.full_like(lengths, P_SIZE)
    own_count = jnp.where(side == 0, full, lengths)
    other_count = jnp.where(side == 0, lengths, full)
    counts = jnp.concatenate([own_count, other_count]).astype(jnp.int32)
    slots = jnp.arange(PAD, dtype=jnp.int32)
    own_valid = (slots[None, :] < own_count[:, None]).astype(F32).reshape(2 * PAD, 1)
    near = lax.dynamic_slice(buckets, (side * P_SIZE, side * P_SIZE), (P_SIZE, P_SIZE))
    far = lax.dynamic_slice(buckets, (side * P_SIZE, (1 - side) * P_SIZE), (P_SIZE, P_SIZE))
    room = ((0, PAD - P_SIZE), (0, HALF_KEYS - P_SIZE))
    ids = jnp.concatenate([jnp.pad(near, room), jnp.pad(far, room)], axis=1)

    inputs = widen(rows[0]).astype(F32)
    normed = layer_norm(inputs, model_vec[0], model_vec[1])
    normed_low = normed.astype(BF)
    if fast:
        normed_low, second_pieces[:2] = lax.optimization_barrier((normed_low, second_pieces[:2]))
    keys_own = matmul(normed_low, w_key).astype(BF)
    values_own = (matmul(normed_low, w_value) + model_vec[3]).astype(BF)
    keys_other, values_other = from_partner((keys_own, values_own), "mod", 0)
    if fast:
        sent_early = tuple(second_pieces[:2])
    query = (matmul(normed_low, w_query) + model_vec[2]).astype(BF)
    keys_both, values_both = (keys_own, keys_other), (values_own, values_other)
    sent_early = sent_early if fast else ()
    attended, logs = attend(counts, ids, table, query, *keys_both, *values_both, sent_early)

    if fast:
        w_inner = spread(0, first_table)
        second_table = assemble(1, spot, second_pieces, (attended, w_inner))
        w_inner = spread(1, second_table, w_inner)
        w_outer, base = second_table, CUT
    else:
        base = 0
    scaled = attended * scale_row
    mixed = layer_norm(scaled, model_vec[4], model_vec[5])
    mixed_low = mixed.astype(BF)
    middle = inputs + (matmul(mixed_low, w_out) + model_vec[6])
    tokens_all = 2 * rows.shape[1] * P_SIZE * lax.axis_size("dp")
    share = 1.0 / tokens_all

    def weight_grad(left, right):
        value = matmul_tn(left, right) * share
        return value.astype(BF) if fast else value

    grad_out = widen(cotangent[0]).astype(F32) * own_valid
    result, normed_two_low, inner_low, grad_inner_low, grad_middle, grad_inner_vec, narrow_vec = feed(
        base, middle, grad_out, w_inner, w_outer, model_vec, inner_vec
    )
    result_rows = narrow(result)
    grad_w_outer = weight_grad(inner_low, grad_out.astype(BF))
    if fast:
        grad_w_inner, kept, lent = inner_grad(
            spot, grad_w_outer, normed_two_low, grad_inner_low, share
        )
    else:
        grad_w_inner = weight_grad(normed_two_low, grad_inner_low).reshape(FF, D)
    grad_attn_low = grad_middle.astype(BF)
    grad_w_out = weight_grad(mixed_low, grad_attn_low)
    grad_b_out = jnp.sum(grad_attn_low.astype(F32), axis=0)
    grad_mixed = matmul_nt(grad_attn_low, w_out)
    grad_scaled, grad_gain_attn, grad_shift_attn = norm_back(
        scaled, model_vec[4], model_vec[5], grad_mixed
    )
    grad_head_scale = jnp.sum(jnp.sum(grad_scaled * attended, axis=0).reshape(H, HD), axis=1)
    grad_attended = (grad_scaled * scale_row).astype(BF)
    parts = (counts, ids, table, logs, query, keys_both, values_both, grad_attended)
    if fast:
        early = attend_back(0, *parts, after=(kept,))
        got = send_mod(lent)
        late_outs, late_ins = reduce_outs(kept, got), reduce_ins(kept, got)
        late = attend_back(H // 4, *parts, before=early[:5], after=late_outs)
    else:
        early = attend_back(0, *parts)
        late = attend_back(H // 4, *parts, before=early[:5])
    grad_query, key_kept, value_kept, key_sent, value_sent, late_terms = late
    terms = (early[5], late_terms)
    back_keys, back_values = from_partner((key_sent, value_sent), "mod", 0)
    if fast:
        back_keys, back_values, late_sent = lax.optimization_barrier(
            (back_keys, back_values, reduce_sends(late_outs))
        )
    grad_key = (key_kept + back_keys.astype(F32)).astype(BF)
    grad_value = (value_kept + back_values.astype(F32)).astype(BF)
    grad_w_query = weight_grad(normed_low, grad_query)
    grad_w_key = weight_grad(normed_low, grad_key)
    grad_w_value = weight_grad(normed_low, grad_value)
    matrices = [grad_w_query, grad_w_key, grad_w_value, grad_w_out, grad_w_inner, grad_w_outer]
    if fast:
        late_next = reduce_next(late_sent, late_ins)
        kept, lent = scatter(0, spot, matrices, late_next)
        got = send_mod(lent)
        first_outs = reduce_outs(kept, got)
        late_sent, late_ins, late_next, _ = lax.optimization_barrier(
            (late_sent, late_ins, late_next, first_outs)
        )
        late_both, late_low = reduce_both(late_sent, late_ins, late_next)
        grad_table = table_grad(ids, terms, (*first_outs, *late_low))
        late_turns, first_sent, grad_table, grad_inner_vec, narrow_vec = lax.optimization_barrier(
            (reduce_z(late_low), reduce_sends(first_outs), grad_table, grad_inner_vec, narrow_vec)
        )
    else:
        grad_table = table_grad(ids, terms)
    grad_b_query = jnp.sum(grad_query.astype(F32), axis=0)
    grad_b_value = jnp.sum(grad_value.astype(F32), axis=0)
    grad_normed = (
        matmul_nt(grad_query, w_query) + matmul_nt(grad_key, w_key) + matmul_nt(grad_value, w_value)
    )
    grad_in_part, grad_gain_one, grad_shift_one = norm_back(
        inputs, model_vec[0], model_vec[1], grad_normed
    )
    grad_rows = narrow(grad_middle + grad_in_part)
    grad_inner_vec = grad_inner_vec[:3]
    grad_gain_two, grad_shift_two, grad_b_outer = narrow_vec[0], narrow_vec[1], narrow_vec[2]
    grad_model_vec = jnp.stack(
        [
            grad_gain_one,
            grad_shift_one,
            grad_b_query,
            grad_b_value,
            grad_gain_attn,
            grad_shift_attn,
            grad_b_out,
            grad_gain_two,
            grad_shift_two,
            grad_b_outer,
        ]
    )
    grad_heads = jnp.concatenate([grad_table, grad_head_scale[None, :]], axis=0)
    vec_grad = (
        jnp.concatenate(
            [grad_model_vec, grad_inner_vec.reshape(12, D), grad_heads.reshape(1, D)], axis=0
        )
        * share
    )
    if fast:
        second = reduce_total(late_both, late_turns)
        first_ins = reduce_ins(kept, got)
        first_next = reduce_next(first_sent, first_ins)
        first_both, first_low = reduce_both(first_sent, first_ins, first_next)
        vec_grad = sum_z_small(jnp.pad(vec_grad, ((0, 1), (0, 0))))
        vec_grad, first_low = lax.optimization_barrier((vec_grad, first_low))
        first = reduce_total(first_both, reduce_z(first_low))
        vec_grad = sum_rest_small(vec_grad)
        square = jnp.sum(first * first) + jnp.sum(second * second)
        square = square + jnp.where(is_last, jnp.sum(vec_grad * vec_grad), 0.0)
        first, second, square = lax.optimization_barrier((first, second, square))
        sent = unpack_sends(first, second, side)
        square_sum, sent = sum_scalar(square, side, place, sent)
        grad_shard = unpack_shard(*sent, vec_grad, side, place)
    else:
        local_grad = jnp.concatenate([part.reshape(-1) for part in matrices + [vec_grad]])
        half_size = local_grad.shape[0] // 2
        own_half = lax.dynamic_slice_in_dim(local_grad, side * half_size, half_size)
        other_half = lax.dynamic_slice_in_dim(local_grad, (1 - side) * half_size, half_size)
        partner_half = from_partner(other_half.astype(BF), "mod", 0).astype(F32)
        grad_shard = lax.psum_scatter(own_half + partner_half, "dp", scatter_dimension=0, tiled=True)
        square_sum = lax.psum(jnp.sum(grad_shard * grad_shard), ("mod", "dp"))
    grad_norm = jnp.sqrt(square_sum)
    clip_scale = jnp.minimum(1.0, 0.25 / (grad_norm + 1e-06))
    clipped = grad_shard * clip_scale
    new_first = 0.5 * first_moment + 0.5 * clipped
    new_second = 0.6 * second_moment + 0.4 * clipped * clipped
    direction = new_first / (1.0 - 0.5**STEP) / (jnp.sqrt(new_second / (1.0 - 0.6**STEP)) + 1e-08)
    new_master = master - 0.04 * (direction + 0.01 * master)
    new_average = 0.5 * average + 0.5 * new_master
    return (
        result_rows,
        grad_rows,
        grad_norm,
        new_master,
        new_first,
        new_second,
        new_average,
        new_master.astype(jnp.bfloat16),
    )


def solution(mesh):
    placed = (
        P("mod", "dp", None, None),
        P("mod", "dp", None, None),
        P(("mod", "dp")),
        P(("mod", "dp")),
        P(("mod", "dp")),
        P(("mod", "dp")),
        P("dp"),
        P(),
    )
    return jax.shard_map(
        on_device,
        mesh=mesh,
        in_specs=placed,
        out_specs=(
            P("mod", "dp", None, None),
            P("mod", "dp", None, None),
            P(),
            P(("mod", "dp")),
            P(("mod", "dp")),
            P(("mod", "dp")),
            P(("mod", "dp")),
            P(("mod", "dp")),
        ),
        check_vma=False,
    )
```
